32 devices in a mesh: batch: 4 (over y, x), ctx: 8 (over z, core).
Axes of the slice: x: 2, y: 2, z: 4, core: 2. Of those that a mesh axis runs over, the one named last changes fastest.
Arguments:
- q_in: bfloat16 [16384, 2048], P(('batch', 'ctx')), parts along dimension 0, may hold values from -6 to 6
- k_in: bfloat16 [16384, 2048], P(('batch', 'ctx')), parts along dimension 0, may hold values from -6 to 6
- v_in: bfloat16 [16384, 2048], P(('batch', 'ctx')), parts along dimension 0, may hold values from -6 to 6
- z_in: bfloat16 [16384, 2048], P(('batch', 'ctx')), parts along dimension 0, may hold values from -6 to 6
- log_gate: float32 [16384, 16], P(('batch', 'ctx')), parts along dimension 0, may hold values from -1 to 0, as said below
- beta: float32 [16384, 16], P(('batch', 'ctx')), parts along dimension 0, may hold values from 0 to 1
- level_weight: float32 [16384, 16, 6], P(('batch', 'ctx')), parts along dimension 0, may hold values from 0.2 to 2
- conv_weight: float32 [3, 4, 2048], replicated, may hold values from -3 to 3
- norm_gain: float32 [128], replicated, may hold values from 0.25 to 1.75
Outputs:
- mixed_out: bfloat16 [16384, 2048], P(('batch', 'ctx')), parts along dimension 0
The draws below stay inside these ranges and needn't reach their ends.
There are 4 independent parts, one for each index of `batch`. The reference program is written for one: setup_inputs(seed, part) draws one part's arguments, and reference() takes and returns one part's arrays. A program takes and returns all parts, laid end to end along the dimension named above; an argument that names none is the same for every part. Nothing has to cross between parts.
Inputs may be any that keep to these rules, and one draw needn't show every extreme that they name: `log_gate`: logarithms of forget gates, never positive.
All inputs are finite; a program needn't handle non-finite values.
Results may differ from the reference program's by a relative error of at most 0.0056.
Values may be sent and summed in bfloat16 or wider, within the bound.
No kernel may reach another device: no remote copies, remote signals or barrier semaphores. Data moves between devices by JAX's collectives and lax.ppermute only.
A program may use at most 128 MiB of HBM per device.

```python
import math
import jax
import jax.numpy as jnp
from jax import lax

HEAD_TOTAL = 16
DK = 128
DM = 2048
TOK_DEV = 512
BLK = 128
CONV = 4
LEVELS = 6
SEQUENCE_TOKENS = 4096
N_CTX = 8


def head_kinds(key):
    share = 0.5
    scores = jax.random.uniform(jax.random.fold_in(key, 11), (HEAD_TOTAL,))
    slow = (scores < share) | (scores == jnp.min(scores))
    return slow & (scores != jnp.max(scores))


def draw_log_gate(key, part):
    slow = head_kinds(key)
    key_vectors = jax.random.split(jax.random.fold_in(key, 21), 6)
    jitter = jax.random.uniform(key_vectors[0], (SEQUENCE_TOKENS, HEAD_TOTAL), minval=0.7, maxval=1.4)
    segment_factor = jax.random.uniform(key_vectors[1], (SEQUENCE_TOKENS // TOK_DEV, HEAD_TOTAL), minval=0.6, maxval=1.6)
    segment_factor = jnp.repeat(segment_factor, TOK_DEV, axis=0)
    slow_rate = jax.random.uniform(key_vectors[2], (HEAD_TOTAL,), minval=0.1, maxval=0.5) / SEQUENCE_TOKENS
    fast_rate = jnp.exp(jax.random.uniform(key_vectors[3], (HEAD_TOTAL,), minval=jnp.log(1.0 / 50.0), maxval=jnp.log(1.0 / 10.0)))
    rate = jnp.where(slow, slow_rate, fast_rate)
    logarithm_values = -rate[None, :] * jitter * segment_factor
    surge_position = jax.random.randint(key_vectors[4], (2, HEAD_TOTAL), 0, SEQUENCE_TOKENS)
    token_position = jnp.arange(SEQUENCE_TOKENS, dtype=jnp.int32)
    surge_matched = jnp.any(token_position[:, None, None] == surge_position[None, :, :], axis=1)
    surge_dropped = jnp.log(jax.random.uniform(key_vectors[5], (SEQUENCE_TOKENS, HEAD_TOTAL), minval=0.6, maxval=0.8))
    return (logarithm_values + jnp.where(surge_matched, surge_dropped, 0.0)).astype(jnp.float32)


def draw_beta(key, part):
    slow = head_kinds(key)
    key_vectors = jax.random.split(jax.random.fold_in(key, 31), 3)
    slow_beta = jax.random.uniform(key_vectors[0], (HEAD_TOTAL,), minval=0.2, maxval=0.6) * DK / SEQUENCE_TOKENS
    jitter = jax.random.uniform(key_vectors[1], (SEQUENCE_TOKENS, HEAD_TOTAL), minval=0.7, maxval=1.4)
    fast_beta = jax.random.uniform(key_vectors[2], (SEQUENCE_TOKENS, HEAD_TOTAL), minval=0.2, maxval=0.9)
    return jnp.where(slow[None, :], slow_beta[None, :] * jitter, fast_beta).astype(jnp.float32)


def block_levels(stream_key, dims, shards, least, top_value):
    def one(position, parts):
        draws = jax.random.uniform(jax.random.fold_in(jax.random.fold_in(stream_key, 6), position), (parts,), jnp.float32, least / len(shards), top_value / len(shards))
        return jnp.repeat(jnp.exp(draws), dims[position] // parts).reshape((-1,) + (1,) * (len(dims) - position - 1))

    loudness = one(*shards[0])
    for cut in shards[1:]:
        loudness = loudness * one(*cut)
    return loudness


def noise(key, dims, spread, reach, cuts=(), kind=jnp.bfloat16):
    values = jax.random.normal(key, dims, jnp.float32) * spread
    if len(cuts) > 0:
        values = block_levels(key, dims, cuts, -0.22, 0.18) * values
    return jnp.clip(values, min=-reach, max=reach).astype(kind)


def setup_inputs(seed: int = 0, part: int = 0) -> dict:
    key_of = jax.random.split(jax.random.key(seed), 10)
    part_splits = jax.random.split(jax.random.fold_in(key_of[9], part), 10)
    q_in = noise(part_splits[0], (SEQUENCE_TOKENS, DM), 1.0, 6.0, ((0, 8),))
    k_in = noise(part_splits[1], (SEQUENCE_TOKENS, DM), 1.0, 6.0, ((0, 8),))
    v_in = noise(part_splits[2], (SEQUENCE_TOKENS, DM), 1.0, 6.0, ((0, 8),))
    z_in = noise(part_splits[3], (SEQUENCE_TOKENS, DM), 1.0, 6.0, ((0, 8),))
    log_gate = draw_log_gate(jax.random.fold_in(jax.random.fold_in(key_of[9], part), 71), part)
    beta = draw_beta(jax.random.fold_in(jax.random.fold_in(key_of[9], part), 71), part)
    level_weight = jnp.clip(jnp.exp(math.log(2.0) - 2.3025851 * jax.random.uniform(part_splits[6], (SEQUENCE_TOKENS, HEAD_TOTAL, LEVELS), jnp.float32) ** block_levels(part_splits[6], (SEQUENCE_TOKENS, HEAD_TOTAL, LEVELS), ((0, 8),), -0.2, 0.2)), 0.2, 2.0)
    conv_weight = noise(key_of[7], (3, CONV, DM), CONV ** -0.5, 3.0, (), jnp.float32)
    norm_gain = jnp.clip(1.0 + 0.15 * jax.random.normal(key_of[8], (DK,), jnp.float32), 0.25, 1.75)
    return {"q_in": q_in, "k_in": k_in, "v_in": v_in, "z_in": z_in, "log_gate": log_gate, "beta": beta, "level_weight": level_weight, "conv_weight": conv_weight, "norm_gain": norm_gain}


EPS = 1e-06

def product(first_op, second_op, pattern):
    return jnp.einsum(pattern, first_op, second_op, precision=lax.Precision.HIGHEST)

def lowered(first_op, second_op, pattern):
    return jnp.einsum(pattern, first_op.astype(jnp.bfloat16), second_op.astype(jnp.bfloat16), preferred_element_type=jnp.float32)

def short_conv(tensor, earlier, weight):
    conv_taps = weight.shape[0]
    length = tensor.shape[0]
    joined = jnp.concatenate([earlier, tensor], axis=0).astype(jnp.float32)
    summed = weight[0] * joined[0:length]
    for offset in range(1, conv_taps):
        summed = summed + weight[offset] * joined[offset:offset + length]
    return jax.nn.silu(summed)

def unit_norm(tensor, head_count):
    shaped = tensor.reshape(tensor.shape[0], head_count, -1)
    return shaped * lax.rsqrt(lax.optimization_barrier(jnp.sum(shaped * shaped, axis=-1, keepdims=True)) + EPS)

def unit_lower_inverse(lower_part, block_size):
    identity = jnp.eye(block_size, dtype=jnp.float32)
    power = -lower_part
    inverse = identity + power
    for section in range(1, (block_size - 1).bit_length()):
        power = product(power, power, 'hts,hsu->htu')
        inverse = inverse + product(inverse, power, 'hts,hsu->htu')
    return inverse

def block_terms(running, inputs):
    prior_a, prior_b = running
    query_block, key_block, value_block, gate_block, beta_block = inputs
    block_size = query_block.shape[1]
    key_size = key_block.shape[2]
    value_size = value_block.shape[2]
    decay_sum = jnp.cumsum(gate_block, axis=-1)
    row_index = lax.broadcasted_iota(jnp.int32, (block_size, block_size), 0)
    col_index = lax.broadcasted_iota(jnp.int32, (block_size, block_size), 1)
    causal = col_index <= row_index
    strict = col_index < row_index
    log_decay = jnp.where(causal, decay_sum[:, :, None] - decay_sum[:, None, :], 0.0)
    decay = jnp.where(causal, jnp.exp(log_decay), 0.0) * beta_block[:, None, :]
    keys_keys = lowered(key_block, key_block, 'hte,hse->hts')
    query_keys = lowered(query_block, key_block, 'hte,hse->hts')
    lower_part = jnp.where(strict, decay * keys_keys, 0.0)
    mixing = (decay * query_keys).astype(jnp.bfloat16)
    gamma = jnp.exp(decay_sum)
    right_side = jnp.concatenate([value_block.astype(jnp.float32), gamma[..., None] * key_block.astype(jnp.float32)], axis=-1)
    inverse = unit_lower_inverse(lower_part, block_size)
    solved = product(inverse, right_side, 'hts,hse->hte')
    values_new = solved[..., :value_size].astype(jnp.bfloat16)
    keys_new = solved[..., value_size:].astype(jnp.bfloat16)
    query_state = (gamma[..., None] * query_block.astype(jnp.float32) - lowered(mixing, keys_new, 'hts,hse->hte')).astype(jnp.bfloat16)
    inside = lowered(mixing, values_new, 'hts,hsv->htv')
    tail_keys = ((jnp.exp(decay_sum[:, -1:] - decay_sum) * beta_block)[..., None] * key_block.astype(jnp.float32)).astype(jnp.bfloat16)
    block_a = gamma[:, -1, None, None] * jnp.eye(key_size, dtype=jnp.float32) - lowered(keys_new, tail_keys, 'hsd,hse->hde')
    block_b = lowered(values_new, tail_keys, 'hsv,hse->hve')
    carried = lowered(query_state, prior_a, 'htd,hed->hte')
    local = inside + lowered(query_state, prior_b, 'htd,hvd->htv')
    next_a = product(prior_a, block_a, 'hde,hef->hdf')
    next_b = product(prior_b, block_a, 'hve,hef->hvf') + block_b
    return ((next_a, next_b), (carried, local))

def segment_terms(queries, key_vectors, values, log_gate, beta, block_size):
    length, head_count, key_size = queries.shape
    value_size = values.shape[2]
    blocks = length // block_size

    def arrange(tensor):
        return tensor.reshape(blocks, block_size, head_count, -1).transpose(0, 2, 1, 3)

    def arrange_rates(tensor):
        return tensor.reshape(blocks, block_size, head_count).transpose(0, 2, 1)
    initial = (jnp.broadcast_to(jnp.eye(key_size, dtype=jnp.float32), (head_count, key_size, key_size)), jnp.zeros((head_count, value_size, key_size), jnp.float32))
    (pair_a, pair_b), (carried, local) = lax.scan(block_terms, initial, (arrange(queries), arrange(key_vectors), arrange(values), arrange_rates(log_gate), arrange_rates(beta)))
    carried = carried.transpose(0, 2, 1, 3).reshape(length, head_count, key_size)
    local = local.transpose(0, 2, 1, 3).reshape(length, head_count, value_size)
    return (pair_a, pair_b, carried, local)

def finish(opened, gates, gain):
    square = lax.optimization_barrier(jnp.mean(opened * opened, axis=-1, keepdims=True))
    normed = opened * lax.rsqrt(square + EPS) * gain
    flat = normed.reshape(opened.shape[0], -1)
    return (flat * jax.nn.silu(gates.astype(jnp.float32))).astype(jnp.bfloat16)

def reference(q_in, k_in, v_in, z_in, log_gate, beta, level_weight, conv_weight, norm_gain):
    earlier = jnp.zeros((CONV - 1, DM), jnp.bfloat16)
    queries = unit_norm(short_conv(q_in, earlier, conv_weight[0]), HEAD_TOTAL).astype(jnp.bfloat16)
    key_vectors = unit_norm(short_conv(k_in, earlier, conv_weight[1]), HEAD_TOTAL).astype(jnp.bfloat16)
    values = short_conv(v_in, earlier, conv_weight[2]).reshape(SEQUENCE_TOKENS, HEAD_TOTAL, DK).astype(jnp.bfloat16)

    def one_segment(inputs):
        return segment_terms(inputs[0], inputs[1], inputs[2], inputs[3], inputs[4], BLK)
    pair_a, pair_b, carried, local = lax.map(one_segment, (queries.reshape(N_CTX, TOK_DEV, HEAD_TOTAL, DK), key_vectors.reshape(N_CTX, TOK_DEV, HEAD_TOTAL, DK), values.reshape(N_CTX, TOK_DEV, HEAD_TOTAL, DK), log_gate.reshape(N_CTX, TOK_DEV, HEAD_TOTAL), beta.reshape(N_CTX, TOK_DEV, HEAD_TOTAL)))
    level_count = N_CTX.bit_length() - 1
    device = jnp.arange(N_CTX, dtype=jnp.int32)
    reach_map = jnp.broadcast_to(jnp.eye(DK, dtype=jnp.float32), (N_CTX, HEAD_TOTAL, DK, DK))
    agg_a, agg_b = (pair_a, pair_b)
    states = []
    for level in range(level_count):
        block_index = device // 2 ** level
        upper_half = block_index % 2 == 1
        sibling = block_index + 1 - 2 * (block_index % 2)
        far_a = agg_a[sibling]
        far_b = agg_b[sibling]
        mask = upper_half[:, None, None, None]
        states.append(jnp.where(mask, product(far_b, reach_map, 'nhvd,nhde->nhve'), 0.0))
        reach_map = jnp.where(mask, product(far_a, reach_map, 'nhde,nhef->nhdf'), reach_map)
        if level < level_count - 1:
            new_a = product(agg_a[0::2], agg_a[1::2], 'nhde,nhef->nhdf')
            new_b = product(agg_b[0::2], agg_a[1::2], 'nhve,nhef->nhvf') + agg_b[1::2]
            agg_a, agg_b = (new_a, new_b)
    stacked = jnp.stack(states, axis=1)

    def one_output(inputs):
        seg_carried, seg_local, seg_states, seg_weight, seg_gates = inputs
        weighted = seg_carried[:, :, None, :] * seg_weight[:, :, 1:level_count + 1, None]
        far_out = lowered(weighted, seg_states, 'thld,lhvd->thv')
        opened = seg_weight[:, :, 0, None] * seg_local + far_out
        return finish(opened, seg_gates, norm_gain)
    result = lax.map(one_output, (carried, local, stacked, level_weight.reshape(N_CTX, TOK_DEV, HEAD_TOTAL, LEVELS), z_in.reshape(N_CTX, TOK_DEV, DM)))
    return result.reshape(SEQUENCE_TOKENS, DM)
```

```python
import functools

import jax
import jax.numpy as jnp
from jax import lax
from jax.experimental import pallas as pl
from jax.experimental.pallas import tpu as pltpu
from jax.sharding import PartitionSpec as P

BLK = 128
SUB = 16
HEADS_PER_STEP = 2
EPS = 1e-06
BF = jnp.bfloat16
F32 = jnp.float32


def dot(first, second):
    return lax.dot_general(
        first, second, (((1,), (0,)), ((), ())), preferred_element_type=F32
    )


def silu(value):
    return value * pl.reciprocal(1.0 + jnp.exp(-value), approx=False)


def fill_padded(pad_ref, slot, x_ref, halo, lanes):
    pad_ref[slot, 4:8, :] = halo.astype(F32)
    pad_ref[slot, 8:, :] = x_ref[:, lanes].astype(F32)


def conv_rows(pad_ref, slot, taps, start, count):
    total = taps[0:1] * pad_ref[slot, start + 5 : start + 5 + count, :]
    for tap in range(1, 4):
        total = total + taps[tap : tap + 1] * pad_ref[
            slot, start + 5 + tap : start + 5 + tap + count, :
        ]
    return silu(total)


def unit(rows):
    return rows * lax.rsqrt(jnp.sum(rows * rows, axis=-1, keepdims=True) + EPS)


def iota2(shape, dim):
    return lax.broadcasted_iota(jnp.int32, shape, dim)


def decay_matrix(g_col, g_row, beta_row):
    size = g_col.shape[0]
    causal = iota2((size, BLK), 1) <= iota2((size, BLK), 0)
    return jnp.exp(jnp.where(causal, g_col - g_row, -1e30)) * beta_row


def make_masks(mask_ref):
    row, col = iota2((BLK, BLK), 0), iota2((BLK, BLK), 1)
    size, index = SUB, 0
    while size < BLK:
        same = row // size == col // size
        pair = row // (2 * size) == col // (2 * size)
        high_low = pair & (row // size % 2 == 1) & (col // size % 2 == 0)
        mask_ref[index] = jnp.where(same, 1.0, 0.0).astype(BF)
        mask_ref[index + 1] = jnp.where(high_low, 1.0, 0.0).astype(BF)
        size, index = size * 2, index + 2


def tiled(packed, times, mask):
    return jnp.concatenate([packed.astype(BF)] * times, axis=0) * mask


def picked(lower, size, offset):
    groups = BLK // size if offset is None else BLK // (2 * size)
    step = size if offset is None else 2 * size
    first = 0 if offset is None else offset
    lane = iota2((size, BLK), 1) // step
    out = lower[first : first + size]
    for group in range(1, groups):
        begin = first + group * step
        out = jnp.where(lane == group, lower[begin : begin + size], out)
    return out


def inverses(lowers, mask_ref):
    count = len(lowers)
    every = range(count)
    row, col = iota2((SUB, BLK), 0), iota2((SUB, BLK), 1) % SUB
    eye = jnp.where(row == col, 1.0, 0.0).astype(F32)
    strict = col < row
    same = mask_ref[0]
    times = BLK // SUB
    powers = [jnp.where(strict, -picked(lower, SUB, None), 0.0) for lower in lowers]
    results = [eye + power for power in powers]
    powers = [dot(p.astype(BF), tiled(p, times, same)) for p in powers]
    reach = 2
    while reach < SUB // 2:
        both = [
            dot(
                jnp.concatenate([powers[i].astype(BF), results[i].astype(BF)], axis=0),
                tiled(powers[i], times, same),
            )
            for i in every
        ]
        powers = [b[:SUB] for b in both]
        results = [results[i] + both[i][SUB:] for i in every]
        reach *= 2
    results = [
        results[i] + dot(results[i].astype(BF), tiled(powers[i], times, same)) for i in every
    ]
    size, index = SUB, 0
    while size < BLK:
        times = BLK // size
        low = iota2((size, BLK), 1) // size % 2 == 0
        cross = [picked(lower, size, size).astype(BF) for lower in lowers]
        moved = [dot(cross[i], tiled(results[i], times, mask_ref[index])) for i in every]
        turned = [
            dot(results[i].astype(BF), tiled(moved[i], times, mask_ref[index + 1]))
            for i in every
        ]
        results = [
            jnp.concatenate(
                [jnp.where(low, results[i], 0.0), jnp.where(low, -turned[i], results[i])], axis=0
            )
            for i in every
        ]
        size, index = size * 2, index + 2
    return results


def key_side(
    rows_ref, g_ref, taps_ref, halo_ref, k_ref, v_ref,
    kt_ref, uw_ref, pair_ref, sent_ref, prior_ref, pad_ref, mask_ref,
):
    step = pl.program_id(0)

    @pl.when(step == 0)
    def _():
        make_masks(mask_ref)

    length = k_ref.shape[0]
    blocks = length // BLK
    turned_g = pltpu.roll(g_ref[...], BLK - HEADS_PER_STEP * step, 1)
    lowers, rights, tails, lasts = [], [], [], []
    for head in range(HEADS_PER_STEP):
        lanes = slice(head * BLK, (head + 1) * BLK)
        fill_padded(pad_ref, 2 * head, k_ref, halo_ref[1, :, lanes], lanes)
        fill_padded(pad_ref, 2 * head + 1, v_ref, halo_ref[2, :, lanes], lanes)
        for block in range(blocks):
            start = block * BLK
            tokens = slice(start, start + BLK)
            keys = unit(conv_rows(pad_ref, 2 * head, taps_ref[1, :, lanes], start, BLK)).astype(BF)
            values = conv_rows(pad_ref, 2 * head + 1, taps_ref[2, :, lanes], start, BLK).astype(BF)
            keys_f = keys.astype(F32)
            turned = keys_f.T
            turned_b = turned.astype(BF)
            kt_ref[head, :, tokens] = turned_b
            g_col = jnp.broadcast_to(turned_g[tokens, head : head + 1], (BLK, BLK))
            g_row = rows_ref[head, 0:1, tokens]
            beta_row = rows_ref[head, 1:2, tokens]
            g_last = g_row[:, BLK - 1 : BLK]
            lowers.append(decay_matrix(g_col, g_row, beta_row) * dot(keys, turned_b))
            rights.append(
                jnp.concatenate([values, (jnp.exp(g_col) * keys_f).astype(BF)], axis=1)
            )
            tails.append((turned * (jnp.exp(g_last - g_row) * beta_row)).astype(BF))
            lasts.append(jnp.exp(g_last))
    solved = inverses(lowers, mask_ref)
    maps = []
    for head in range(HEADS_PER_STEP):
        for block in range(blocks):
            i = head * blocks + block
            fresh = dot(solved[i].astype(BF), rights[i]).astype(BF)
            uw_ref[head, block * BLK : (block + 1) * BLK, :] = fresh
            maps.append(dot(tails[i], fresh))
    eye = jnp.where(iota2((BLK, BLK), 0) == iota2((BLK, BLK), 1), 1.0, 0.0).astype(F32)
    for head in range(HEADS_PER_STEP):
        i = head * blocks
        state_a = lasts[i] * eye - maps[i][:, BLK:]
        state_b = maps[i][:, :BLK]
        for block in range(1, blocks):
            i = head * blocks + block
            state = jnp.concatenate([state_a, state_b], axis=1)
            low = state.astype(BF)
            prior_ref[head, block - 1] = low
            state = lasts[i] * state - dot(maps[i][:, BLK:].astype(BF), low)
            state_a = state[:, :BLK]
            state_b = state[:, BLK:] + maps[i][:, :BLK]
        state = jnp.concatenate([state_a, state_b], axis=1)
        pair_ref[head] = state
        sent_ref[head] = state.astype(BF)


def query_side(
    rows_ref, g_ref, taps_ref, halo_ref, q_ref, kt_ref, uw_ref, prior_ref,
    carried_ref, local_ref, pad_ref,
):
    step = pl.program_id(0)
    length = q_ref.shape[0]
    blocks = length // BLK
    turned_g = pltpu.roll(g_ref[...], BLK - HEADS_PER_STEP * step, 1)
    for head in range(HEADS_PER_STEP):
        lanes = slice(head * BLK, (head + 1) * BLK)
        fill_padded(pad_ref, head, q_ref, halo_ref[0, :, lanes], lanes)
        for block in range(blocks):
            start = block * BLK
            tokens = slice(start, start + BLK)
            queries = unit(conv_rows(pad_ref, head, taps_ref[0, :, lanes], start, BLK)).astype(BF)
            g_col = jnp.broadcast_to(turned_g[tokens, head : head + 1], (BLK, BLK))
            g_row = rows_ref[head, 0:1, tokens]
            beta_row = rows_ref[head, 1:2, tokens]
            mixing = (
                decay_matrix(g_col, g_row, beta_row) * dot(queries, kt_ref[head, :, tokens])
            ).astype(BF)
            inner = dot(mixing, uw_ref[head, tokens, :])
            through = (jnp.exp(g_col) * queries.astype(F32) - inner[:, BLK:]).astype(BF)
            if block == 0:
                carried_ref[tokens, lanes] = through
                local_ref[tokens, lanes] = inner[:, :BLK].astype(local_ref.dtype)
            else:
                passed = dot(through, prior_ref[head, block - 1])
                carried_ref[tokens, lanes] = passed[:, :BLK].astype(carried_ref.dtype)
                local_ref[tokens, lanes] = (inner[:, :BLK] + passed[:, BLK:]).astype(
                    local_ref.dtype
                )


def finish_side(weight_ref, gain_ref, z_ref, carried_ref, local_ref, *rest):
    state_refs, out_ref = rest[:-1], rest[-1]
    step = pl.program_id(0)
    levels = len(state_refs)
    per_head = levels + 1
    width = weight_ref.shape[1]
    length = z_ref.shape[0]
    blocks = length // BLK
    stride = HEADS_PER_STEP * per_head
    for head in range(HEADS_PER_STEP):
        lanes = slice(head * BLK, (head + 1) * BLK)
        states = jnp.concatenate([ref[head] for ref in state_refs], axis=0)
        for block in range(blocks):
            tokens = slice(block * BLK, (block + 1) * BLK)
            weights = pltpu.roll(weight_ref[tokens, :], width - stride * step, 1)
            first = head * per_head
            carried = carried_ref[tokens, lanes].astype(F32)
            scaled = [
                (carried * weights[:, first + level : first + level + 1]).astype(BF)
                for level in range(1, per_head)
            ]
            far = dot(jnp.concatenate(scaled, axis=1), states)
            opened = weights[:, first : first + 1] * local_ref[tokens, lanes].astype(F32) + far
            square = jnp.sum(opened * opened, axis=-1, keepdims=True) * (1.0 / BLK)
            normed = opened * lax.rsqrt(square + EPS) * gain_ref[...]
            gate = z_ref[tokens, lanes].astype(F32)
            out_ref[tokens, lanes] = (normed * silu(gate)).astype(BF)


def combine_side(upper_ref, pair_ref, far_ref, reach_ref, next_ref, sent_ref, state_ref, new_reach_ref):
    heads = pair_ref.shape[0]

    @pl.when(upper_ref[0] == 1)
    def _():
        for head in range(heads):
            far = far_ref[head]
            own = pair_ref[head]
            seen = dot(reach_ref[head], far)
            new_reach_ref[head] = seen[:, :BLK].astype(BF)
            state_ref[head] = seen[:, BLK:].astype(BF)
            merged = dot(own[:, :BLK].astype(BF), far)
            merged = jnp.concatenate([merged[:, :BLK], merged[:, BLK:] + own[:, BLK:]], axis=1)
            next_ref[head] = merged
            sent_ref[head] = merged.astype(BF)

    @pl.when(upper_ref[0] == 0)
    def _():
        for head in range(heads):
            far = far_ref[head]
            merged = dot(far[:, :BLK], pair_ref[head].astype(BF))
            merged = jnp.concatenate(
                [merged[:, :BLK], merged[:, BLK:] + far[:, BLK:].astype(F32)], axis=1
            )
            next_ref[head] = merged
            sent_ref[head] = merged.astype(BF)
            state_ref[head] = jnp.zeros((BLK, BLK), BF)
            new_reach_ref[head] = reach_ref[head]


def top_side(upper_ref, far_ref, reach_ref, state_ref):
    @pl.when(upper_ref[0] == 1)
    def _():
        for head in range(far_ref.shape[0]):
            state_ref[head] = dot(reach_ref[head], far_ref[head]).astype(BF)

    @pl.when(upper_ref[0] == 0)
    def _():
        state_ref[...] = jnp.zeros(state_ref.shape, BF)


def shape_of(shape, dtype):
    return jax.ShapeDtypeStruct(shape, dtype)


def whole(shape):
    return pl.BlockSpec(shape, lambda i: (0,) * len(shape))


def by_head(shape):
    return pl.BlockSpec((HEADS_PER_STEP,) + shape, lambda i: (i,) + (0,) * len(shape))


def by_column(shape):
    lead = len(shape) - 1
    return pl.BlockSpec(shape, lambda i: (0,) * lead + (i,))


VMEM = pl.BlockSpec(memory_space=pltpu.VMEM)
SMEM = pl.BlockSpec(memory_space=pltpu.SMEM)


def per_device(q_in, k_in, v_in, z_in, log_gate, beta, level_weight, conv_weight, norm_gain):
    length, heads = log_gate.shape
    blocks = length // BLK
    width = HEADS_PER_STEP * BLK
    steps = heads // HEADS_PER_STEP
    ctx = lax.axis_size("ctx")
    levels = ctx.bit_length() - 1
    position = lax.axis_index("ctx")
    edge = jnp.stack([x[length - 4 :] for x in (q_in, k_in, v_in)], axis=0)
    halo = lax.ppermute(edge, "ctx", [(i, i + 1) for i in range(ctx - 1)])

    g = jnp.cumsum(log_gate.reshape(blocks, BLK, heads), axis=1).reshape(length, heads)
    g_pad = jnp.pad(g, ((0, 0), (0, BLK - heads)))
    rows = jnp.stack([g.T, beta.T], axis=1)
    weights = level_weight[:, :, : levels + 1].reshape(length, heads * (levels + 1))
    weights = jnp.pad(weights, ((0, 0), (0, -weights.shape[1] % BLK)))

    params = pltpu.CompilerParams(dimension_semantics=("arbitrary",), vmem_limit_bytes=60 << 20)
    kt, uw, pair, sent, prior = pl.pallas_call(
        key_side,
        grid=(steps,),
        in_specs=[
            by_head((2, length)), whole(g_pad.shape), by_column((3, 4, width)),
            by_column((3, 4, width)), by_column((length, width)), by_column((length, width)),
        ],
        out_specs=[
            by_head((BLK, length)), by_head((length, 2 * BLK)), by_head((BLK, 2 * BLK)),
            by_head((BLK, 2 * BLK)), by_head((blocks - 1, BLK, 2 * BLK)),
        ],
        out_shape=[
            shape_of((heads, BLK, length), BF), shape_of((heads, length, 2 * BLK), BF),
            shape_of((heads, BLK, 2 * BLK), F32), shape_of((heads, BLK, 2 * BLK), BF),
            shape_of((heads, blocks - 1, BLK, 2 * BLK), BF),
        ],
        scratch_shapes=[
            pltpu.VMEM((2 * HEADS_PER_STEP, length + 8, BLK), F32),
            pltpu.VMEM((6, BLK, BLK), BF),
        ],
        compiler_params=params,
        cost_estimate=pl.CostEstimate(flops=10**10, bytes_accessed=2 * 10**7, transcendentals=10**7),
        name="key_side",
    )(rows, g_pad, conv_weight, halo, k_in, v_in)

    carried, local = pl.pallas_call(
        query_side,
        grid=(steps,),
        in_specs=[
            by_head((2, length)), whole(g_pad.shape), by_column((3, 4, width)),
            by_column((3, 4, width)), by_column((length, width)), by_head((BLK, length)),
            by_head((length, 2 * BLK)), by_head((blocks - 1, BLK, 2 * BLK)),
        ],
        out_specs=[by_column((length, width)), by_column((length, width))],
        out_shape=[shape_of(q_in.shape, BF), shape_of(q_in.shape, BF)],
        scratch_shapes=[pltpu.VMEM((HEADS_PER_STEP, length + 8, BLK), F32)],
        compiler_params=params,
        cost_estimate=pl.CostEstimate(flops=10**10, bytes_accessed=2 * 10**7, transcendentals=10**7),
        name="query_side",
    )(rows, g_pad, conv_weight, halo, q_in, kt, uw, prior)

    reach = jnp.broadcast_to(jnp.eye(BLK, dtype=BF), (heads, BLK, BLK))
    states = []
    square = (heads, BLK, BLK)
    for level in range(levels - 1):
        far = lax.ppermute(sent, "ctx", [(i, i ^ 2**level) for i in range(ctx)])
        upper = (position // 2**level % 2).astype(jnp.int32).reshape(1)
        pair, sent, state, reach = pl.pallas_call(
            combine_side,
            in_specs=[SMEM, VMEM, VMEM, VMEM],
            out_specs=[VMEM] * 4,
            out_shape=[
                shape_of(pair.shape, F32), shape_of(pair.shape, BF), shape_of(square, BF),
                shape_of(square, BF),
            ],
            name="combine",
        )(upper, pair, far, reach)
        states.append(state)
    top = levels - 1
    far = lax.ppermute(
        sent[:, :, BLK:], "ctx", [(i, i + 2**top) for i in range(ctx - 2**top)]
    )
    upper = (position // 2**top % 2).astype(jnp.int32).reshape(1)
    states.append(
        pl.pallas_call(
            top_side,
            in_specs=[SMEM, VMEM, VMEM],
            out_specs=VMEM,
            out_shape=shape_of(square, BF),
            name="top",
        )(upper, far, reach)
    )
    return pl.pallas_call(
        finish_side,
        grid=(steps,),
        in_specs=[
            whole(weights.shape), whole((1, BLK)), by_column((length, width)),
            by_column((length, width)), by_column((length, width)),
        ]
        + [by_head((BLK, BLK))] * levels,
        out_specs=by_column((length, width)),
        out_shape=shape_of(z_in.shape, BF),
        compiler_params=params,
        name="finish_side",
    )(weights, norm_gain.reshape(1, BLK), z_in, carried, local, *states)


def solution(mesh):
    placed = (
        P(("batch", "ctx"), None),
        P(("batch", "ctx"), None),
        P(("batch", "ctx"), None),
        P(("batch", "ctx"), None),
        P(("batch", "ctx"), None),
        P(("batch", "ctx"), None),
        P(("batch", "ctx"), None, None),
        P(),
        P(),
    )
    return jax.shard_map(
        per_device, mesh=mesh, in_specs=placed, out_specs=P(("batch", "ctx"), None), check_vma=False
    )
```

```python
import functools

import jax
import jax.numpy as jnp
from jax import lax
from jax.experimental import pallas as pl
from jax.experimental.pallas import tpu as pltpu
from jax.sharding import PartitionSpec as P

BLK = 128
SUB = 16
HEADS_PER_STEP = 2
EPS = 1e-06
BF = jnp.bfloat16
F32 = jnp.float32


def dot(first, second):
    return lax.dot_general(
        first, second, (((1,), (0,)), ((), ())), preferred_element_type=F32
    )


def silu(value):
    return value * pl.reciprocal(1.0 + jnp.exp(-value), approx=False)


def fill_padded(pad_ref, slot, x_ref, halo, lanes):
    pad_ref[slot, 4:8, :] = halo.astype(F32)
    pad_ref[slot, 8:, :] = x_ref[:, lanes].astype(F32)


def conv_rows(pad_ref, slot, taps, start, count):
    total = taps[0:1] * pad_ref[slot, start + 5 : start + 5 + count, :]
    for tap in range(1, 4):
        total = total + taps[tap : tap + 1] * pad_ref[
            slot, start + 5 + tap : start + 5 + tap + count, :
        ]
    return silu(total)


def unit(rows):
    return rows * lax.rsqrt(jnp.sum(rows * rows, axis=-1, keepdims=True) + EPS)


def iota2(shape, dim):
    return lax.broadcasted_iota(jnp.int32, shape, dim)


def decay_matrix(g_col, g_row, beta_row):
    size = g_col.shape[0]
    causal = iota2((size, BLK), 1) <= iota2((size, BLK), 0)
    return jnp.exp(jnp.where(causal, g_col - g_row, -1e30)) * beta_row


def make_masks(mask_ref):
    row, col = iota2((BLK, BLK), 0), iota2((BLK, BLK), 1)
    size, index = SUB, 0
    while size < BLK:
        same = row // size == col // size
        pair = row // (2 * size) == col // (2 * size)
        high_low = pair & (row // size % 2 == 1) & (col // size % 2 == 0)
        mask_ref[index] = jnp.where(same, 1.0, 0.0).astype(BF)
        mask_ref[index + 1] = jnp.where(high_low, 1.0, 0.0).astype(BF)
        size, index = size * 2, index + 2


def tiled(packed, times, mask):
    return jnp.concatenate([packed.astype(BF)] * times, axis=0) * mask


def picked(lower, size, offset):
    groups = BLK // size if offset is None else BLK // (2 * size)
    step = size if offset is None else 2 * size
    first = 0 if offset is None else offset
    lane = iota2((size, BLK), 1) // step
    out = lower[first : first + size]
    for group in range(1, groups):
        begin = first + group * step
        out = jnp.where(lane == group, lower[begin : begin + size], out)
    return out


def inverses(lowers, mask_ref):
    count = len(lowers)
    every = range(count)
    row, col = iota2((SUB, BLK), 0), iota2((SUB, BLK), 1) % SUB
    eye = jnp.where(row == col, 1.0, 0.0).astype(F32)
    strict = col < row
    same = mask_ref[0]
    times = BLK // SUB
    powers = [jnp.where(strict, -picked(lower, SUB, None), 0.0) for lower in lowers]
    results = [eye + power for power in powers]
    powers = [dot(p.astype(BF), tiled(p, times, same)) for p in powers]
    reach = 2
    while reach < SUB // 2:
        both = [
            dot(
                jnp.concatenate([powers[i].astype(BF), results[i].astype(BF)], axis=0),
                tiled(powers[i], times, same),
            )
            for i in every
        ]
        powers = [b[:SUB] for b in both]
        results = [results[i] + both[i][SUB:] for i in every]
        reach *= 2
    results = [
        results[i] + dot(results[i].astype(BF), tiled(powers[i], times, same)) for i in every
    ]
    size, index = SUB, 0
    while size < BLK:
        times = BLK // size
        low = iota2((size, BLK), 1) // size % 2 == 0
        cross = [picked(lower, size, size).astype(BF) for lower in lowers]
        moved = [dot(cross[i], tiled(results[i], times, mask_ref[index])) for i in every]
        turned = [
            dot(results[i].astype(BF), tiled(moved[i], times, mask_ref[index + 1]))
            for i in every
        ]
        results = [
            jnp.concatenate(
                [jnp.where(low, results[i], 0.0), jnp.where(low, -turned[i], results[i])], axis=0
            )
            for i in every
        ]
        size, index = size * 2, index + 2
    return results


def key_side(
    rows_ref, g_ref, taps_ref, halo_ref, k_ref, v_ref,
    kt_ref, uw_ref, pair_ref, sent_ref, prior_ref, pad_ref, mask_ref,
):
    step = pl.program_id(0)

    @pl.when(step == 0)
    def _():
        make_masks(mask_ref)

    length = k_ref.shape[0]
    blocks = length // BLK
    turned_g = pltpu.roll(g_ref[...], BLK - HEADS_PER_STEP * step, 1)
    lowers, rights, tails, lasts = [], [], [], []
    for head in range(HEADS_PER_STEP):
        lanes = slice(head * BLK, (head + 1) * BLK)
        fill_padded(pad_ref, 2 * head, k_ref, halo_ref[1, :, lanes], lanes)
        fill_padded(pad_ref, 2 * head + 1, v_ref, halo_ref[2, :, lanes], lanes)
        for block in range(blocks):
            start = block * BLK
            tokens = slice(start, start + BLK)
            keys = unit(conv_rows(pad_ref, 2 * head, taps_ref[1, :, lanes], start, BLK)).astype(BF)
            values = conv_rows(pad_ref, 2 * head + 1, taps_ref[2, :, lanes], start, BLK).astype(BF)
            keys_f = keys.astype(F32)
            turned = keys_f.T
            turned_b = turned.astype(BF)
            kt_ref[head, :, tokens] = turned_b
            g_col = jnp.broadcast_to(turned_g[tokens, head : head + 1], (BLK, BLK))
            g_row = rows_ref[head, 0:1, tokens]
            beta_row = rows_ref[head, 1:2, tokens]
            g_last = g_row[:, BLK - 1 : BLK]
            lowers.append(decay_matrix(g_col, g_row, beta_row) * dot(keys, turned_b))
            rights.append(
                jnp.concatenate([values, (jnp.exp(g_col) * keys_f).astype(BF)], axis=1)
            )
            tails.append((turned * (jnp.exp(g_last - g_row) * beta_row)).astype(BF))
            lasts.append(jnp.exp(g_last))
    solved = inverses(lowers, mask_ref)
    maps = []
    for head in range(HEADS_PER_STEP):
        for block in range(blocks):
            i = head * blocks + block
            fresh = dot(solved[i].astype(BF), rights[i]).astype(BF)
            uw_ref[head, block * BLK : (block + 1) * BLK, :] = fresh
            maps.append(dot(tails[i], fresh))
    eye = jnp.where(iota2((BLK, BLK), 0) == iota2((BLK, BLK), 1), 1.0, 0.0).astype(F32)
    for head in range(HEADS_PER_STEP):
        i = head * blocks
        state_a = lasts[i] * eye - maps[i][:, BLK:]
        state_b = maps[i][:, :BLK]
        for block in range(1, blocks):
            i = head * blocks + block
            state = jnp.concatenate([state_a, state_b], axis=1)
            low = state.astype(BF)
            prior_ref[head, block - 1] = low
            state = lasts[i] * state - dot(maps[i][:, BLK:].astype(BF), low)
            state_a = state[:, :BLK]
            state_b = state[:, BLK:] + maps[i][:, :BLK]
        state = jnp.concatenate([state_a, state_b], axis=1)
        pair_ref[head] = state
        sent_ref[head] = state.astype(BF)


def query_side(
    odd_ref, rows_ref, g_ref, weight_ref, taps_ref, halo_ref, q_ref, kt_ref, uw_ref, prior_ref,
    near_ref, *rest, first_step,
):
    scaled_ref, base_ref, pad_ref = rest[-3:]
    step = pl.program_id(0) + first_step
    length = q_ref.shape[0]
    blocks = length // BLK
    levels = scaled_ref.shape[1] // (HEADS_PER_STEP * BLK) + 1
    per_head = levels + 1
    width = weight_ref.shape[1]
    odd = odd_ref[0].astype(F32)
    turned_g = pltpu.roll(g_ref[...], BLK - HEADS_PER_STEP * step, 1)
    turned_w = pltpu.roll(weight_ref[...], width - HEADS_PER_STEP * per_head * step, 1)
    for head in range(HEADS_PER_STEP):
        lanes = slice(head * BLK, (head + 1) * BLK)
        fill_padded(pad_ref, head, q_ref, halo_ref[0, :, lanes], lanes)
        near = near_ref[head] * odd.astype(BF)
        first = head * per_head
        for block in range(blocks):
            start = block * BLK
            tokens = slice(start, start + BLK)
            queries = unit(conv_rows(pad_ref, head, taps_ref[0, :, lanes], start, BLK)).astype(BF)
            g_col = jnp.broadcast_to(turned_g[tokens, head : head + 1], (BLK, BLK))
            g_row = rows_ref[head, 0:1, tokens]
            beta_row = rows_ref[head, 1:2, tokens]
            mixing = (
                decay_matrix(g_col, g_row, beta_row) * dot(queries, kt_ref[head, :, tokens])
            ).astype(BF)
            inner = dot(mixing, uw_ref[head, tokens, :])
            through = jnp.exp(g_col) * queries.astype(F32) - inner[:, BLK:]
            if block == 0:
                carried, local = through, inner[:, :BLK]
            else:
                passed = dot(through.astype(BF), prior_ref[head, block - 1])
                carried, local = passed[:, :BLK], inner[:, :BLK] + passed[:, BLK:]
            scaled = [
                (carried * turned_w[tokens, first + level : first + level + 1]).astype(BF)
                for level in range(1, per_head)
            ]
            base_ref[tokens, lanes] = turned_w[tokens, first : first + 1] * local + dot(
                scaled[0], near
            )
            begin = head * (levels - 1) * BLK
            scaled_ref[tokens, begin : begin + (levels - 1) * BLK] = jnp.concatenate(
                scaled[1:], axis=1
            )


def finish_side(
    core_ref, gain_ref, z_ref, base_ref, scaled_ref, near_ref, own_ref, other_ref, out_ref
):
    step = pl.program_id(0)
    core = core_ref[0]
    length = z_ref.shape[0]
    blocks = length // BLK
    levels = own_ref.shape[2] // BLK
    mine = step // (pl.num_programs(0) // 2) == core
    eye = jnp.where(iota2((BLK, BLK), 0) == iota2((BLK, BLK), 1), 1.0, 0.0).astype(BF)
    for head in range(HEADS_PER_STEP):
        lanes = slice(head * BLK, (head + 1) * BLK)
        reach = jnp.where(core == 1, near_ref[head], eye)
        seen = dot(reach, jnp.where(mine, own_ref[head], other_ref[head])).astype(BF)
        states = jnp.concatenate(
            [seen[:, level * BLK : (level + 1) * BLK] for level in range(levels)], axis=0
        )
        begin = head * levels * BLK
        for block in range(blocks):
            tokens = slice(block * BLK, (block + 1) * BLK)
            opened = base_ref[tokens, lanes] + dot(
                scaled_ref[tokens, begin : begin + levels * BLK], states
            )
            square = jnp.sum(opened * opened, axis=-1, keepdims=True) * (1.0 / BLK)
            normed = opened * lax.rsqrt(square + EPS) * gain_ref[...]
            gate = z_ref[tokens, lanes].astype(F32)
            out_ref[tokens, lanes] = (normed * silu(gate)).astype(BF)


def merged(left, right_a, right_b):
    moved = dot(right_a.astype(BF), left.astype(BF))
    return jnp.concatenate([moved[:, :BLK], moved[:, BLK:] + right_b.astype(F32)], axis=1)


def join_near(core_ref, pair_ref, far_ref, next_ref, sent_ref):
    @pl.when(core_ref[0] == 1)
    def _():
        for head in range(pair_ref.shape[0]):
            own = pair_ref[head]
            joined = merged(far_ref[head], own[:, :BLK], own[:, BLK:])
            next_ref[head] = joined
            sent_ref[head] = joined.astype(BF)

    @pl.when(core_ref[0] == 0)
    def _():
        for head in range(pair_ref.shape[0]):
            far = far_ref[head]
            joined = merged(pair_ref[head], far[:, :BLK], far[:, BLK:])
            next_ref[head] = joined
            sent_ref[head] = joined.astype(BF)


def join_far(upper_ref, pair_ref, far_ref, *rest):
    next_ref, sent_ref, state_ref, onward_ref = rest[-4:]
    reach_ref = rest[0] if len(rest) == 5 else None

    @pl.when(upper_ref[0] == 1)
    def _():
        for head in range(pair_ref.shape[0]):
            far = far_ref[head]
            own = pair_ref[head]
            seen = far if reach_ref is None else dot(reach_ref[head], far).astype(BF)
            onward_ref[head] = seen[:, :BLK]
            state_ref[head] = seen[:, BLK:]
            joined = merged(far, own[:, :BLK], own[:, BLK:])
            next_ref[head] = joined
            sent_ref[head] = joined.astype(BF)

    @pl.when(upper_ref[0] == 0)
    def _():
        for head in range(pair_ref.shape[0]):
            far = far_ref[head]
            joined = merged(pair_ref[head], far[:, :BLK], far[:, BLK:])
            next_ref[head] = joined
            sent_ref[head] = joined.astype(BF)
            state_ref[head] = jnp.zeros((BLK, BLK), BF)
            if reach_ref is None:
                row, col = iota2((BLK, BLK), 0), iota2((BLK, BLK), 1)
                onward_ref[head] = jnp.where(row == col, 1.0, 0.0).astype(BF)
            else:
                onward_ref[head] = reach_ref[head]


def join_top(upper_ref, far_ref, reach_ref, *rest):
    state_refs, out_ref = rest[:-1], rest[-1]
    levels = len(state_refs)
    for level in range(levels):
        for head in range(far_ref.shape[0]):
            out_ref[head, :, level * BLK : (level + 1) * BLK] = state_refs[level][head]

    @pl.when(upper_ref[0] == 1)
    def _():
        for head in range(far_ref.shape[0]):
            out_ref[head, :, levels * BLK :] = dot(reach_ref[head], far_ref[head]).astype(BF)

    @pl.when(upper_ref[0] == 0)
    def _():
        for head in range(far_ref.shape[0]):
            out_ref[head, :, levels * BLK :] = jnp.zeros((BLK, BLK), BF)


def shape_of(shape, dtype):
    return jax.ShapeDtypeStruct(shape, dtype)


def whole(shape):
    return pl.BlockSpec(shape, lambda i: (0,) * len(shape))


def by_head(shape, first=0, lane=0):
    tail = (0,) * (len(shape) - 1) + (lane,)
    return pl.BlockSpec((HEADS_PER_STEP,) + shape, lambda i: (i + first,) + tail)


def by_column(shape, first=0):
    lead = len(shape) - 1
    return pl.BlockSpec(shape, lambda i: (0,) * lead + (i + first,))


ANY = pl.BlockSpec(memory_space=pl.ANY)
SMEM = pl.BlockSpec(memory_space=pltpu.SMEM)
JOIN_STEPS = 2


def bit(position, level):
    return (position // 2**level % 2).astype(jnp.int32).reshape(1)


def per_device(q_in, k_in, v_in, z_in, log_gate, beta, level_weight, conv_weight, norm_gain):
    length, heads = log_gate.shape
    blocks = length // BLK
    width = HEADS_PER_STEP * BLK
    steps = heads // HEADS_PER_STEP
    half = heads // 2
    ctx = lax.axis_size("ctx")
    levels = ctx.bit_length() - 1
    position = lax.axis_index("ctx")
    edge = jnp.stack([x[length - 4 :] for x in (q_in, k_in, v_in)], axis=0)
    halo = lax.ppermute(edge, "ctx", [(i, i + 1) for i in range(ctx - 1)])

    g = jnp.cumsum(log_gate.reshape(blocks, BLK, heads), axis=1).reshape(length, heads)
    g_pad = jnp.pad(g, ((0, 0), (0, BLK - heads)))
    rows = jnp.stack([g.T, beta.T], axis=1)
    weights = level_weight[:, :, : levels + 1].reshape(length, heads * (levels + 1))
    weights = jnp.pad(weights, ((0, 0), (0, -weights.shape[1] % BLK)))
    core = bit(position, 0)

    params = pltpu.CompilerParams(dimension_semantics=("arbitrary",), vmem_limit_bytes=60 << 20)
    cost = pl.CostEstimate(flops=10**10, bytes_accessed=2 * 10**7, transcendentals=10**7)
    kt, uw, pair, sent, prior = pl.pallas_call(
        key_side,
        grid=(steps,),
        in_specs=[
            by_head((2, length)), whole(g_pad.shape), by_column((3, 4, width)),
            by_column((3, 4, width)), by_column((length, width)), by_column((length, width)),
        ],
        out_specs=[
            by_head((BLK, length)), by_head((length, 2 * BLK)), by_head((BLK, 2 * BLK)),
            by_head((BLK, 2 * BLK)), by_head((blocks - 1, BLK, 2 * BLK)),
        ],
        out_shape=[
            shape_of((heads, BLK, length), BF), shape_of((heads, length, 2 * BLK), BF),
            shape_of((heads, BLK, 2 * BLK), F32), shape_of((heads, BLK, 2 * BLK), BF),
            shape_of((heads, blocks - 1, BLK, 2 * BLK), BF),
        ],
        scratch_shapes=[
            pltpu.VMEM((2 * HEADS_PER_STEP, length + 8, BLK), F32),
            pltpu.VMEM((6, BLK, BLK), BF),
        ],
        compiler_params=params,
        cost_estimate=cost,
        name="key_side",
    )(rows, g_pad, conv_weight, halo, k_in, v_in)
    near = lax.ppermute(sent, "ctx", [(i, i ^ 1) for i in range(ctx)])

    def queries_of(first, queries, previous):
        count = len(previous)
        scaled_width = width * (levels - 1)
        return pl.pallas_call(
            functools.partial(query_side, first_step=first),
            grid=(steps // 2,),
            in_specs=[
                SMEM, by_head((2, length), first), whole(g_pad.shape), whole(weights.shape),
                by_column((3, 4, width), first), by_column((3, 4, width), first),
                by_column((length, width), first), by_head((BLK, length), first),
                by_head((length, 2 * BLK), first), by_head((blocks - 1, BLK, 2 * BLK), first),
                by_head((BLK, BLK), first, 1),
            ]
            + [ANY] * count,
            out_specs=[by_column((length, scaled_width), first), by_column((length, width), first)],
            out_shape=[
                shape_of((length, heads * (levels - 1) * BLK), BF), shape_of(q_in.shape, F32)
            ],
            scratch_shapes=[pltpu.VMEM((HEADS_PER_STEP, length + 8, BLK), F32)],
            input_output_aliases={11 + i: i for i in range(count)},
            compiler_params=params,
            cost_estimate=cost,
            name="query_side",
        )(
            core, rows, g_pad, weights, conv_weight, halo, queries, kt, uw, prior, near, *previous
        )

    group = half // JOIN_STEPS
    joined_shapes = [
        shape_of((half, BLK, 2 * BLK), F32), shape_of((half, BLK, 2 * BLK), BF),
    ]

    def part(lanes):
        return pl.BlockSpec((group, BLK, lanes), lambda i, *_: (i, 0, 0))

    chosen = pl.BlockSpec((group, BLK, 2 * BLK), lambda i, which: (which[0] * JOIN_STEPS + i, 0, 0))
    pair, sent = pl.pallas_call(
        join_near,
        grid_spec=pltpu.PrefetchScalarGridSpec(
            num_scalar_prefetch=1, grid=(JOIN_STEPS,), in_specs=[chosen, chosen],
            out_specs=[part(2 * BLK)] * 2,
        ),
        out_shape=joined_shapes,
        name="join_near",
    )(core, pair, near)

    square = shape_of((half, BLK, BLK), BF)
    reach, states, parts = None, [], ()
    for level in range(1, levels - 1):
        far = lax.ppermute(sent, "ctx", [(i, i ^ 2**level) for i in range(ctx)])
        if level == 1:
            parts = queries_of(0, q_in, ())
            far, *parts = lax.optimization_barrier((far, *parts))
        given = (pair, far) if reach is None else (pair, far, reach)
        pair, sent, state, reach = pl.pallas_call(
            join_far,
            grid=(JOIN_STEPS,),
            in_specs=[SMEM, part(2 * BLK), part(2 * BLK)] + [part(BLK)] * (len(given) - 2),
            out_specs=[part(2 * BLK), part(2 * BLK), part(BLK), part(BLK)],
            out_shape=joined_shapes + [square, square],
            name="join_far",
        )(bit(position, level), *given)
        states.append(state)
    top = levels - 1
    sent_b, later_q = lax.optimization_barrier((sent[:, :, BLK:], q_in))
    far = lax.ppermute(sent_b, "ctx", [(i, i + 2**top) for i in range(ctx - 2**top)])
    parts = queries_of(steps // 2, later_q, parts)
    far, scaled, base = lax.optimization_barrier((far, *parts))
    own = pl.pallas_call(
        join_top,
        grid=(JOIN_STEPS,),
        in_specs=[SMEM] + [part(BLK)] * (2 + len(states)),
        out_specs=part((levels - 1) * BLK),
        out_shape=shape_of((half, BLK, (levels - 1) * BLK), BF),
        name="join_top",
    )(bit(position, top), far, reach, *states)
    other = lax.ppermute(own, "ctx", [(i, i ^ 1) for i in range(ctx)])
    fold = steps // 2
    from_half = pl.BlockSpec(
        (HEADS_PER_STEP, BLK, (levels - 1) * BLK), lambda i: (i % fold, 0, 0)
    )
    return pl.pallas_call(
        finish_side,
        grid=(steps,),
        in_specs=[
            SMEM, whole((1, BLK)), by_column((length, width)), by_column((length, width)),
            by_column((length, width * (levels - 1))), by_head((BLK, BLK)), from_half, from_half,
        ],
        out_specs=by_column((length, width)),
        out_shape=shape_of(z_in.shape, BF),
        compiler_params=params,
        name="finish_side",
    )(core, norm_gain.reshape(1, BLK), z_in, base, scaled, near, own, other)


def solution(mesh):
    placed = (
        P(("batch", "ctx"), None),
        P(("batch", "ctx"), None),
        P(("batch", "ctx"), None),
        P(("batch", "ctx"), None),
        P(("batch", "ctx"), None),
        P(("batch", "ctx"), None),
        P(("batch", "ctx"), None, None),
        P(),
        P(),
    )
    return jax.shard_map(
        per_device, mesh=mesh, in_specs=placed, out_specs=P(("batch", "ctx"), None), check_vma=False
    )
```

```python
import functools

import jax
import jax.numpy as jnp
from jax import lax
from jax.experimental import pallas as pl
from jax.experimental.pallas import tpu as pltpu
from jax.sharding import PartitionSpec as P

BLK = 128
SUB = 16
KEY_HEADS = 4
QUERY_HEADS = 2
FINISH_HEADS = 4
EPS = 1e-06
BF = jnp.bfloat16
F32 = jnp.float32


def dot(first, second):
    return lax.dot_general(
        first, second, (((1,), (0,)), ((), ())), preferred_element_type=F32
    )


def silu(value):
    return value * pl.reciprocal(1.0 + jnp.exp(-value), approx=False)


def fill_padded(pad_ref, slot, x_ref, halo, lanes):
    pad_ref[slot, 4:8, :] = halo.astype(F32)
    pad_ref[slot, 8:, :] = x_ref[:, lanes].astype(F32)


def conv_rows(pad_ref, slot, taps, start, count):
    total = taps[0:1] * pad_ref[slot, start + 5 : start + 5 + count, :]
    for tap in range(1, 4):
        total = total + taps[tap : tap + 1] * pad_ref[
            slot, start + 5 + tap : start + 5 + tap + count, :
        ]
    return silu(total)


def unit(rows):
    return rows * lax.rsqrt(jnp.sum(rows * rows, axis=-1, keepdims=True) + EPS)


def iota2(shape, dim):
    return lax.broadcasted_iota(jnp.int32, shape, dim)


def decay_matrix(g_col, g_row, beta_row):
    size = g_col.shape[0]
    causal = iota2((size, BLK), 1) <= iota2((size, BLK), 0)
    return jnp.exp(jnp.where(causal, g_col - g_row, -1e30)) * beta_row


def make_masks(mask_ref):
    row, col = iota2((BLK, BLK), 0), iota2((BLK, BLK), 1)
    size, index = SUB, 0
    while size < BLK:
        same = row // size == col // size
        pair = row // (2 * size) == col // (2 * size)
        high_low = pair & (row // size % 2 == 1) & (col // size % 2 == 0)
        mask_ref[index] = jnp.where(same, 1.0, 0.0).astype(BF)
        mask_ref[index + 1] = jnp.where(high_low, 1.0, 0.0).astype(BF)
        size, index = size * 2, index + 2


def tiled(packed, times, mask):
    return jnp.concatenate([packed.astype(BF)] * times, axis=0) * mask


def picked(lower, size, offset):
    groups = BLK // size if offset is None else BLK // (2 * size)
    step = size if offset is None else 2 * size
    first = 0 if offset is None else offset
    lane = iota2((size, BLK), 1) // step
    out = lower[first : first + size]
    for group in range(1, groups):
        begin = first + group * step
        out = jnp.where(lane == group, lower[begin : begin + size], out)
    return out


def inverses(lowers, mask_ref):
    count = len(lowers)
    every = range(count)
    row, col = iota2((SUB, BLK), 0), iota2((SUB, BLK), 1) % SUB
    eye = jnp.where(row == col, 1.0, 0.0).astype(F32)
    strict = col < row
    same = mask_ref[0]
    times = BLK // SUB
    powers = [jnp.where(strict, -picked(lower, SUB, None), 0.0) for lower in lowers]
    results = [eye + power for power in powers]
    powers = [dot(p.astype(BF), tiled(p, times, same)) for p in powers]
    reach = 2
    while reach < SUB // 2:
        both = [
            dot(
                jnp.concatenate([powers[i].astype(BF), results[i].astype(BF)], axis=0),
                tiled(powers[i], times, same),
            )
            for i in every
        ]
        powers = [b[:SUB] for b in both]
        results = [results[i] + both[i][SUB:] for i in every]
        reach *= 2
    results = [
        results[i] + dot(results[i].astype(BF), tiled(powers[i], times, same)) for i in every
    ]
    size, index = SUB, 0
    while size < BLK:
        times = BLK // size
        low = iota2((size, BLK), 1) // size % 2 == 0
        cross = [picked(lower, size, size).astype(BF) for lower in lowers]
        moved = [dot(cross[i], tiled(results[i], times, mask_ref[index])) for i in every]
        turned = [
            dot(results[i].astype(BF), tiled(moved[i], times, mask_ref[index + 1]))
            for i in every
        ]
        results = [
            jnp.concatenate(
                [jnp.where(low, results[i], 0.0), jnp.where(low, -turned[i], results[i])], axis=0
            )
            for i in every
        ]
        size, index = size * 2, index + 2
    return results


def key_side(
    rows_ref, g_ref, taps_ref, halo_ref, k_ref, v_ref,
    kt_ref, uw_ref, pair_ref, prior_ref, pad_ref, mask_ref,
):
    step = pl.program_id(0)

    @pl.when(step == 0)
    def _():
        make_masks(mask_ref)

    length = k_ref.shape[0]
    blocks = length // BLK
    turned_g = pltpu.roll(g_ref[...], BLK - KEY_HEADS * step, 1)
    lowers, rights, tails, lasts = [], [], [], []
    for head in range(KEY_HEADS):
        lanes = slice(head * BLK, (head + 1) * BLK)
        fill_padded(pad_ref, 2 * head, k_ref, halo_ref[1, :, lanes], lanes)
        fill_padded(pad_ref, 2 * head + 1, v_ref, halo_ref[2, :, lanes], lanes)
        for block in range(blocks):
            start = block * BLK
            tokens = slice(start, start + BLK)
            keys = unit(conv_rows(pad_ref, 2 * head, taps_ref[1, :, lanes], start, BLK)).astype(BF)
            values = conv_rows(pad_ref, 2 * head + 1, taps_ref[2, :, lanes], start, BLK).astype(BF)
            keys_f = keys.astype(F32)
            turned = keys_f.T
            turned_b = turned.astype(BF)
            kt_ref[head, :, tokens] = turned_b
            g_col = jnp.broadcast_to(turned_g[tokens, head : head + 1], (BLK, BLK))
            g_row = rows_ref[head, 0:1, tokens]
            beta_row = rows_ref[head, 1:2, tokens]
            g_last = g_row[:, BLK - 1 : BLK]
            lowers.append(decay_matrix(g_col, g_row, beta_row) * dot(keys, turned_b))
            rights.append(
                jnp.concatenate([values, (jnp.exp(g_col) * keys_f).astype(BF)], axis=1)
            )
            tails.append((turned * (jnp.exp(g_last - g_row) * beta_row)).astype(BF))
            lasts.append(jnp.exp(g_last))
    solved = inverses(lowers, mask_ref)
    maps = []
    for head in range(KEY_HEADS):
        for block in range(blocks):
            i = head * blocks + block
            fresh = dot(solved[i].astype(BF), rights[i]).astype(BF)
            uw_ref[head, block * BLK : (block + 1) * BLK, :] = fresh
            maps.append(dot(tails[i], fresh))
    eye = jnp.where(iota2((BLK, BLK), 0) == iota2((BLK, BLK), 1), 1.0, 0.0).astype(F32)
    for head in range(KEY_HEADS):
        i = head * blocks
        state_a = lasts[i] * eye - maps[i][:, BLK:]
        state_b = maps[i][:, :BLK]
        for block in range(1, blocks):
            i = head * blocks + block
            state = jnp.concatenate([state_a, state_b], axis=1)
            low = state.astype(BF)
            prior_ref[head, block - 1] = low
            state = lasts[i] * state - dot(maps[i][:, BLK:].astype(BF), low)
            state_a = state[:, :BLK]
            state_b = state[:, BLK:] + maps[i][:, :BLK]
        state = jnp.concatenate([state_a, state_b], axis=1)
        pair_ref[head] = state.astype(BF)


def query_side(
    odd_ref, rows_ref, g_ref, weight_ref, taps_ref, halo_ref, q_ref, kt_ref, uw_ref, prior_ref,
    near_ref, *rest, first_step,
):
    scaled_ref, base_ref, pad_ref = rest[-3:]
    step = pl.program_id(0) + first_step
    length = q_ref.shape[0]
    blocks = length // BLK
    levels = scaled_ref.shape[1] // (QUERY_HEADS * BLK) + 1
    per_head = levels + 1
    width = weight_ref.shape[1]
    odd = odd_ref[0].astype(F32)
    turned_g = pltpu.roll(g_ref[...], BLK - QUERY_HEADS * step, 1)
    turned_w = pltpu.roll(weight_ref[...], width - QUERY_HEADS * per_head * step, 1)
    for head in range(QUERY_HEADS):
        lanes = slice(head * BLK, (head + 1) * BLK)
        fill_padded(pad_ref, head, q_ref, halo_ref[0, :, lanes], lanes)
        near = near_ref[head] * odd.astype(BF)
        first = head * per_head
        for block in range(blocks):
            start = block * BLK
            tokens = slice(start, start + BLK)
            queries = unit(conv_rows(pad_ref, head, taps_ref[0, :, lanes], start, BLK)).astype(BF)
            g_col = jnp.broadcast_to(turned_g[tokens, head : head + 1], (BLK, BLK))
            g_row = rows_ref[head, 0:1, tokens]
            beta_row = rows_ref[head, 1:2, tokens]
            mixing = (
                decay_matrix(g_col, g_row, beta_row) * dot(queries, kt_ref[head, :, tokens])
            ).astype(BF)
            inner = dot(mixing, uw_ref[head, tokens, :])
            through = jnp.exp(g_col) * queries.astype(F32) - inner[:, BLK:]
            if block == 0:
                carried, local = through, inner[:, :BLK]
            else:
                passed = dot(through.astype(BF), prior_ref[head, block - 1])
                carried, local = passed[:, :BLK], inner[:, :BLK] + passed[:, BLK:]
            scaled = [
                (carried * turned_w[tokens, first + level : first + level + 1]).astype(BF)
                for level in range(1, per_head)
            ]
            base_ref[tokens, lanes] = turned_w[tokens, first : first + 1] * local + dot(
                scaled[0], near
            )
            begin = head * (levels - 1) * BLK
            scaled_ref[tokens, begin : begin + (levels - 1) * BLK] = jnp.concatenate(
                scaled[1:], axis=1
            )


def finish_side(
    core_ref, gain_ref, z_ref, base_ref, scaled_ref, near_ref, own_ref, far_ref, out_ref,
    other_ref, sem,
):
    step = pl.program_id(0)
    core = core_ref[0]
    length = z_ref.shape[0]
    blocks = length // BLK
    levels = own_ref.shape[2] // BLK
    fold = pl.num_programs(0) // 2
    mine = step // fold == core
    begin_head = step % fold * FINISH_HEADS

    @pl.when(step == 0)
    def _():
        fetch([(far_ref, other_ref)], sem)

    eye = jnp.where(iota2((BLK, BLK), 0) == iota2((BLK, BLK), 1), 1.0, 0.0).astype(BF)
    for head in range(FINISH_HEADS):
        lanes = slice(head * BLK, (head + 1) * BLK)
        reach = jnp.where(core == 1, near_ref[head], eye)
        seen = dot(reach, jnp.where(mine, own_ref[head], other_ref[begin_head + head])).astype(BF)
        states = jnp.concatenate(
            [seen[:, level * BLK : (level + 1) * BLK] for level in range(levels)], axis=0
        )
        begin = head * levels * BLK
        for block in range(blocks):
            tokens = slice(block * BLK, (block + 1) * BLK)
            opened = base_ref[tokens, lanes] + dot(
                scaled_ref[tokens, begin : begin + levels * BLK], states
            )
            square = jnp.sum(opened * opened, axis=-1, keepdims=True) * (1.0 / BLK)
            normed = opened * lax.rsqrt(square + EPS) * gain_ref[...]
            gate = z_ref[tokens, lanes].astype(F32)
            out_ref[tokens, lanes] = (normed * silu(gate)).astype(BF)


def merged(left, right_a, right_b):
    moved = dot(right_a.astype(BF), left.astype(BF))
    return jnp.concatenate([moved[:, :BLK], moved[:, BLK:] + right_b.astype(F32)], axis=1)


def fetch(pairs, sem):
    copies = [
        pltpu.make_async_copy(source, target, sem.at[i])
        for i, (source, target) in enumerate(pairs)
    ]
    for copy in copies:
        copy.start()
    for copy in copies:
        copy.wait()


def join_near(core_ref, pair_ref, far_ref, next_ref, own, far, sem):
    core = core_ref[0]
    half = pl.ds(core * own.shape[0], own.shape[0])
    fetch([(pair_ref.at[half], own), (far_ref.at[half], far)], sem)

    @pl.when(core == 1)
    def _():
        for head in range(own.shape[0]):
            next_ref[head] = merged(far[head], own[head, :, :BLK], own[head, :, BLK:]).astype(BF)

    @pl.when(core == 0)
    def _():
        for head in range(own.shape[0]):
            next_ref[head] = merged(own[head], far[head, :, :BLK], far[head, :, BLK:]).astype(BF)


def join_far(upper_ref, pair_ref, far_ref, *rest):
    next_ref, state_ref, onward_ref, own, far, sem = rest[-6:]
    reach_ref = rest[0] if len(rest) == 7 else None
    lanes = slice(2 * BLK - next_ref.shape[2], 2 * BLK)
    fetch([(pair_ref, own), (far_ref, far)], sem)

    @pl.when(upper_ref[0] == 1)
    def _():
        for head in range(own.shape[0]):
            seen = far[head] if reach_ref is None else dot(reach_ref[head], far[head]).astype(BF)
            onward_ref[head] = seen[:, :BLK]
            state_ref[head] = seen[:, BLK:]
            joined = merged(far[head], own[head, :, :BLK], own[head, :, BLK:]).astype(BF)
            next_ref[head] = joined[:, lanes]

    @pl.when(upper_ref[0] == 0)
    def _():
        row, col = iota2((BLK, BLK), 0), iota2((BLK, BLK), 1)
        for head in range(own.shape[0]):
            joined = merged(own[head], far[head, :, :BLK], far[head, :, BLK:]).astype(BF)
            next_ref[head] = joined[:, lanes]
            state_ref[head] = jnp.zeros((BLK, BLK), BF)
            if reach_ref is None:
                onward_ref[head] = jnp.where(row == col, 1.0, 0.0).astype(BF)
            else:
                onward_ref[head] = reach_ref[head]


def join_top(upper_ref, far_ref, reach_ref, *rest):
    state_refs, (out_ref, far, sem) = rest[:-3], rest[-3:]
    levels = len(state_refs)
    fetch([(far_ref, far)], sem)
    for level in range(levels):
        for head in range(far.shape[0]):
            out_ref[head, :, level * BLK : (level + 1) * BLK] = state_refs[level][head]

    @pl.when(upper_ref[0] == 1)
    def _():
        for head in range(far.shape[0]):
            out_ref[head, :, levels * BLK :] = dot(reach_ref[head], far[head]).astype(BF)

    @pl.when(upper_ref[0] == 0)
    def _():
        for head in range(far.shape[0]):
            out_ref[head, :, levels * BLK :] = jnp.zeros((BLK, BLK), BF)


def shape_of(shape, dtype):
    return jax.ShapeDtypeStruct(shape, dtype)


def whole(shape):
    return pl.BlockSpec(shape, lambda i: (0,) * len(shape))


def by_head(count, shape, first=0, lane=0):
    tail = (0,) * (len(shape) - 1) + (lane,)
    return pl.BlockSpec((count,) + shape, lambda i: (i + first,) + tail)


def by_column(shape, first=0):
    lead = len(shape) - 1
    return pl.BlockSpec(shape, lambda i: (0,) * lead + (i + first,))


ANY = pl.BlockSpec(memory_space=pl.ANY)
SMEM = pl.BlockSpec(memory_space=pltpu.SMEM)
VMEM = pl.BlockSpec(memory_space=pltpu.VMEM)
COST = pl.CostEstimate(flops=10**10, bytes_accessed=2 * 10**7, transcendentals=10**7)
PARAMS = pltpu.CompilerParams(dimension_semantics=("arbitrary",), vmem_limit_bytes=62 << 20)

SMALL = pltpu.CompilerParams(vmem_limit_bytes=8 << 20)


def bit(position, level):
    return (position // 2**level % 2).astype(jnp.int32).reshape(1)


def keys_of(rows, g_pad, conv_weight, halo, k_in, v_in):
    heads, _, length = rows.shape
    blocks = length // BLK
    width = KEY_HEADS * BLK
    return pl.pallas_call(
        key_side,
        grid=(heads // KEY_HEADS,),
        in_specs=[
            by_head(KEY_HEADS, (2, length)), whole(g_pad.shape), by_column((3, 4, width)),
            by_column((3, 4, width)), by_column((length, width)), by_column((length, width)),
        ],
        out_specs=[
            by_head(KEY_HEADS, (BLK, length)), by_head(KEY_HEADS, (length, 2 * BLK)),
            by_head(KEY_HEADS, (BLK, 2 * BLK)), by_head(KEY_HEADS, (blocks - 1, BLK, 2 * BLK)),
        ],
        out_shape=[
            shape_of((heads, BLK, length), BF), shape_of((heads, length, 2 * BLK), BF),
            shape_of((heads, BLK, 2 * BLK), BF), shape_of((heads, blocks - 1, BLK, 2 * BLK), BF),
        ],
        scratch_shapes=[
            pltpu.VMEM((2 * KEY_HEADS, length + 8, BLK), F32),
            pltpu.VMEM((6, BLK, BLK), BF),
        ],
        compiler_params=PARAMS,
        cost_estimate=COST,
        name="key_side",
    )(rows, g_pad, conv_weight, halo, k_in, v_in)


def queries_of(second, levels, core, rows, g_pad, weights, taps, halo, q_in, kt, uw, prior, near, previous):
    heads, _, length = rows.shape
    blocks = length // BLK
    steps = heads // QUERY_HEADS // 2
    first = steps if second else 0
    width = QUERY_HEADS * BLK
    scaled_width = width * (levels - 1)
    count = len(previous)
    return pl.pallas_call(
        functools.partial(query_side, first_step=first),
        grid=(steps,),
        in_specs=[
            SMEM, by_head(QUERY_HEADS, (2, length), first), whole(g_pad.shape),
            whole(weights.shape), by_column((3, 4, width), first), by_column((3, 4, width), first),
            by_column((length, width), first), by_head(QUERY_HEADS, (BLK, length), first),
            by_head(QUERY_HEADS, (length, 2 * BLK), first),
            by_head(QUERY_HEADS, (blocks - 1, BLK, 2 * BLK), first),
            by_head(QUERY_HEADS, (BLK, BLK), first, 1),
        ]
        + [ANY] * count,
        out_specs=[by_column((length, scaled_width), first), by_column((length, width), first)],
        out_shape=[shape_of((length, heads * (levels - 1) * BLK), BF), shape_of(q_in.shape, F32)],
        scratch_shapes=[pltpu.VMEM((QUERY_HEADS, length + 8, BLK), F32)],
        input_output_aliases={11 + i: i for i in range(count)},
        compiler_params=PARAMS,
        cost_estimate=COST,
        name="query_side",
    )(core, rows, g_pad, weights, taps, halo, q_in, kt, uw, prior, near, *previous)


def finished(core, gain, z_in, base, scaled, near, own, other):
    length = z_in.shape[0]
    heads, levels = near.shape[0], own.shape[2] // BLK
    width = FINISH_HEADS * BLK
    fold = heads // FINISH_HEADS // 2
    return pl.pallas_call(
        finish_side,
        grid=(2 * fold,),
        in_specs=[
            SMEM, whole(gain.shape), by_column((length, width)), by_column((length, width)),
            by_column((length, width * levels)), by_head(FINISH_HEADS, (BLK, BLK)),
            pl.BlockSpec((FINISH_HEADS, BLK, levels * BLK), lambda i: (i % fold, 0, 0)), ANY,
        ],
        out_specs=by_column((length, width)),
        out_shape=shape_of(z_in.shape, BF),
        scratch_shapes=[pltpu.VMEM(other.shape, BF), pltpu.SemaphoreType.DMA((1,))],
        compiler_params=PARAMS,
        name="finish_side",
    )(core, gain, z_in, base, scaled, near, own, other)


def joined_near(core, pair, near):
    shape = (pair.shape[0] // 2,) + pair.shape[1:]
    return pl.pallas_call(
        join_near,
        in_specs=[SMEM, ANY, ANY],
        out_specs=VMEM,
        out_shape=shape_of(shape, BF),
        scratch_shapes=[
            pltpu.VMEM(shape, BF), pltpu.VMEM(shape, BF), pltpu.SemaphoreType.DMA((2,)),
        ],
        compiler_params=SMALL,
        name="join_near",
    )(core, pair, near)


def joined_far(upper, pair, far, reach, last):
    square = (pair.shape[0], BLK, BLK)
    given = () if reach is None else (reach,)
    return pl.pallas_call(
        join_far,
        in_specs=[SMEM, ANY, ANY] + [VMEM] * len(given),
        out_specs=[VMEM] * 3,
        out_shape=[shape_of(square if last else pair.shape, BF)] + [shape_of(square, BF)] * 2,
        scratch_shapes=[
            pltpu.VMEM(pair.shape, BF), pltpu.VMEM(pair.shape, BF), pltpu.SemaphoreType.DMA((2,)),
        ],
        compiler_params=SMALL,
        name="join_far",
    )(upper, pair, far, *given)


def joined_top(upper, far, reach, states):
    shape = (far.shape[0], BLK, (len(states) + 1) * BLK)
    return pl.pallas_call(
        join_top,
        in_specs=[SMEM, ANY] + [VMEM] * (1 + len(states)),
        out_specs=VMEM,
        out_shape=shape_of(shape, BF),
        scratch_shapes=[pltpu.VMEM(far.shape, BF), pltpu.SemaphoreType.DMA((1,))],
        compiler_params=SMALL,
        name="join_top",
    )(upper, far, reach, *states)


def per_device(q_in, k_in, v_in, z_in, log_gate, beta, level_weight, conv_weight, norm_gain):
    length, heads = log_gate.shape
    blocks = length // BLK
    ctx = lax.axis_size("ctx")
    levels = ctx.bit_length() - 1
    position = lax.axis_index("ctx")
    edge = jnp.stack([x[length - 4 :] for x in (q_in, k_in, v_in)], axis=0)
    halo = lax.ppermute(edge, "ctx", [(i, i + 1) for i in range(ctx - 1)])

    g = jnp.cumsum(log_gate.reshape(blocks, BLK, heads), axis=1).reshape(length, heads)
    g_pad = jnp.pad(g, ((0, 0), (0, BLK - heads)))
    rows = jnp.stack([g.T, beta.T], axis=1)
    weights = level_weight[:, :, : levels + 1].reshape(length, heads * (levels + 1))
    weights = jnp.pad(weights, ((0, 0), (0, -weights.shape[1] % BLK)))
    core = bit(position, 0)

    kt, uw, pair, prior = keys_of(rows, g_pad, conv_weight, halo, k_in, v_in)
    near = lax.ppermute(pair, "ctx", [(i, i ^ 1) for i in range(ctx)])
    pair = joined_near(core, pair, near)

    def queries(second, q_in, previous):
        return queries_of(
            second, levels, core, rows, g_pad, weights, conv_weight, halo, q_in, kt, uw, prior,
            near, previous,
        )

    reach, states, parts = None, [], ()
    for level in range(1, levels - 1):
        far = lax.ppermute(pair, "ctx", [(i, i ^ 2**level) for i in range(ctx)])
        if level == 1:
            parts = queries(False, q_in, ())
            far, *parts = lax.optimization_barrier((far, *parts))
        pair, state, reach = joined_far(bit(position, level), pair, far, reach, level == levels - 2)
        states.append(state)
    top = levels - 1
    pair, later_q = lax.optimization_barrier((pair, q_in))
    far = lax.ppermute(pair, "ctx", [(i, i + 2**top) for i in range(ctx - 2**top)])
    parts = queries(True, later_q, parts)
    far, scaled, base = lax.optimization_barrier((far, *parts))
    own = joined_top(bit(position, top), far, reach, states)
    other = lax.ppermute(own, "ctx", [(i, i ^ 1) for i in range(ctx)])
    return finished(core, norm_gain.reshape(1, BLK), z_in, base, scaled, near, own, other)


def solution(mesh):
    placed = (
        P(("batch", "ctx"), None),
        P(("batch", "ctx"), None),
        P(("batch", "ctx"), None),
        P(("batch", "ctx"), None),
        P(("batch", "ctx"), None),
        P(("batch", "ctx"), None),
        P(("batch", "ctx"), None, None),
        P(),
        P(),
    )
    return jax.shard_map(
        per_device, mesh=mesh, in_specs=placed, out_specs=P(("batch", "ctx"), None), check_vma=False
    )
```

```python
import functools

import jax
import jax.numpy as jnp
from jax import lax
from jax.experimental import pallas as pl
from jax.experimental.pallas import tpu as pltpu
from jax.sharding import PartitionSpec as P

BLK = 128
SUB = 16
KEY_HEADS = 4
QUERY_HEADS = 2
FINISH_HEADS = 4
EPS = 1e-06
BF = jnp.bfloat16
F32 = jnp.float32


def dot(first, second):
    return lax.dot_general(
        first, second, (((1,), (0,)), ((), ())), preferred_element_type=F32
    )


def silu(value):
    return value * pl.reciprocal(1.0 + jnp.exp(-value), approx=False)


def fill_padded(pad_ref, slot, x_ref, halo, lanes):
    pad_ref[slot, 4:8, :] = halo.astype(F32)
    pad_ref[slot, 8:, :] = x_ref[:, lanes].astype(F32)


def conv_rows(pad_ref, slot, taps, start, count):
    total = taps[0:1] * pad_ref[slot, start + 5 : start + 5 + count, :]
    for tap in range(1, 4):
        total = total + taps[tap : tap + 1] * pad_ref[
            slot, start + 5 + tap : start + 5 + tap + count, :
        ]
    return silu(total)


def unit(rows):
    return rows * lax.rsqrt(jnp.sum(rows * rows, axis=-1, keepdims=True) + EPS)


def iota2(shape, dim):
    return lax.broadcasted_iota(jnp.int32, shape, dim)


def decay_matrix(g_col, g_row, beta_row):
    size = g_col.shape[0]
    causal = iota2((size, BLK), 1) <= iota2((size, BLK), 0)
    return jnp.exp(jnp.where(causal, g_col - g_row, -1e30)) * beta_row


def make_masks(mask_ref):
    row, col = iota2((BLK, BLK), 0), iota2((BLK, BLK), 1)
    size, index = SUB, 0
    while size < BLK:
        same = row // size == col // size
        pair = row // (2 * size) == col // (2 * size)
        high_low = pair & (row // size % 2 == 1) & (col // size % 2 == 0)
        mask_ref[index] = jnp.where(same, 1.0, 0.0).astype(BF)
        mask_ref[index + 1] = jnp.where(high_low, 1.0, 0.0).astype(BF)
        size, index = size * 2, index + 2


def tiled(packed, times, mask):
    return jnp.concatenate([packed.astype(BF)] * times, axis=0) * mask


def picked(lower, size, offset):
    groups = BLK // size if offset is None else BLK // (2 * size)
    step = size if offset is None else 2 * size
    first = 0 if offset is None else offset
    lane = iota2((size, BLK), 1) // step
    out = lower[first : first + size]
    for group in range(1, groups):
        begin = first + group * step
        out = jnp.where(lane == group, lower[begin : begin + size], out)
    return out


def inverses(lowers, mask_ref):
    count = len(lowers)
    every = range(count)
    row, col = iota2((SUB, BLK), 0), iota2((SUB, BLK), 1) % SUB
    eye = jnp.where(row == col, 1.0, 0.0).astype(F32)
    strict = col < row
    same = mask_ref[0]
    times = BLK // SUB
    powers = [jnp.where(strict, -picked(lower, SUB, None), 0.0) for lower in lowers]
    results = [eye + power for power in powers]
    powers = [dot(p.astype(BF), tiled(p, times, same)) for p in powers]
    reach = 2
    while reach < SUB // 2:
        both = [
            dot(
                jnp.concatenate([powers[i].astype(BF), results[i].astype(BF)], axis=0),
                tiled(powers[i], times, same),
            )
            for i in every
        ]
        powers = [b[:SUB] for b in both]
        results = [results[i] + both[i][SUB:] for i in every]
        reach *= 2
    results = [
        results[i] + dot(results[i].astype(BF), tiled(powers[i], times, same)) for i in every
    ]
    size, index = SUB, 0
    while size < BLK:
        times = BLK // size
        low = iota2((size, BLK), 1) // size % 2 == 0
        cross = [picked(lower, size, size).astype(BF) for lower in lowers]
        moved = [dot(cross[i], tiled(results[i], times, mask_ref[index])) for i in every]
        turned = [
            dot(results[i].astype(BF), tiled(moved[i], times, mask_ref[index + 1]))
            for i in every
        ]
        results = [
            jnp.concatenate(
                [jnp.where(low, results[i], 0.0), jnp.where(low, -turned[i], results[i])], axis=0
            )
            for i in every
        ]
        size, index = size * 2, index + 2
    return results


def key_side(
    rows_ref, g_ref, taps_ref, halo_ref, k_ref, v_ref,
    kt_ref, uw_ref, pair_ref, prior_ref, pad_ref, mask_ref,
):
    step = pl.program_id(0)

    @pl.when(step == 0)
    def _():
        make_masks(mask_ref)

    length = k_ref.shape[0]
    blocks = length // BLK
    turned_g = pltpu.roll(g_ref[...], BLK - KEY_HEADS * step, 1)
    lowers, rights, tails, lasts = [], [], [], []
    for head in range(KEY_HEADS):
        lanes = slice(head * BLK, (head + 1) * BLK)
        fill_padded(pad_ref, 2 * head, k_ref, halo_ref[1, :, lanes], lanes)
        fill_padded(pad_ref, 2 * head + 1, v_ref, halo_ref[2, :, lanes], lanes)
        for block in range(blocks):
            start = block * BLK
            tokens = slice(start, start + BLK)
            keys = unit(conv_rows(pad_ref, 2 * head, taps_ref[1, :, lanes], start, BLK)).astype(BF)
            values = conv_rows(pad_ref, 2 * head + 1, taps_ref[2, :, lanes], start, BLK).astype(BF)
            keys_f = keys.astype(F32)
            turned = keys_f.T
            turned_b = turned.astype(BF)
            kt_ref[head, :, tokens] = turned_b
            g_col = jnp.broadcast_to(turned_g[tokens, head : head + 1], (BLK, BLK))
            g_row = rows_ref[head, 0:1, tokens]
            beta_row = rows_ref[head, 1:2, tokens]
            g_last = g_row[:, BLK - 1 : BLK]
            lowers.append(decay_matrix(g_col, g_row, beta_row) * dot(keys, turned_b))
            rights.append(
                jnp.concatenate([values, (jnp.exp(g_col) * keys_f).astype(BF)], axis=1)
            )
            tails.append((turned * (jnp.exp(g_last - g_row) * beta_row)).astype(BF))
            lasts.append(jnp.exp(g_last))
    solved = inverses(lowers, mask_ref)
    maps = []
    for head in range(KEY_HEADS):
        for block in range(blocks):
            i = head * blocks + block
            fresh = dot(solved[i].astype(BF), rights[i]).astype(BF)
            uw_ref[head, block * BLK : (block + 1) * BLK, :] = fresh
            maps.append(dot(tails[i], fresh))
    eye = jnp.where(iota2((BLK, BLK), 0) == iota2((BLK, BLK), 1), 1.0, 0.0).astype(F32)
    for head in range(KEY_HEADS):
        i = head * blocks
        state_a = lasts[i] * eye - maps[i][:, BLK:]
        state_b = maps[i][:, :BLK]
        for block in range(1, blocks):
            i = head * blocks + block
            state = jnp.concatenate([state_a, state_b], axis=1)
            low = state.astype(BF)
            prior_ref[head, block - 1] = low
            state = lasts[i] * state - dot(maps[i][:, BLK:].astype(BF), low)
            state_a = state[:, :BLK]
            state_b = state[:, BLK:] + maps[i][:, :BLK]
        state = jnp.concatenate([state_a, state_b], axis=1)
        pair_ref[head] = state.astype(BF)


def query_side(
    odd_ref, rows_ref, g_ref, weight_ref, taps_ref, halo_ref, q_ref, kt_ref, uw_ref, prior_ref,
    near_ref, *rest, first_step,
):
    scaled_ref, base_ref, pad_ref = rest[-3:]
    step = pl.program_id(0) + first_step
    length = q_ref.shape[0]
    blocks = length // BLK
    levels = scaled_ref.shape[1] // (QUERY_HEADS * BLK) + 1
    per_head = levels + 1
    width = weight_ref.shape[1]
    odd = odd_ref[0].astype(F32)
    turned_g = pltpu.roll(g_ref[...], BLK - QUERY_HEADS * step, 1)
    turned_w = pltpu.roll(weight_ref[...], width - QUERY_HEADS * per_head * step, 1)
    for head in range(QUERY_HEADS):
        lanes = slice(head * BLK, (head + 1) * BLK)
        fill_padded(pad_ref, head, q_ref, halo_ref[0, :, lanes], lanes)
        near = near_ref[head] * odd.astype(BF)
        first = head * per_head
        for block in range(blocks):
            start = block * BLK
            tokens = slice(start, start + BLK)
            queries = unit(conv_rows(pad_ref, head, taps_ref[0, :, lanes], start, BLK)).astype(BF)
            g_col = jnp.broadcast_to(turned_g[tokens, head : head + 1], (BLK, BLK))
            g_row = rows_ref[head, 0:1, tokens]
            beta_row = rows_ref[head, 1:2, tokens]
            mixing = (
                decay_matrix(g_col, g_row, beta_row) * dot(queries, kt_ref[head, :, tokens])
            ).astype(BF)
            inner = dot(mixing, uw_ref[head, tokens, :])
            through = jnp.exp(g_col) * queries.astype(F32) - inner[:, BLK:]
            if block == 0:
                carried, local = through, inner[:, :BLK]
            else:
                passed = dot(through.astype(BF), prior_ref[head, block - 1])
                carried, local = passed[:, :BLK], inner[:, :BLK] + passed[:, BLK:]
            scaled = [
                (carried * turned_w[tokens, first + level : first + level + 1]).astype(BF)
                for level in range(1, per_head)
            ]
            base_ref[tokens, lanes] = turned_w[tokens, first : first + 1] * local + dot(
                scaled[0], near
            )
            begin = head * (levels - 1) * BLK
            scaled_ref[tokens, begin : begin + (levels - 1) * BLK] = jnp.concatenate(
                scaled[1:], axis=1
            )


def finish_side(
    core_ref, gain_ref, z_ref, base_ref, scaled_ref, near_ref, own_ref, far_ref, out_ref,
    other_ref, sem,
):
    step = pl.program_id(0)
    core = core_ref[0]
    length = z_ref.shape[0]
    blocks = length // BLK
    levels = own_ref.shape[2] // BLK
    fold = pl.num_programs(0) // 2
    mine = step // fold == core
    begin_head = step % fold * FINISH_HEADS

    @pl.when(step == 0)
    def _():
        fetch([(far_ref, other_ref)], sem)

    eye = jnp.where(iota2((BLK, BLK), 0) == iota2((BLK, BLK), 1), 1.0, 0.0).astype(BF)
    for head in range(FINISH_HEADS):
        lanes = slice(head * BLK, (head + 1) * BLK)
        reach = jnp.where(core == 1, near_ref[head], eye)
        seen = dot(reach, jnp.where(mine, own_ref[head], other_ref[begin_head + head])).astype(BF)
        states = jnp.concatenate(
            [seen[:, level * BLK : (level + 1) * BLK] for level in range(levels)], axis=0
        )
        begin = head * levels * BLK
        for block in range(blocks):
            tokens = slice(block * BLK, (block + 1) * BLK)
            opened = base_ref[tokens, lanes] + dot(
                scaled_ref[tokens, begin : begin + levels * BLK], states
            )
            square = jnp.sum(opened * opened, axis=-1, keepdims=True) * (1.0 / BLK)
            normed = opened * lax.rsqrt(square + EPS) * gain_ref[...]
            gate = z_ref[tokens, lanes].astype(F32)
            out_ref[tokens, lanes] = (normed * silu(gate)).astype(BF)


def merged(left, right_a, right_b):
    moved = dot(right_a.astype(BF), left.astype(BF))
    return jnp.concatenate([moved[:, :BLK], moved[:, BLK:] + right_b.astype(F32)], axis=1)


def fetch(pairs, sem):
    copies = [
        pltpu.make_async_copy(source, target, sem.at[i])
        for i, (source, target) in enumerate(pairs)
    ]
    for copy in copies:
        copy.start()
    for copy in copies:
        copy.wait()


def join_near(core_ref, pair_ref, far_ref, next_ref, own, far, sem):
    core = core_ref[0]
    half = pl.ds(core * own.shape[0], own.shape[0])
    fetch([(pair_ref.at[half], own), (far_ref.at[half], far)], sem)

    @pl.when(core == 1)
    def _():
        for head in range(own.shape[0]):
            next_ref[head] = merged(far[head], own[head, :, :BLK], own[head, :, BLK:]).astype(BF)

    @pl.when(core == 0)
    def _():
        for head in range(own.shape[0]):
            next_ref[head] = merged(own[head], far[head, :, :BLK], far[head, :, BLK:]).astype(BF)


def join_far(upper_ref, pair_ref, far_ref, *rest):
    next_ref, state_ref, onward_ref, own, far, sem = rest[-6:]
    reach_ref = rest[0] if len(rest) == 7 else None
    lanes = slice(2 * BLK - next_ref.shape[2], 2 * BLK)
    fetch([(pair_ref, own), (far_ref, far)], sem)

    @pl.when(upper_ref[0] == 1)
    def _():
        for head in range(own.shape[0]):
            seen = far[head] if reach_ref is None else dot(reach_ref[head], far[head]).astype(BF)
            onward_ref[head] = seen[:, :BLK]
            state_ref[head] = seen[:, BLK:]
            joined = merged(far[head], own[head, :, :BLK], own[head, :, BLK:]).astype(BF)
            next_ref[head] = joined[:, lanes]

    @pl.when(upper_ref[0] == 0)
    def _():
        row, col = iota2((BLK, BLK), 0), iota2((BLK, BLK), 1)
        for head in range(own.shape[0]):
            joined = merged(own[head], far[head, :, :BLK], far[head, :, BLK:]).astype(BF)
            next_ref[head] = joined[:, lanes]
            state_ref[head] = jnp.zeros((BLK, BLK), BF)
            if reach_ref is None:
                onward_ref[head] = jnp.where(row == col, 1.0, 0.0).astype(BF)
            else:
                onward_ref[head] = reach_ref[head]


def join_top(upper_ref, far_ref, reach_ref, *rest):
    state_refs, (out_ref, far, sem) = rest[:-3], rest[-3:]
    levels = len(state_refs)
    fetch([(far_ref, far)], sem)
    for level in range(levels):
        for head in range(far.shape[0]):
            out_ref[head, :, level * BLK : (level + 1) * BLK] = state_refs[level][head]

    @pl.when(upper_ref[0] == 1)
    def _():
        for head in range(far.shape[0]):
            out_ref[head, :, levels * BLK :] = dot(reach_ref[head], far[head]).astype(BF)

    @pl.when(upper_ref[0] == 0)
    def _():
        for head in range(far.shape[0]):
            out_ref[head, :, levels * BLK :] = jnp.zeros((BLK, BLK), BF)


def shape_of(shape, dtype):
    return jax.ShapeDtypeStruct(shape, dtype)


def in_vmem(*arrays):
    return [pltpu.with_memory_space_constraint(x, pltpu.VMEM) for x in arrays]


def in_hbm(*arrays):
    return [pltpu.with_memory_space_constraint(x, pltpu.HBM) for x in arrays]


def whole(shape):
    return pl.BlockSpec(shape, lambda i: (0,) * len(shape))


def by_head(count, shape, first=0, lane=0):
    tail = (0,) * (len(shape) - 1) + (lane,)
    return pl.BlockSpec((count,) + shape, lambda i: (i + first,) + tail)


def by_column(shape, first=0):
    lead = len(shape) - 1
    return pl.BlockSpec(shape, lambda i: (0,) * lead + (i + first,))


ANY = pl.BlockSpec(memory_space=pl.ANY)
SMEM = pl.BlockSpec(memory_space=pltpu.SMEM)
VMEM = pl.BlockSpec(memory_space=pltpu.VMEM)
COST = pl.CostEstimate(flops=10**10, bytes_accessed=2 * 10**7, transcendentals=10**7)
PARAMS = pltpu.CompilerParams(dimension_semantics=("arbitrary",), vmem_limit_bytes=22 << 20)

SMALL = pltpu.CompilerParams(vmem_limit_bytes=8 << 20)


def bit(position, level):
    return (position // 2**level % 2).astype(jnp.int32).reshape(1)


def keys_of(rows, g_pad, conv_weight, halo, k_in, v_in):
    heads, _, length = rows.shape
    blocks = length // BLK
    width = KEY_HEADS * BLK
    return pl.pallas_call(
        key_side,
        grid=(heads // KEY_HEADS,),
        in_specs=[
            by_head(KEY_HEADS, (2, length)), whole(g_pad.shape), by_column((3, 4, width)),
            by_column((3, 4, width)), by_column((length, width)), by_column((length, width)),
        ],
        out_specs=[
            by_head(KEY_HEADS, (BLK, length)), by_head(KEY_HEADS, (length, 2 * BLK)),
            by_head(KEY_HEADS, (BLK, 2 * BLK)), by_head(KEY_HEADS, (blocks - 1, BLK, 2 * BLK)),
        ],
        out_shape=[
            pltpu.VMEM((heads, BLK, length), BF), pltpu.VMEM((heads, length, 2 * BLK), BF),
            pltpu.VMEM((heads, BLK, 2 * BLK), BF),
            pltpu.VMEM((heads, blocks - 1, BLK, 2 * BLK), BF),
        ],
        scratch_shapes=[
            pltpu.VMEM((2 * KEY_HEADS, length + 8, BLK), F32),
            pltpu.VMEM((6, BLK, BLK), BF),
        ],
        compiler_params=PARAMS,
        cost_estimate=COST,
        name="key_side",
    )(rows, g_pad, conv_weight, halo, *in_hbm(k_in, v_in))


def queries_of(second, levels, core, rows, g_pad, weights, taps, halo, q_in, kt, uw, prior, near, previous):
    heads, _, length = rows.shape
    blocks = length // BLK
    steps = heads // QUERY_HEADS // 2
    first = steps if second else 0
    width = QUERY_HEADS * BLK
    scaled_width = width * (levels - 1)
    count = len(previous)
    return pl.pallas_call(
        functools.partial(query_side, first_step=first),
        grid=(steps,),
        in_specs=[
            SMEM, by_head(QUERY_HEADS, (2, length), first), whole(g_pad.shape),
            whole(weights.shape), by_column((3, 4, width), first), by_column((3, 4, width), first),
            by_column((length, width), first), by_head(QUERY_HEADS, (BLK, length), first),
            by_head(QUERY_HEADS, (length, 2 * BLK), first),
            by_head(QUERY_HEADS, (blocks - 1, BLK, 2 * BLK), first),
            by_head(QUERY_HEADS, (BLK, BLK), first, 1),
        ]
        + [ANY] * count,
        out_specs=[by_column((length, scaled_width), first), by_column((length, width), first)],
        out_shape=[
            pltpu.VMEM((length, heads * (levels - 1) * BLK), BF), pltpu.VMEM(q_in.shape, F32)
        ],
        scratch_shapes=[pltpu.VMEM((QUERY_HEADS, length + 8, BLK), F32)],
        input_output_aliases={11 + i: i for i in range(count)},
        compiler_params=PARAMS,
        cost_estimate=COST,
        name="query_side",
    )(
        core, rows, g_pad, weights, taps, halo, *in_hbm(q_in), *in_vmem(kt, uw, prior, near),
        *in_vmem(*previous),
    )


def finished(core, gain, z_in, base, scaled, near, own, other):
    length = z_in.shape[0]
    heads, levels = near.shape[0], own.shape[2] // BLK
    width = FINISH_HEADS * BLK
    fold = heads // FINISH_HEADS // 2
    return pl.pallas_call(
        finish_side,
        grid=(2 * fold,),
        in_specs=[
            SMEM, whole(gain.shape), by_column((length, width)), by_column((length, width)),
            by_column((length, width * levels)), by_head(FINISH_HEADS, (BLK, BLK)),
            pl.BlockSpec((FINISH_HEADS, BLK, levels * BLK), lambda i: (i % fold, 0, 0)), ANY,
        ],
        out_specs=by_column((length, width)),
        out_shape=shape_of(z_in.shape, BF),
        scratch_shapes=[pltpu.VMEM(other.shape, BF), pltpu.SemaphoreType.DMA((1,))],
        compiler_params=PARAMS,
        name="finish_side",
    )(core, gain, *in_hbm(z_in), *in_vmem(base, scaled, near, own, other))


def joined_near(core, pair, near):
    shape = (pair.shape[0] // 2,) + pair.shape[1:]
    return pl.pallas_call(
        join_near,
        in_specs=[SMEM, ANY, ANY],
        out_specs=VMEM,
        out_shape=shape_of(shape, BF),
        scratch_shapes=[
            pltpu.VMEM(shape, BF), pltpu.VMEM(shape, BF), pltpu.SemaphoreType.DMA((2,)),
        ],
        compiler_params=SMALL,
        name="join_near",
    )(core, pair, near)


def joined_far(upper, pair, far, reach, last):
    square = (pair.shape[0], BLK, BLK)
    given = () if reach is None else (reach,)
    return pl.pallas_call(
        join_far,
        in_specs=[SMEM, ANY, ANY] + [VMEM] * len(given),
        out_specs=[VMEM] * 3,
        out_shape=[shape_of(square if last else pair.shape, BF)] + [shape_of(square, BF)] * 2,
        scratch_shapes=[
            pltpu.VMEM(pair.shape, BF), pltpu.VMEM(pair.shape, BF), pltpu.SemaphoreType.DMA((2,)),
        ],
        compiler_params=SMALL,
        name="join_far",
    )(upper, pair, far, *given)


def joined_top(upper, far, reach, states):
    shape = (far.shape[0], BLK, (len(states) + 1) * BLK)
    return pl.pallas_call(
        join_top,
        in_specs=[SMEM, ANY] + [VMEM] * (1 + len(states)),
        out_specs=VMEM,
        out_shape=shape_of(shape, BF),
        scratch_shapes=[pltpu.VMEM(far.shape, BF), pltpu.SemaphoreType.DMA((1,))],
        compiler_params=SMALL,
        name="join_top",
    )(upper, far, reach, *states)


def per_device(q_in, k_in, v_in, z_in, log_gate, beta, level_weight, conv_weight, norm_gain):
    length, heads = log_gate.shape
    blocks = length // BLK
    ctx = lax.axis_size("ctx")
    levels = ctx.bit_length() - 1
    position = lax.axis_index("ctx")
    edge = jnp.stack([x[length - 4 :] for x in (q_in, k_in, v_in)], axis=0)
    halo = lax.ppermute(edge, "ctx", [(i, i + 1) for i in range(ctx - 1)])

    g = jnp.cumsum(log_gate.reshape(blocks, BLK, heads), axis=1).reshape(length, heads)
    g_pad = jnp.pad(g, ((0, 0), (0, BLK - heads)))
    rows = jnp.stack([g.T, beta.T], axis=1)
    weights = level_weight[:, :, : levels + 1].reshape(length, heads * (levels + 1))
    weights = jnp.pad(weights, ((0, 0), (0, -weights.shape[1] % BLK)))
    bits = [bit(position, level) for level in range(levels)]
    halo, rows, g_pad, weights, *bits = lax.optimization_barrier(
        (halo, rows, g_pad, weights, *bits)
    )
    core = bits[0]

    kt, uw, pair, prior = keys_of(rows, g_pad, conv_weight, halo, k_in, v_in)
    near = lax.ppermute(pair, "ctx", [(i, i ^ 1) for i in range(ctx)])
    pair = joined_near(core, pair, near)

    def queries(second, q_in, previous):
        return queries_of(
            second, levels, core, rows, g_pad, weights, conv_weight, halo, q_in, kt, uw, prior,
            near, previous,
        )

    reach, states, parts = None, [], ()
    for level in range(1, levels - 1):
        far = lax.ppermute(pair, "ctx", [(i, i ^ 2**level) for i in range(ctx)])
        if level == 1:
            parts = queries(False, q_in, ())
            far, *parts = lax.optimization_barrier((far, *parts))
        pair, state, reach = joined_far(bits[level], pair, far, reach, level == levels - 2)
        states.append(state)
    top = levels - 1
    pair, later_q = lax.optimization_barrier((pair, q_in))
    far = lax.ppermute(pair, "ctx", [(i, i + 2**top) for i in range(ctx - 2**top)])
    parts = queries(True, later_q, parts)
    far, scaled, base = lax.optimization_barrier((far, *parts))
    own = joined_top(bits[top], far, reach, states)
    other = lax.ppermute(own, "ctx", [(i, i ^ 1) for i in range(ctx)])
    return finished(core, norm_gain.reshape(1, BLK), z_in, base, scaled, near, own, other)


def solution(mesh):
    placed = (
        P(("batch", "ctx"), None),
        P(("batch", "ctx"), None),
        P(("batch", "ctx"), None),
        P(("batch", "ctx"), None),
        P(("batch", "ctx"), None),
        P(("batch", "ctx"), None),
        P(("batch", "ctx"), None, None),
        P(),
        P(),
    )
    return jax.shard_map(
        per_device, mesh=mesh, in_specs=placed, out_specs=P(("batch", "ctx"), None), check_vma=False
    )
```

```python
import functools

import jax
import jax.numpy as jnp
from jax import lax
from jax.experimental import pallas as pl
from jax.experimental.pallas import tpu as pltpu
from jax.sharding import PartitionSpec as P

BLK = 128
SUB = 16
KEY_HEADS = 4
QUERY_HEADS = 2
FINISH_HEADS = 4
EPS = 1e-06
LOG2_E = 1.4426950408889634
BF = jnp.bfloat16
F32 = jnp.float32


def dot(first, second):
    return lax.dot_general(
        first, second, (((1,), (0,)), ((), ())), preferred_element_type=F32
    )


def silu(value):
    return value * pl.reciprocal(1.0 + jnp.exp(-value), approx=False)


def fill_padded(pad_ref, slot, x_ref, halo, lanes):
    pad_ref[slot, 4:8, :] = halo.astype(F32)
    pad_ref[slot, 8:, :] = x_ref[:, lanes].astype(F32)


def conv_rows(pad_ref, slot, taps, start, count):
    total = taps[0:1] * pad_ref[slot, start + 5 : start + 5 + count, :]
    for tap in range(1, 4):
        total = total + taps[tap : tap + 1] * pad_ref[
            slot, start + 5 + tap : start + 5 + tap + count, :
        ]
    return silu(total)


def unit(rows):
    return rows * lax.rsqrt(jnp.sum(rows * rows, axis=-1, keepdims=True) + EPS)


def iota2(shape, dim):
    return lax.broadcasted_iota(jnp.int32, shape, dim)


def decay_matrix(g_col, g_row, beta_row):
    size = g_col.shape[0]
    causal = iota2((size, BLK), 1) <= iota2((size, BLK), 0)
    return jnp.exp2(jnp.where(causal, g_col - g_row, -1e30)) * beta_row


def make_masks(mask_ref):
    row, col = iota2((BLK, BLK), 0), iota2((BLK, BLK), 1)
    size, index = SUB, 0
    while size < BLK:
        same = row // size == col // size
        pair = row // (2 * size) == col // (2 * size)
        high_low = pair & (row // size % 2 == 1) & (col // size % 2 == 0)
        mask_ref[index] = jnp.where(same, 1.0, 0.0).astype(BF)
        mask_ref[index + 1] = jnp.where(high_low, 1.0, 0.0).astype(BF)
        size, index = size * 2, index + 2


def tiled(packed, times, mask):
    return jnp.concatenate([packed.astype(BF)] * times, axis=0) * mask


def picked(lower, size, offset):
    groups = BLK // size if offset is None else BLK // (2 * size)
    step = size if offset is None else 2 * size
    first = 0 if offset is None else offset
    lane = iota2((size, BLK), 1) // step
    out = lower[first : first + size]
    for group in range(1, groups):
        begin = first + group * step
        out = jnp.where(lane == group, lower[begin : begin + size], out)
    return out


def inverses(lowers, mask_ref, results):
    every = range(len(lowers))
    row, col = iota2((SUB, BLK), 0), iota2((SUB, BLK), 1) % SUB
    eye = jnp.where(row == col, 1.0, 0.0).astype(F32)
    strict = col < row
    same = mask_ref[0]
    times = BLK // SUB
    powers = [jnp.where(strict, -picked(lower, SUB, None), 0.0) for lower in lowers]
    results[:] = [eye + power for power in powers]
    powers = [dot(p.astype(BF), tiled(p, times, same)) for p in powers]
    yield
    reach = 2
    while reach < SUB // 2:
        both = [
            dot(
                jnp.concatenate([powers[i].astype(BF), results[i].astype(BF)], axis=0),
                tiled(powers[i], times, same),
            )
            for i in every
        ]
        yield
        powers = [x[:SUB] for x in both]
        results[:] = [results[i] + both[i][SUB:] for i in every]
        reach *= 2
    results[:] = [
        results[i] + dot(results[i].astype(BF), tiled(powers[i], times, same)) for i in every
    ]
    yield
    size, index = SUB, 0
    while size < BLK:
        times = BLK // size
        low = iota2((size, BLK), 1) // size % 2 == 0
        cross = [picked(lower, size, size).astype(BF) for lower in lowers]
        moved = [dot(cross[i], tiled(results[i], times, mask_ref[index])) for i in every]
        yield
        turned = [
            dot(results[i].astype(BF), tiled(moved[i], times, mask_ref[index + 1]))
            for i in every
        ]
        yield
        results[:] = [
            jnp.concatenate(
                [jnp.where(low, results[i], 0.0), jnp.where(low, -turned[i], results[i])], axis=0
            )
            for i in every
        ]
        size, index = size * 2, index + 2


def chained(first, second):
    yield from first
    yield from second


def together(first, second):
    live = [first, second]
    while live:
        for stages in list(live):
            if next(stages, live) is live:
                live.remove(stages)


def key_side(
    rows_ref, g_ref, taps_ref, halo_ref, k_ref, v_ref,
    kt_ref, uw_ref, pair_ref, prior_ref, pad_ref, mask_ref,
):
    step = pl.program_id(0)

    @pl.when(step == 0)
    def _():
        make_masks(mask_ref)

    length = k_ref.shape[0]
    blocks = length // BLK
    base = KEY_HEADS * step
    turned_g = pltpu.roll(g_ref[...], BLK - KEY_HEADS * step, 1)
    eye = jnp.where(iota2((BLK, BLK), 0) == iota2((BLK, BLK), 1), 1.0, 0.0).astype(F32)

    def front(heads, lowers, others):
        for head in heads:
            lanes = slice(head * BLK, (head + 1) * BLK)
            fill_padded(pad_ref, 2 * head, k_ref, halo_ref[1, :, lanes], lanes)
            fill_padded(pad_ref, 2 * head + 1, v_ref, halo_ref[2, :, lanes], lanes)
            for block in range(blocks):
                start = block * BLK
                tokens = slice(start, start + BLK)
                keys = unit(conv_rows(pad_ref, 2 * head, taps_ref[1, :, lanes], start, BLK))
                keys = keys.astype(BF)
                values = conv_rows(pad_ref, 2 * head + 1, taps_ref[2, :, lanes], start, BLK)
                keys_f = keys.astype(F32)
                turned = keys_f.T
                turned_b = turned.astype(BF)
                kt_ref[base + head, :, tokens] = turned_b
                g_col = jnp.broadcast_to(turned_g[tokens, head : head + 1], (BLK, BLK))
                g_row = rows_ref[head, 0:1, tokens]
                beta_row = rows_ref[head, 1:2, tokens]
                g_last = g_row[:, BLK - 1 : BLK]
                lowers.append(decay_matrix(g_col, g_row, beta_row) * dot(keys, turned_b))
                right = jnp.concatenate(
                    [values.astype(BF), (jnp.exp2(g_col) * keys_f).astype(BF)], axis=1
                )
                tail = (turned * (jnp.exp2(g_last - g_row) * beta_row)).astype(BF)
                others.append((right, tail, jnp.exp2(g_last)))
                yield

    def back(heads, solved, others):
        maps = []
        for place, head in enumerate(heads):
            for block in range(blocks):
                i = place * blocks + block
                fresh = dot(solved[i].astype(BF), others[i][0]).astype(BF)
                uw_ref[base + head, block * BLK : (block + 1) * BLK, :] = fresh
                maps.append(fresh)
            yield
        for place, head in enumerate(heads):
            for block in range(blocks):
                i = place * blocks + block
                maps[i] = dot(others[i][1], maps[i])
            yield
        states = []
        for place, head in enumerate(heads):
            i = place * blocks
            states.append(
                jnp.concatenate(
                    [others[i][2] * eye - maps[i][:, BLK:], maps[i][:, :BLK]], axis=1
                )
            )
        for block in range(1, blocks):
            for place, head in enumerate(heads):
                i = place * blocks + block
                low = states[place].astype(BF)
                prior_ref[base + head, block - 1] = low
                state = others[i][2] * states[place] - dot(maps[i][:, BLK:].astype(BF), low)
                states[place] = jnp.concatenate(
                    [state[:, :BLK], state[:, BLK:] + maps[i][:, :BLK]], axis=1
                )
            yield
        for place, head in enumerate(heads):
            pair_ref[base + head] = states[place].astype(BF)

    groups = [range(i, i + 2) for i in range(0, KEY_HEADS, 2)]
    lowers, others, solved = [], [], []
    for _ in front(groups[0], lowers, others):
        pass
    ending = iter(())
    for place in range(len(groups)):
        solved = []
        later, later_others = [], []
        if place + 1 < len(groups):
            beside = front(groups[place + 1], later, later_others)
        else:
            beside = iter(())

        together(inverses(lowers, mask_ref, solved), chained(ending, beside))
        ending = back(groups[place], solved, others)
        lowers, others = later, later_others
    for _ in ending:
        pass


def query_side(
    odd_ref, rows_ref, g_ref, weight_ref, taps_ref, halo_ref, q_ref, kt_ref, uw_ref, prior_ref,
    near_ref, scaled_ref, base_ref, pad_ref, *, first_step,
):
    local_step = pl.program_id(0)
    step = local_step + first_step
    length = q_ref.shape[0]
    blocks = length // BLK
    levels = scaled_ref.shape[2] // BLK + 1
    per_head = levels + 1
    width = weight_ref.shape[1]
    odd = odd_ref[0].astype(F32)
    turned_g = pltpu.roll(g_ref[...], BLK - QUERY_HEADS * step, 1)
    turned_w = pltpu.roll(weight_ref[...], width - QUERY_HEADS * per_head * step, 1)
    for head in range(QUERY_HEADS):
        lanes = slice(head * BLK, (head + 1) * BLK)
        fill_padded(pad_ref, head, q_ref, halo_ref[0, :, lanes], lanes)
        where = QUERY_HEADS * step + head
        out = QUERY_HEADS * local_step + head
        near = near_ref[where, :, BLK:] * odd.astype(BF)
        first = head * per_head
        for block in range(blocks):
            start = block * BLK
            tokens = slice(start, start + BLK)
            queries = unit(conv_rows(pad_ref, head, taps_ref[0, :, lanes], start, BLK)).astype(BF)
            g_col = jnp.broadcast_to(turned_g[tokens, head : head + 1], (BLK, BLK))
            g_row = rows_ref[head, 0:1, tokens]
            beta_row = rows_ref[head, 1:2, tokens]
            mixing = (
                decay_matrix(g_col, g_row, beta_row) * dot(queries, kt_ref[where, :, tokens])
            ).astype(BF)
            inner = dot(mixing, uw_ref[where, tokens, :])
            through = jnp.exp2(g_col) * queries.astype(F32) - inner[:, BLK:]
            if block == 0:
                carried, local = through, inner[:, :BLK]
            else:
                passed = dot(through.astype(BF), prior_ref[where, block - 1])
                carried, local = passed[:, :BLK], inner[:, :BLK] + passed[:, BLK:]
            scaled = [
                (carried * turned_w[tokens, first + level : first + level + 1]).astype(BF)
                for level in range(1, per_head)
            ]
            base_ref[out, tokens, :] = turned_w[tokens, first : first + 1] * local + dot(
                scaled[0], near
            )
            scaled_ref[out, tokens, :] = jnp.concatenate(scaled[1:], axis=1)


def finish_side(
    core_ref, gain_ref, z_ref, near_ref, own_ref, other_ref, base_0, scaled_0, base_1, scaled_1,
    out_ref,
):
    step = pl.program_id(0)
    core = core_ref[0]
    length = z_ref.shape[0]
    blocks = length // BLK
    levels = own_ref.shape[2] // BLK
    fold = pl.num_programs(0) // 2
    eye = jnp.where(iota2((BLK, BLK), 0) == iota2((BLK, BLK), 1), 1.0, 0.0).astype(BF)

    def part(second, base_ref, scaled_ref):
        mine = core == second
        for head in range(FINISH_HEADS):
            lanes = slice(head * BLK, (head + 1) * BLK)
            place = step % fold * FINISH_HEADS + head
            reach = jnp.where(core == 1, near_ref[step * FINISH_HEADS + head, :, :BLK], eye)
            seen = dot(reach, jnp.where(mine, own_ref[place], other_ref[place])).astype(BF)
            states = jnp.concatenate(
                [seen[:, level * BLK : (level + 1) * BLK] for level in range(levels)], axis=0
            )
            for block in range(blocks):
                tokens = slice(block * BLK, (block + 1) * BLK)
                opened = base_ref[place, tokens, :] + dot(scaled_ref[place, tokens, :], states)
                square = jnp.sum(opened * opened, axis=-1, keepdims=True) * (1.0 / BLK)
                normed = opened * lax.rsqrt(square + EPS) * gain_ref[...]
                gate = z_ref[tokens, lanes].astype(F32)
                out_ref[tokens, lanes] = (normed * silu(gate)).astype(BF)

    @pl.when(step < fold)
    def _():
        part(0, base_0, scaled_0)

    @pl.when(step >= fold)
    def _():
        part(1, base_1, scaled_1)


def merged(left, right_a, right_b):
    moved = dot(right_a.astype(BF), left.astype(BF))
    return jnp.concatenate([moved[:, :BLK], moved[:, BLK:] + right_b.astype(F32)], axis=1)


def fetch(pairs, sem):
    copies = [
        pltpu.make_async_copy(source, target, sem.at[i])
        for i, (source, target) in enumerate(pairs)
    ]
    for copy in copies:
        copy.start()
    for copy in copies:
        copy.wait()


def join_near(core_ref, pair_ref, far_ref, next_ref, own, far, sem):
    core = core_ref[0]
    half = pl.ds(core * own.shape[0], own.shape[0])
    fetch([(pair_ref.at[half], own), (far_ref.at[half], far)], sem)

    @pl.when(core == 1)
    def _():
        for head in range(own.shape[0]):
            next_ref[head] = merged(far[head], own[head, :, :BLK], own[head, :, BLK:]).astype(BF)

    @pl.when(core == 0)
    def _():
        for head in range(own.shape[0]):
            next_ref[head] = merged(own[head], far[head, :, :BLK], far[head, :, BLK:]).astype(BF)


def join_far(upper_ref, pair_ref, far_ref, *rest):
    next_ref, state_ref, onward_ref, own, far, sem = rest[-6:]
    reach_ref = rest[0] if len(rest) == 7 else None
    lanes = slice(2 * BLK - next_ref.shape[2], 2 * BLK)
    fetch([(pair_ref, own), (far_ref, far)], sem)

    @pl.when(upper_ref[0] == 1)
    def _():
        for head in range(own.shape[0]):
            seen = far[head] if reach_ref is None else dot(reach_ref[head], far[head]).astype(BF)
            onward_ref[head] = seen[:, :BLK]
            state_ref[head] = seen[:, BLK:]
            joined = merged(far[head], own[head, :, :BLK], own[head, :, BLK:]).astype(BF)
            next_ref[head] = joined[:, lanes]

    @pl.when(upper_ref[0] == 0)
    def _():
        row, col = iota2((BLK, BLK), 0), iota2((BLK, BLK), 1)
        for head in range(own.shape[0]):
            joined = merged(own[head], far[head, :, :BLK], far[head, :, BLK:]).astype(BF)
            next_ref[head] = joined[:, lanes]
            state_ref[head] = jnp.zeros((BLK, BLK), BF)
            if reach_ref is None:
                onward_ref[head] = jnp.where(row == col, 1.0, 0.0).astype(BF)
            else:
                onward_ref[head] = reach_ref[head]


def join_top(upper_ref, far_ref, reach_ref, *rest):
    state_refs, (out_ref, far, sem) = rest[:-3], rest[-3:]
    levels = len(state_refs)
    fetch([(far_ref, far)], sem)
    for level in range(levels):
        for head in range(far.shape[0]):
            out_ref[head, :, level * BLK : (level + 1) * BLK] = state_refs[level][head]

    @pl.when(upper_ref[0] == 1)
    def _():
        for head in range(far.shape[0]):
            out_ref[head, :, levels * BLK :] = dot(reach_ref[head], far[head]).astype(BF)

    @pl.when(upper_ref[0] == 0)
    def _():
        for head in range(far.shape[0]):
            out_ref[head, :, levels * BLK :] = jnp.zeros((BLK, BLK), BF)


def shape_of(shape, dtype):
    return jax.ShapeDtypeStruct(shape, dtype)


def in_vmem(*arrays):
    return [pltpu.with_memory_space_constraint(x, pltpu.VMEM) for x in arrays]


def in_hbm(*arrays):
    return [pltpu.with_memory_space_constraint(x, pltpu.HBM) for x in arrays]


def whole(shape):
    return pl.BlockSpec(shape, lambda i: (0,) * len(shape))


def by_head(count, shape, first=0, lane=0):
    tail = (0,) * (len(shape) - 1) + (lane,)
    return pl.BlockSpec((count,) + shape, lambda i: (i + first,) + tail)


def by_column(shape, first=0):
    lead = len(shape) - 1
    return pl.BlockSpec(shape, lambda i: (0,) * lead + (i + first,))


ANY = pl.BlockSpec(memory_space=pl.ANY)
SMEM = pl.BlockSpec(memory_space=pltpu.SMEM)
VMEM = pl.BlockSpec(memory_space=pltpu.VMEM)
COST = pl.CostEstimate(flops=10**10, bytes_accessed=2 * 10**7, transcendentals=10**7)
PARAMS = pltpu.CompilerParams(dimension_semantics=("arbitrary",), vmem_limit_bytes=22 << 20)

SMALL = pltpu.CompilerParams(vmem_limit_bytes=8 << 20)


def bit(position, level):
    return (position // 2**level % 2).astype(jnp.int32).reshape(1)


def keys_of(rows, g_pad, conv_weight, halo, k_in, v_in):
    heads, _, length = rows.shape
    blocks = length // BLK
    width = KEY_HEADS * BLK
    return pl.pallas_call(
        key_side,
        grid=(heads // KEY_HEADS,),
        in_specs=[
            by_head(KEY_HEADS, (2, length)), whole(g_pad.shape), by_column((3, 4, width)),
            by_column((3, 4, width)), by_column((length, width)), by_column((length, width)),
        ],
        out_specs=[VMEM] * 4,
        out_shape=[
            pltpu.VMEM((heads, BLK, length), BF), pltpu.VMEM((heads, length, 2 * BLK), BF),
            pltpu.VMEM((heads, BLK, 2 * BLK), BF),
            pltpu.VMEM((heads, blocks - 1, BLK, 2 * BLK), BF),
        ],
        scratch_shapes=[
            pltpu.VMEM((2 * KEY_HEADS, length + 8, BLK), F32),
            pltpu.VMEM((6, BLK, BLK), BF),
        ],
        compiler_params=PARAMS,
        cost_estimate=COST,
        name="key_side",
    )(rows, g_pad, conv_weight, halo, *in_hbm(k_in, v_in))


def queries_of(second, levels, core, rows, g_pad, weights, taps, halo, q_in, kt, uw, prior, near):
    heads, _, length = rows.shape
    steps = heads // QUERY_HEADS // 2
    first = steps if second else 0
    width = QUERY_HEADS * BLK
    return pl.pallas_call(
        functools.partial(query_side, first_step=first),
        grid=(steps,),
        in_specs=[
            SMEM, by_head(QUERY_HEADS, (2, length), first), whole(g_pad.shape),
            whole(weights.shape), by_column((3, 4, width), first), by_column((3, 4, width), first),
            by_column((length, width), first),
        ]
        + [VMEM] * 4,
        out_specs=[VMEM] * 2,
        out_shape=[
            pltpu.VMEM((heads // 2, length, (levels - 1) * BLK), BF),
            pltpu.VMEM((heads // 2, length, BLK), F32),
        ],
        scratch_shapes=[pltpu.VMEM((QUERY_HEADS, length + 8, BLK), F32)],
        compiler_params=PARAMS,
        cost_estimate=COST,
        name="query_side",
    )(core, rows, g_pad, weights, taps, halo, *in_hbm(q_in), *in_vmem(kt, uw, prior, near))


def finished(core, gain, z_in, near, own, other, base_0, scaled_0, base_1, scaled_1):
    length = z_in.shape[0]
    width = FINISH_HEADS * BLK
    return pl.pallas_call(
        finish_side,
        grid=(near.shape[0] // FINISH_HEADS,),
        in_specs=[SMEM, whole(gain.shape), by_column((length, width))] + [VMEM] * 7,
        out_specs=by_column((length, width)),
        out_shape=shape_of(z_in.shape, BF),
        compiler_params=PARAMS,
        name="finish_side",
    )(
        core, gain, *in_hbm(z_in),
        *in_vmem(near, own, other, base_0, scaled_0, base_1, scaled_1),
    )


def joined_near(core, pair, near):
    shape = (pair.shape[0] // 2,) + pair.shape[1:]
    return pl.pallas_call(
        join_near,
        in_specs=[SMEM, ANY, ANY],
        out_specs=VMEM,
        out_shape=shape_of(shape, BF),
        scratch_shapes=[
            pltpu.VMEM(shape, BF), pltpu.VMEM(shape, BF), pltpu.SemaphoreType.DMA((2,)),
        ],
        compiler_params=SMALL,
        name="join_near",
    )(core, pair, near)


def joined_far(upper, pair, far, reach, last):
    square = (pair.shape[0], BLK, BLK)
    given = () if reach is None else (reach,)
    return pl.pallas_call(
        join_far,
        in_specs=[SMEM, ANY, ANY] + [VMEM] * len(given),
        out_specs=[VMEM] * 3,
        out_shape=[shape_of(square if last else pair.shape, BF)] + [shape_of(square, BF)] * 2,
        scratch_shapes=[
            pltpu.VMEM(pair.shape, BF), pltpu.VMEM(pair.shape, BF), pltpu.SemaphoreType.DMA((2,)),
        ],
        compiler_params=SMALL,
        name="join_far",
    )(upper, pair, far, *given)


def joined_top(upper, far, reach, states):
    shape = (far.shape[0], BLK, (len(states) + 1) * BLK)
    return pl.pallas_call(
        join_top,
        in_specs=[SMEM, ANY] + [VMEM] * (1 + len(states)),
        out_specs=VMEM,
        out_shape=shape_of(shape, BF),
        scratch_shapes=[pltpu.VMEM(far.shape, BF), pltpu.SemaphoreType.DMA((1,))],
        compiler_params=SMALL,
        name="join_top",
    )(upper, far, reach, *states)


def per_device(q_in, k_in, v_in, z_in, log_gate, beta, level_weight, conv_weight, norm_gain):
    length, heads = log_gate.shape
    blocks = length // BLK
    ctx = lax.axis_size("ctx")
    levels = ctx.bit_length() - 1
    position = lax.axis_index("ctx")
    edge = jnp.stack([x[length - 4 :] for x in (q_in, k_in, v_in)], axis=0)
    halo = lax.ppermute(edge, "ctx", [(i, i + 1) for i in range(ctx - 1)])

    g = jnp.cumsum(log_gate.reshape(blocks, BLK, heads), axis=1).reshape(length, heads) * LOG2_E
    g_pad = jnp.pad(g, ((0, 0), (0, BLK - heads)))
    rows = jnp.stack([g.T, beta.T], axis=1)
    weights = level_weight[:, :, : levels + 1].reshape(length, heads * (levels + 1))
    weights = jnp.pad(weights, ((0, 0), (0, -weights.shape[1] % BLK)))
    bits = [bit(position, level) for level in range(levels)]
    halo, rows, g_pad, weights, *bits = lax.optimization_barrier(
        (halo, rows, g_pad, weights, *bits)
    )
    core = bits[0]

    kt, uw, pair, prior = keys_of(rows, g_pad, conv_weight, halo, k_in, v_in)
    near = lax.ppermute(pair, "ctx", [(i, i ^ 1) for i in range(ctx)])
    pair = joined_near(core, pair, near)

    def queries(second, q_in):
        return queries_of(
            second, levels, core, rows, g_pad, weights, conv_weight, halo, q_in, kt, uw, prior, near
        )

    reach, states = None, []
    for level in range(1, levels - 1):
        far = lax.ppermute(pair, "ctx", [(i, i ^ 2**level) for i in range(ctx)])
        if level == 1:
            far, scaled_0, base_0 = lax.optimization_barrier((far, *queries(False, q_in)))
        pair, state, reach = joined_far(bits[level], pair, far, reach, level == levels - 2)
        states.append(state)
    top = levels - 1
    pair, later_q = lax.optimization_barrier((pair, q_in))
    far = lax.ppermute(pair, "ctx", [(i, i ^ 2**top) for i in range(ctx)])
    far, scaled_1, base_1 = lax.optimization_barrier((far, *queries(True, later_q)))
    own = joined_top(bits[top], far, reach, states)
    other = lax.ppermute(own, "ctx", [(i, i ^ 1) for i in range(ctx)])
    return finished(
        core, norm_gain.reshape(1, BLK), z_in, near, own, other, base_0, scaled_0, base_1, scaled_1
    )


def solution(mesh):
    placed = (
        P(("batch", "ctx"), None),
        P(("batch", "ctx"), None),
        P(("batch", "ctx"), None),
        P(("batch", "ctx"), None),
        P(("batch", "ctx"), None),
        P(("batch", "ctx"), None),
        P(("batch", "ctx"), None, None),
        P(),
        P(),
    )
    return jax.shard_map(
        per_device, mesh=mesh, in_specs=placed, out_specs=P(("batch", "ctx"), None), check_vma=False
    )
```

```python
import functools

import jax
import jax.numpy as jnp
from jax import lax
from jax.experimental import pallas as pl
from jax.experimental.pallas import tpu as pltpu
from jax.sharding import PartitionSpec as P

BLK = 128
SUB = 16
PAIR = 4
QUERY_HEADS = 4
FINISH_HEADS = 4
EPS = 1e-06
LOG2_E = 1.4426950408889634
BF = jnp.bfloat16
F32 = jnp.float32


def dot(first, second):
    return lax.dot_general(
        first, second, (((1,), (0,)), ((), ())), preferred_element_type=F32
    )


def silu(value):
    return value * pl.reciprocal(1.0 + jnp.exp(-value), approx=False)


def fill_padded(pad_ref, slot, x_ref, halo, lanes):
    pad_ref[slot, 4:8, :] = halo.astype(F32)
    pad_ref[slot, 8:, :] = x_ref[:, lanes].astype(F32)


def conv_rows(pad_ref, slot, taps, start, count):
    total = taps[0:1] * pad_ref[slot, start + 5 : start + 5 + count, :]
    for tap in range(1, 4):
        total = total + taps[tap : tap + 1] * pad_ref[
            slot, start + 5 + tap : start + 5 + tap + count, :
        ]
    return silu(total)


def unit(rows):
    return rows * lax.rsqrt(jnp.sum(rows * rows, axis=-1, keepdims=True) + EPS)


def iota2(shape, dim):
    return lax.broadcasted_iota(jnp.int32, shape, dim)


def decay_matrix(g_col, g_row, beta_row):
    size = g_col.shape[0]
    causal = iota2((size, BLK), 1) <= iota2((size, BLK), 0)
    return jnp.exp2(jnp.where(causal, g_col - g_row, -1e30)) * beta_row


def make_masks(mask_ref):
    row, col = iota2((BLK, BLK), 0), iota2((BLK, BLK), 1)
    size, index = SUB, 0
    while size < BLK:
        same = row // size == col // size
        pair = row // (2 * size) == col // (2 * size)
        high_low = pair & (row // size % 2 == 1) & (col // size % 2 == 0)
        mask_ref[index] = jnp.where(same, 1.0, 0.0).astype(BF)
        mask_ref[index + 1] = jnp.where(high_low, 1.0, 0.0).astype(BF)
        size, index = size * 2, index + 2


def tiled(packed, times, mask):
    return jnp.concatenate([packed.astype(BF)] * times, axis=0) * mask


def picked(lower, size, offset):
    groups = BLK // size if offset is None else BLK // (2 * size)
    step = size if offset is None else 2 * size
    first = 0 if offset is None else offset
    lane = iota2((size, BLK), 1) // step
    out = lower[first : first + size]
    for group in range(1, groups):
        begin = first + group * step
        out = jnp.where(lane == group, lower[begin : begin + size], out)
    return out


def inverses(lowers, mask_ref, results):
    every = range(len(lowers))
    row, col = iota2((SUB, BLK), 0), iota2((SUB, BLK), 1) % SUB
    eye = jnp.where(row == col, 1.0, 0.0).astype(F32)
    strict = col < row
    same = mask_ref[0]
    times = BLK // SUB
    powers = [jnp.where(strict, -picked(lower, SUB, None), 0.0) for lower in lowers]
    results[:] = [eye + power for power in powers]
    powers = [dot(p.astype(BF), tiled(p, times, same)) for p in powers]
    yield
    reach = 2
    while reach < SUB // 2:
        both = [
            dot(
                jnp.concatenate([powers[i].astype(BF), results[i].astype(BF)], axis=0),
                tiled(powers[i], times, same),
            )
            for i in every
        ]
        yield
        powers = [x[:SUB] for x in both]
        results[:] = [results[i] + both[i][SUB:] for i in every]
        reach *= 2
    results[:] = [
        results[i] + dot(results[i].astype(BF), tiled(powers[i], times, same)) for i in every
    ]
    yield
    size, index = SUB, 0
    while size < BLK:
        times = BLK // size
        low = iota2((size, BLK), 1) // size % 2 == 0
        cross = [picked(lower, size, size).astype(BF) for lower in lowers]
        moved = [dot(cross[i], tiled(results[i], times, mask_ref[index])) for i in every]
        yield
        turned = [
            dot(results[i].astype(BF), tiled(moved[i], times, mask_ref[index + 1]))
            for i in every
        ]
        yield
        results[:] = [
            jnp.concatenate(
                [jnp.where(low, results[i], 0.0), jnp.where(low, -turned[i], results[i])], axis=0
            )
            for i in every
        ]
        size, index = size * 2, index + 2


def together(first, second):
    live = [first, second]
    while live:
        for stages in list(live):
            if next(stages, live) is live:
                live.remove(stages)


def key_side(
    rows_ref, g_ref, taps_ref, halo_ref, k_first, v_first, k_next, v_next,
    kt_ref, uw_ref, pair_ref, prior_ref, pad_ref, low_ref, right_ref, tail_ref, mask_ref,
):
    step = pl.program_id(0)
    length = k_first.shape[0]
    blocks = length // BLK
    last = kt_ref.shape[0] // PAIR - 1
    eye = jnp.where(iota2((BLK, BLK), 0) == iota2((BLK, BLK), 1), 1.0, 0.0).astype(F32)

    def front(pair, k_ref, v_ref, slot):
        turned_g = pltpu.roll(g_ref[...], BLK - PAIR * pair, 1)
        for place in range(PAIR):
            head = PAIR * pair + place
            lanes = slice(place * BLK, (place + 1) * BLK)
            columns = pl.ds(pl.multiple_of(head * BLK, BLK), BLK)
            pad = 2 * (PAIR * slot + place)
            fill_padded(pad_ref, pad, k_ref, halo_ref[1, :, columns], lanes)
            fill_padded(pad_ref, pad + 1, v_ref, halo_ref[2, :, columns], lanes)
            key_taps, value_taps = taps_ref[1, :, columns], taps_ref[2, :, columns]
            for block in range(blocks):
                i = place * blocks + block
                start = block * BLK
                tokens = slice(start, start + BLK)
                keys = unit(conv_rows(pad_ref, pad, key_taps, start, BLK)).astype(BF)
                values = conv_rows(pad_ref, pad + 1, value_taps, start, BLK)
                keys_f = keys.astype(F32)
                turned = keys_f.T
                turned_b = turned.astype(BF)
                kt_ref[head, :, tokens] = turned_b
                right_ref[slot, i, :, :BLK] = values.astype(BF)
                yield
                g_col = jnp.broadcast_to(turned_g[tokens, place : place + 1], (BLK, BLK))
                g_row = rows_ref[head, 0:1, tokens]
                beta_row = rows_ref[head, 1:2, tokens]
                g_last = g_row[:, BLK - 1 : BLK]
                low_ref[slot, i] = decay_matrix(g_col, g_row, beta_row) * dot(keys, turned_b)
                right_ref[slot, i, :, BLK:] = (jnp.exp2(g_col) * keys_f).astype(BF)
                tail_ref[slot, i] = (turned * (jnp.exp2(g_last - g_row) * beta_row)).astype(BF)
                yield

    def back(pair, slot):
        solved = []
        yield from inverses(
            [low_ref.at[slot, i] for i in range(PAIR * blocks)], mask_ref, solved
        )
        maps = []
        for i in range(PAIR * blocks):
            fresh = dot(solved[i].astype(BF), right_ref[slot, i]).astype(BF)
            tokens = slice(i % blocks * BLK, (i % blocks + 1) * BLK)
            uw_ref[PAIR * pair + i // blocks, tokens, :] = fresh
            maps.append(fresh)
        yield
        maps = [dot(tail_ref[slot, i], maps[i]) for i in range(PAIR * blocks)]
        yield
        states, falls = [], []
        for i in range(PAIR * blocks):
            end = (i % blocks + 1) * BLK
            falls.append(
                jnp.exp2(rows_ref[PAIR * pair + i // blocks, 0:1, end - 1 : end])
            )
        for place in range(PAIR):
            i = place * blocks
            states.append(
                jnp.concatenate([falls[i] * eye - maps[i][:, BLK:], maps[i][:, :BLK]], axis=1)
            )
        for block in range(1, blocks):
            for place in range(PAIR):
                i = place * blocks + block
                low = states[place].astype(BF)
                prior_ref[PAIR * pair + place, block - 1] = low
                state = falls[i] * states[place] - dot(maps[i][:, BLK:].astype(BF), low)
                states[place] = jnp.concatenate(
                    [state[:, :BLK], state[:, BLK:] + maps[i][:, :BLK]], axis=1
                )
            yield
        for place in range(PAIR):
            pair_ref[PAIR * pair + place] = states[place].astype(BF)

    @pl.when(step == 0)
    def _():
        make_masks(mask_ref)
        for _ in front(0, k_first, v_first, 0):
            pass

    for slot in range(2):

        @pl.when((step % 2 == slot) & (step < last))
        def _():
            together(back(step, slot), front(step + 1, k_next, v_next, 1 - slot))

    @pl.when(step == last)
    def _():
        for _ in back(last, last % 2):
            pass


def query_side(
    odd_ref, rows_ref, g_ref, weight_ref, taps_ref, halo_ref, gain_ref, q_ref, z_ref, kt_ref,
    uw_ref, prior_ref, near_ref, scaled_ref, base_ref, gate_ref, pad_ref, *, first_step,
):
    local_step = pl.program_id(0)
    step = local_step + first_step
    length = q_ref.shape[0]
    blocks = length // BLK
    levels = scaled_ref.shape[2] // BLK + 1
    per_head = levels + 1
    width = weight_ref.shape[1]
    odd = odd_ref[0].astype(F32)
    turned_g = pltpu.roll(g_ref[...], BLK - QUERY_HEADS * step, 1)
    turned_w = pltpu.roll(weight_ref[...], width - QUERY_HEADS * per_head * step, 1)
    for head in range(QUERY_HEADS):
        lanes = slice(head * BLK, (head + 1) * BLK)
        fill_padded(pad_ref, head, q_ref, halo_ref[0, :, lanes], lanes)
        where = QUERY_HEADS * step + head
        out = QUERY_HEADS * local_step + head
        near = near_ref[where, :, BLK:] * odd.astype(BF)
        first = head * per_head
        for block in range(blocks):
            start = block * BLK
            tokens = slice(start, start + BLK)
            queries = unit(conv_rows(pad_ref, head, taps_ref[0, :, lanes], start, BLK)).astype(BF)
            g_col = jnp.broadcast_to(turned_g[tokens, head : head + 1], (BLK, BLK))
            g_row = rows_ref[head, 0:1, tokens]
            beta_row = rows_ref[head, 1:2, tokens]
            mixing = (
                decay_matrix(g_col, g_row, beta_row) * dot(queries, kt_ref[where, :, tokens])
            ).astype(BF)
            inner = dot(mixing, uw_ref[where, tokens, :])
            through = jnp.exp2(g_col) * queries.astype(F32) - inner[:, BLK:]
            if block == 0:
                carried, local = through, inner[:, :BLK]
            else:
                passed = dot(through.astype(BF), prior_ref[where, block - 1])
                carried, local = passed[:, :BLK], inner[:, :BLK] + passed[:, BLK:]
            scaled = [
                (carried * turned_w[tokens, first + level : first + level + 1]).astype(BF)
                for level in range(1, per_head)
            ]
            base_ref[out, tokens, :] = turned_w[tokens, first : first + 1] * local + dot(
                scaled[0], near
            )
            scaled_ref[out, tokens, :] = jnp.concatenate(scaled[1:], axis=1)
            gate_ref[out, tokens, :] = silu(z_ref[tokens, lanes].astype(F32)) * gain_ref[...]


def finish_side(
    core_ref, near_ref, own_ref, other_ref, scaled_0, base_0, gate_0, scaled_1, base_1, gate_1,
    out_ref,
):
    step = pl.program_id(0)
    core = core_ref[0]
    length = out_ref.shape[0]
    blocks = length // BLK
    levels = own_ref.shape[2] // BLK
    fold = pl.num_programs(0) // 2
    eye = jnp.where(iota2((BLK, BLK), 0) == iota2((BLK, BLK), 1), 1.0, 0.0).astype(BF)

    def part(second, scaled_ref, base_ref, gate_ref):
        mine = core == second
        for head in range(FINISH_HEADS):
            lanes = slice(head * BLK, (head + 1) * BLK)
            place = step % fold * FINISH_HEADS + head
            reach = jnp.where(core == 1, near_ref[step * FINISH_HEADS + head, :, :BLK], eye)
            seen = dot(reach, jnp.where(mine, own_ref[place], other_ref[place])).astype(BF)
            states = jnp.concatenate(
                [seen[:, level * BLK : (level + 1) * BLK] for level in range(levels)], axis=0
            )
            for block in range(blocks):
                tokens = slice(block * BLK, (block + 1) * BLK)
                opened = base_ref[place, tokens, :] + dot(scaled_ref[place, tokens, :], states)
                square = jnp.sum(opened * opened, axis=-1, keepdims=True) * (1.0 / BLK)
                normed = opened * lax.rsqrt(square + EPS)
                out_ref[tokens, lanes] = (normed * gate_ref[place, tokens, :]).astype(BF)

    @pl.when(step < fold)
    def _():
        part(0, scaled_0, base_0, gate_0)

    @pl.when(step >= fold)
    def _():
        part(1, scaled_1, base_1, gate_1)


def merged(left, right_a, right_b):
    moved = dot(right_a.astype(BF), left.astype(BF))
    return jnp.concatenate([moved[:, :BLK], moved[:, BLK:] + right_b.astype(F32)], axis=1)


def fetch(pairs, sem):
    copies = [
        pltpu.make_async_copy(source, target, sem.at[i])
        for i, (source, target) in enumerate(pairs)
    ]
    for copy in copies:
        copy.start()
    for copy in copies:
        copy.wait()


def join_near(core_ref, pair_ref, far_ref, next_ref, own, far, sem):
    core = core_ref[0]
    half = pl.ds(core * own.shape[0], own.shape[0])
    fetch([(pair_ref.at[half], own), (far_ref.at[half], far)], sem)

    @pl.when(core == 1)
    def _():
        for head in range(own.shape[0]):
            next_ref[head] = merged(far[head], own[head, :, :BLK], own[head, :, BLK:]).astype(BF)

    @pl.when(core == 0)
    def _():
        for head in range(own.shape[0]):
            next_ref[head] = merged(own[head], far[head, :, :BLK], far[head, :, BLK:]).astype(BF)


def join_far(upper_ref, pair_ref, far_ref, *rest):
    next_ref, state_ref, onward_ref, own, far, sem = rest[-6:]
    reach_ref = rest[0] if len(rest) == 7 else None
    lanes = slice(2 * BLK - next_ref.shape[2], 2 * BLK)
    fetch([(pair_ref, own), (far_ref, far)], sem)

    @pl.when(upper_ref[0] == 1)
    def _():
        for head in range(own.shape[0]):
            seen = far[head] if reach_ref is None else dot(reach_ref[head], far[head]).astype(BF)
            onward_ref[head] = seen[:, :BLK]
            state_ref[head] = seen[:, BLK:]
            joined = merged(far[head], own[head, :, :BLK], own[head, :, BLK:]).astype(BF)
            next_ref[head] = joined[:, lanes]

    @pl.when(upper_ref[0] == 0)
    def _():
        row, col = iota2((BLK, BLK), 0), iota2((BLK, BLK), 1)
        for head in range(own.shape[0]):
            joined = merged(own[head], far[head, :, :BLK], far[head, :, BLK:]).astype(BF)
            next_ref[head] = joined[:, lanes]
            state_ref[head] = jnp.zeros((BLK, BLK), BF)
            if reach_ref is None:
                onward_ref[head] = jnp.where(row == col, 1.0, 0.0).astype(BF)
            else:
                onward_ref[head] = reach_ref[head]


def join_top(upper_ref, far_ref, reach_ref, *rest):
    state_refs, (out_ref, far, sem) = rest[:-3], rest[-3:]
    levels = len(state_refs)
    fetch([(far_ref, far)], sem)
    for level in range(levels):
        for head in range(far.shape[0]):
            out_ref[head, :, level * BLK : (level + 1) * BLK] = state_refs[level][head]

    @pl.when(upper_ref[0] == 1)
    def _():
        for head in range(far.shape[0]):
            out_ref[head, :, levels * BLK :] = dot(reach_ref[head], far[head]).astype(BF)

    @pl.when(upper_ref[0] == 0)
    def _():
        for head in range(far.shape[0]):
            out_ref[head, :, levels * BLK :] = jnp.zeros((BLK, BLK), BF)


def shape_of(shape, dtype):
    return jax.ShapeDtypeStruct(shape, dtype)


def in_vmem(*arrays):
    return [pltpu.with_memory_space_constraint(x, pltpu.VMEM) for x in arrays]


def in_hbm(*arrays):
    return [pltpu.with_memory_space_constraint(x, pltpu.HBM) for x in arrays]


def whole(shape):
    return pl.BlockSpec(shape, lambda i: (0,) * len(shape))


def by_head(count, shape, first=0, lane=0):
    tail = (0,) * (len(shape) - 1) + (lane,)
    return pl.BlockSpec((count,) + shape, lambda i: (i + first,) + tail)


def by_column(shape, first=0):
    lead = len(shape) - 1
    return pl.BlockSpec(shape, lambda i: (0,) * lead + (i + first,))


ANY = pl.BlockSpec(memory_space=pl.ANY)
SMEM = pl.BlockSpec(memory_space=pltpu.SMEM)
VMEM = pl.BlockSpec(memory_space=pltpu.VMEM)
COST = pl.CostEstimate(flops=10**10, bytes_accessed=2 * 10**7, transcendentals=10**7)
PARAMS = pltpu.CompilerParams(dimension_semantics=("arbitrary",), vmem_limit_bytes=22 << 20)

SMALL = pltpu.CompilerParams(vmem_limit_bytes=8 << 20)


def bit(position, level):
    return (position // 2**level % 2).astype(jnp.int32).reshape(1)


def keys_of(rows, g_pad, conv_weight, halo, k_in, v_in):
    heads, _, length = rows.shape
    blocks = length // BLK
    width = PAIR * BLK
    steps = heads // PAIR
    units = PAIR * blocks
    first = pl.BlockSpec((length, width), lambda i: (0, 0))
    following = pl.BlockSpec((length, width), lambda i: (0, jnp.minimum(i + 1, steps - 1)))
    keys, values = in_hbm(k_in, v_in)
    return pl.pallas_call(
        key_side,
        grid=(steps,),
        in_specs=[
            whole(rows.shape), whole(g_pad.shape), whole(conv_weight.shape), whole(halo.shape),
            first, first, following, following,
        ],
        out_specs=[VMEM] * 4,
        out_shape=[
            pltpu.VMEM((heads, BLK, length), BF), pltpu.VMEM((heads, length, 2 * BLK), BF),
            pltpu.VMEM((heads, BLK, 2 * BLK), BF),
            pltpu.VMEM((heads, blocks - 1, BLK, 2 * BLK), BF),
        ],
        scratch_shapes=[
            pltpu.VMEM((4 * PAIR, length + 8, BLK), F32),
            pltpu.VMEM((2, units, BLK, BLK), F32),
            pltpu.VMEM((2, units, BLK, 2 * BLK), BF),
            pltpu.VMEM((2, units, BLK, BLK), BF),
            pltpu.VMEM((6, BLK, BLK), BF),
        ],
        compiler_params=PARAMS,
        cost_estimate=COST,
        name="key_side",
    )(rows, g_pad, conv_weight, halo, keys, values, keys, values)


def queries_of(second, levels, core, rows, g_pad, weights, taps, halo, gain, q_in, z_in, *kept):
    heads, _, length = rows.shape
    steps = heads // QUERY_HEADS // 2
    first = steps if second else 0
    width = QUERY_HEADS * BLK
    return pl.pallas_call(
        functools.partial(query_side, first_step=first),
        grid=(steps,),
        in_specs=[
            SMEM, by_head(QUERY_HEADS, (2, length), first), whole(g_pad.shape),
            whole(weights.shape), by_column((3, 4, width), first), by_column((3, 4, width), first),
            whole(gain.shape), by_column((length, width), first), by_column((length, width), first),
        ]
        + [VMEM] * 4,
        out_specs=[VMEM] * 3,
        out_shape=[
            pltpu.VMEM((heads // 2, length, (levels - 1) * BLK), BF),
            pltpu.VMEM((heads // 2, length, BLK), F32),
            pltpu.VMEM((heads // 2, length, BLK), F32),
        ],
        scratch_shapes=[pltpu.VMEM((QUERY_HEADS, length + 8, BLK), F32)],
        compiler_params=PARAMS,
        cost_estimate=COST,
        name="query_side",
    )(core, rows, g_pad, weights, taps, halo, gain, *in_hbm(q_in, z_in), *in_vmem(*kept))


def finished(core, near, own, other, *parts):
    heads, length = near.shape[0], parts[0].shape[1]
    return pl.pallas_call(
        finish_side,
        grid=(heads // FINISH_HEADS,),
        in_specs=[SMEM] + [VMEM] * 9,
        out_specs=by_column((length, FINISH_HEADS * BLK)),
        out_shape=shape_of((length, heads * BLK), BF),
        compiler_params=PARAMS,
        name="finish_side",
    )(core, *in_vmem(near, own, other, *parts))


def cut_edges(q_ref, k_ref, v_ref, out_ref, rows_ref, sem):
    length = q_ref.shape[0]
    last = pl.ds(length - 8, 8)
    fetch([(ref.at[last], rows_ref.at[i]) for i, ref in enumerate((q_ref, k_ref, v_ref))], sem)
    for i in range(3):
        out_ref[i] = rows_ref[i, 4:8, :]


def edges_of(*arrays):
    columns = arrays[0].shape[1]
    return pl.pallas_call(
        cut_edges,
        in_specs=[ANY] * 3,
        out_specs=VMEM,
        out_shape=pltpu.VMEM((3, 4, columns), BF),
        scratch_shapes=[pltpu.VMEM((3, 8, columns), BF), pltpu.SemaphoreType.DMA((3,))],
        compiler_params=SMALL,
        name="cut_edges",
    )(*in_hbm(*arrays))


def joined_near(core, pair, near):
    shape = (pair.shape[0] // 2,) + pair.shape[1:]
    return pl.pallas_call(
        join_near,
        in_specs=[SMEM, ANY, ANY],
        out_specs=VMEM,
        out_shape=shape_of(shape, BF),
        scratch_shapes=[
            pltpu.VMEM(shape, BF), pltpu.VMEM(shape, BF), pltpu.SemaphoreType.DMA((2,)),
        ],
        compiler_params=SMALL,
        name="join_near",
    )(core, pair, near)


def joined_far(upper, pair, far, reach, last):
    square = (pair.shape[0], BLK, BLK)
    given = () if reach is None else (reach,)
    return pl.pallas_call(
        join_far,
        in_specs=[SMEM, ANY, ANY] + [VMEM] * len(given),
        out_specs=[VMEM] * 3,
        out_shape=[shape_of(square if last else pair.shape, BF)] + [shape_of(square, BF)] * 2,
        scratch_shapes=[
            pltpu.VMEM(pair.shape, BF), pltpu.VMEM(pair.shape, BF), pltpu.SemaphoreType.DMA((2,)),
        ],
        compiler_params=SMALL,
        name="join_far",
    )(upper, pair, far, *given)


def joined_top(upper, far, reach, states):
    shape = (far.shape[0], BLK, (len(states) + 1) * BLK)
    return pl.pallas_call(
        join_top,
        in_specs=[SMEM, ANY] + [VMEM] * (1 + len(states)),
        out_specs=VMEM,
        out_shape=shape_of(shape, BF),
        scratch_shapes=[pltpu.VMEM(far.shape, BF), pltpu.SemaphoreType.DMA((1,))],
        compiler_params=SMALL,
        name="join_top",
    )(upper, far, reach, *states)


def per_device(q_in, k_in, v_in, z_in, log_gate, beta, level_weight, conv_weight, norm_gain):
    length, heads = log_gate.shape
    blocks = length // BLK
    ctx = lax.axis_size("ctx")
    levels = ctx.bit_length() - 1
    position = lax.axis_index("ctx")
    halo = lax.ppermute(edges_of(q_in, k_in, v_in), "ctx", [(i, i + 1) for i in range(ctx - 1)])

    g = jnp.cumsum(log_gate.reshape(blocks, BLK, heads), axis=1).reshape(length, heads) * LOG2_E
    g_pad = jnp.pad(g, ((0, 0), (0, BLK - heads)))
    rows = jnp.stack([g.T, beta.T], axis=1)
    weights = level_weight[:, :, : levels + 1].reshape(length, heads * (levels + 1))
    weights = jnp.pad(weights, ((0, 0), (0, -weights.shape[1] % BLK)))
    bits = [bit(position, level) for level in range(levels)]
    halo, rows, g_pad, weights, *bits = lax.optimization_barrier(
        (halo, rows, g_pad, weights, *bits)
    )
    core = bits[0]

    kt, uw, pair, prior = keys_of(rows, g_pad, conv_weight, halo, k_in, v_in)
    near = lax.ppermute(pair, "ctx", [(i, i ^ 1) for i in range(ctx)])
    pair = joined_near(core, pair, near)

    gain = norm_gain.reshape(1, BLK)

    def queries(second, q_in):
        return queries_of(
            second, levels, core, rows, g_pad, weights, conv_weight, halo, gain, q_in, z_in,
            kt, uw, prior, near,
        )

    reach, states = None, []
    for level in range(1, levels - 1):
        far = lax.ppermute(pair, "ctx", [(i, i ^ 2**level) for i in range(ctx)])
        if level == 1:
            far, *parts = lax.optimization_barrier((far, *queries(False, q_in)))
        pair, state, reach = joined_far(bits[level], pair, far, reach, level == levels - 2)
        states.append(state)
    top = levels - 1
    pair, later_q = lax.optimization_barrier((pair, q_in))
    far = lax.ppermute(pair, "ctx", [(i, i ^ 2**top) for i in range(ctx)])
    far, *more = lax.optimization_barrier((far, *queries(True, later_q)))
    own = joined_top(bits[top], far, reach, states)
    other = lax.ppermute(own, "ctx", [(i, i ^ 1) for i in range(ctx)])
    return finished(core, near, own, other, *parts, *more)


def solution(mesh):
    placed = (
        P(("batch", "ctx"), None),
        P(("batch", "ctx"), None),
        P(("batch", "ctx"), None),
        P(("batch", "ctx"), None),
        P(("batch", "ctx"), None),
        P(("batch", "ctx"), None),
        P(("batch", "ctx"), None, None),
        P(),
        P(),
    )
    return jax.shard_map(
        per_device, mesh=mesh, in_specs=placed, out_specs=P(("batch", "ctx"), None), check_vma=False
    )
```

```python
import functools

import jax
import jax.numpy as jnp
from jax import lax
from jax.experimental import pallas as pl
from jax.experimental.pallas import tpu as pltpu
from jax.sharding import PartitionSpec as P

BLK = 128
SUB = 16
PAIR = 4
QUERY_HEADS = 4
FINISH_HEADS = 4
EPS = 1e-06
LOG2_E = 1.4426950408889634
BF = jnp.bfloat16
F32 = jnp.float32


def dot(first, second):
    return lax.dot_general(
        first, second, (((1,), (0,)), ((), ())), preferred_element_type=F32
    )


def silu(value):
    return value * pl.reciprocal(1.0 + jnp.exp(-value), approx=False)


def fill_padded(pad_ref, slot, x_ref, halo, lanes):
    pad_ref[slot, 4:8, :] = halo.astype(F32)
    pad_ref[slot, 8:, :] = x_ref[:, lanes].astype(F32)


def conv_rows(pad_ref, slot, taps, start, count):
    total = taps[0:1] * pad_ref[slot, start + 5 : start + 5 + count, :]
    for tap in range(1, 4):
        total = total + taps[tap : tap + 1] * pad_ref[
            slot, start + 5 + tap : start + 5 + tap + count, :
        ]
    return silu(total)


def unit(rows):
    return rows * lax.rsqrt(jnp.sum(rows * rows, axis=-1, keepdims=True) + EPS)


def iota2(shape, dim):
    return lax.broadcasted_iota(jnp.int32, shape, dim)


def decay_matrix(g_col, g_row, beta_row):
    size = g_col.shape[0]
    causal = iota2((size, BLK), 1) <= iota2((size, BLK), 0)
    return jnp.exp2(jnp.where(causal, g_col - g_row, -1e30)) * beta_row


def make_masks(mask_ref):
    row, col = iota2((BLK, BLK), 0), iota2((BLK, BLK), 1)
    size, index = SUB, 0
    while size < BLK:
        same = row // size == col // size
        pair = row // (2 * size) == col // (2 * size)
        high_low = pair & (row // size % 2 == 1) & (col // size % 2 == 0)
        mask_ref[index] = jnp.where(same, 1.0, 0.0).astype(BF)
        mask_ref[index + 1] = jnp.where(high_low, 1.0, 0.0).astype(BF)
        size, index = size * 2, index + 2


def tiled(packed, times, mask):
    return jnp.concatenate([packed.astype(BF)] * times, axis=0) * mask


def picked(lower, size, offset):
    groups = BLK // size if offset is None else BLK // (2 * size)
    step = size if offset is None else 2 * size
    first = 0 if offset is None else offset
    lane = iota2((size, BLK), 1) // step
    out = lower[first : first + size]
    for group in range(1, groups):
        begin = first + group * step
        out = jnp.where(lane == group, lower[begin : begin + size], out)
    return out


def inverses(lowers, mask_ref, results):
    every = range(len(lowers))
    row, col = iota2((SUB, BLK), 0), iota2((SUB, BLK), 1) % SUB
    eye = jnp.where(row == col, 1.0, 0.0).astype(F32)
    strict = col < row
    same = mask_ref[0]
    times = BLK // SUB
    powers = [jnp.where(strict, -picked(lower, SUB, None), 0.0) for lower in lowers]
    results[:] = [eye + power for power in powers]
    powers = [dot(p.astype(BF), tiled(p, times, same)) for p in powers]
    yield
    reach = 2
    while reach < SUB // 2:
        both = [
            dot(
                jnp.concatenate([powers[i].astype(BF), results[i].astype(BF)], axis=0),
                tiled(powers[i], times, same),
            )
            for i in every
        ]
        yield
        powers = [x[:SUB] for x in both]
        results[:] = [results[i] + both[i][SUB:] for i in every]
        reach *= 2
    results[:] = [
        results[i] + dot(results[i].astype(BF), tiled(powers[i], times, same)) for i in every
    ]
    yield
    size, index = SUB, 0
    while size < BLK:
        times = BLK // size
        low = iota2((size, BLK), 1) // size % 2 == 0
        cross = [picked(lower, size, size).astype(BF) for lower in lowers]
        moved = [dot(cross[i], tiled(results[i], times, mask_ref[index])) for i in every]
        yield
        turned = [
            dot(results[i].astype(BF), tiled(moved[i], times, mask_ref[index + 1]))
            for i in every
        ]
        yield
        results[:] = [
            jnp.concatenate(
                [jnp.where(low, results[i], 0.0), jnp.where(low, -turned[i], results[i])], axis=0
            )
            for i in every
        ]
        size, index = size * 2, index + 2


def together(first, second):
    live = [first, second]
    while live:
        for stages in list(live):
            if next(stages, live) is live:
                live.remove(stages)


def key_side(
    rows_ref, g_ref, taps_ref, halo_ref, k_first, v_first, k_next, v_next,
    kt_ref, uw_ref, pair_ref, prior_ref, pad_ref, low_ref, right_ref, tail_ref, mask_ref,
):
    step = pl.program_id(0)
    length = k_first.shape[0]
    blocks = length // BLK
    last = kt_ref.shape[0] // PAIR - 1
    eye = jnp.where(iota2((BLK, BLK), 0) == iota2((BLK, BLK), 1), 1.0, 0.0).astype(F32)

    def front(pair, k_ref, v_ref, slot):
        turned_g = pltpu.roll(g_ref[...], BLK - PAIR * pair, 1)
        for place in range(PAIR):
            head = PAIR * pair + place
            lanes = slice(place * BLK, (place + 1) * BLK)
            columns = pl.ds(pl.multiple_of(head * BLK, BLK), BLK)
            pad = 2 * (PAIR * slot + place)
            fill_padded(pad_ref, pad, k_ref, halo_ref[1, :, columns], lanes)
            fill_padded(pad_ref, pad + 1, v_ref, halo_ref[2, :, columns], lanes)
            key_taps, value_taps = taps_ref[1, :, columns], taps_ref[2, :, columns]
            for block in range(blocks):
                i = place * blocks + block
                start = block * BLK
                tokens = slice(start, start + BLK)
                keys = unit(conv_rows(pad_ref, pad, key_taps, start, BLK)).astype(BF)
                values = conv_rows(pad_ref, pad + 1, value_taps, start, BLK)
                keys_f = keys.astype(F32)
                turned = keys_f.T
                turned_b = turned.astype(BF)
                kt_ref[head, :, tokens] = turned_b
                right_ref[slot, i, :, :BLK] = values.astype(BF)
                yield
                g_col = jnp.broadcast_to(turned_g[tokens, place : place + 1], (BLK, BLK))
                g_row = rows_ref[head, 0:1, tokens]
                beta_row = rows_ref[head, 1:2, tokens]
                g_last = g_row[:, BLK - 1 : BLK]
                low_ref[slot, i] = decay_matrix(g_col, g_row, beta_row) * dot(keys, turned_b)
                right_ref[slot, i, :, BLK:] = (jnp.exp2(g_col) * keys_f).astype(BF)
                tail_ref[slot, i] = (turned * (jnp.exp2(g_last - g_row) * beta_row)).astype(BF)
                yield

    def back(pair, slot):
        solved = []
        yield from inverses(
            [low_ref.at[slot, i] for i in range(PAIR * blocks)], mask_ref, solved
        )
        maps = []
        for i in range(PAIR * blocks):
            fresh = dot(solved[i].astype(BF), right_ref[slot, i]).astype(BF)
            tokens = slice(i % blocks * BLK, (i % blocks + 1) * BLK)
            uw_ref[PAIR * pair + i // blocks, tokens, :] = fresh
            maps.append(fresh)
        yield
        maps = [dot(tail_ref[slot, i], maps[i]) for i in range(PAIR * blocks)]
        yield
        states, falls = [], []
        for i in range(PAIR * blocks):
            end = (i % blocks + 1) * BLK
            falls.append(
                jnp.exp2(rows_ref[PAIR * pair + i // blocks, 0:1, end - 1 : end])
            )
        for place in range(PAIR):
            i = place * blocks
            states.append(
                jnp.concatenate([falls[i] * eye - maps[i][:, BLK:], maps[i][:, :BLK]], axis=1)
            )
        for block in range(1, blocks):
            for place in range(PAIR):
                i = place * blocks + block
                low = states[place].astype(BF)
                prior_ref[PAIR * pair + place, block - 1] = low
                state = falls[i] * states[place] - dot(maps[i][:, BLK:].astype(BF), low)
                states[place] = jnp.concatenate(
                    [state[:, :BLK], state[:, BLK:] + maps[i][:, :BLK]], axis=1
                )
            yield
        for place in range(PAIR):
            pair_ref[PAIR * pair + place] = states[place].astype(BF)

    @pl.when(step == 0)
    def _():
        make_masks(mask_ref)
        for _ in front(0, k_first, v_first, 0):
            pass

    for slot in range(2):

        @pl.when((step % 2 == slot) & (step < last))
        def _():
            together(back(step, slot), front(step + 1, k_next, v_next, 1 - slot))

    @pl.when(step == last)
    def _():
        for _ in back(last, last % 2):
            pass


def query_side(
    odd_ref, rows_ref, g_ref, weight_ref, taps_ref, halo_ref, gain_ref, q_ref, z_ref, kt_ref,
    uw_ref, prior_ref, near_ref, scaled_ref, base_ref, gate_ref, pad_ref, *, first_step,
):
    local_step = pl.program_id(0)
    step = local_step + first_step
    length = q_ref.shape[0]
    blocks = length // BLK
    levels = scaled_ref.shape[2] // BLK + 1
    per_head = levels + 1
    width = weight_ref.shape[1]
    odd = odd_ref[0].astype(F32)
    turned_g = pltpu.roll(g_ref[...], BLK - QUERY_HEADS * step, 1)
    turned_w = pltpu.roll(weight_ref[...], width - QUERY_HEADS * per_head * step, 1)
    for head in range(QUERY_HEADS):
        lanes = slice(head * BLK, (head + 1) * BLK)
        fill_padded(pad_ref, head, q_ref, halo_ref[0, :, lanes], lanes)
        where = QUERY_HEADS * step + head
        out = QUERY_HEADS * local_step + head
        near = near_ref[where, :, BLK:] * odd.astype(BF)
        first = head * per_head
        for block in range(blocks):
            start = block * BLK
            tokens = slice(start, start + BLK)
            queries = unit(conv_rows(pad_ref, head, taps_ref[0, :, lanes], start, BLK)).astype(BF)
            g_col = jnp.broadcast_to(turned_g[tokens, head : head + 1], (BLK, BLK))
            g_row = rows_ref[head, 0:1, tokens]
            beta_row = rows_ref[head, 1:2, tokens]
            mixing = (
                decay_matrix(g_col, g_row, beta_row) * dot(queries, kt_ref[where, :, tokens])
            ).astype(BF)
            inner = dot(mixing, uw_ref[where, tokens, :])
            through = jnp.exp2(g_col) * queries.astype(F32) - inner[:, BLK:]
            if block == 0:
                carried, local = through, inner[:, :BLK]
            else:
                passed = dot(through.astype(BF), prior_ref[where, block - 1])
                carried, local = passed[:, :BLK], inner[:, :BLK] + passed[:, BLK:]
            scaled = [
                (carried * turned_w[tokens, first + level : first + level + 1]).astype(BF)
                for level in range(1, per_head)
            ]
            base_ref[out, tokens, :] = turned_w[tokens, first : first + 1] * local + dot(
                scaled[0], near
            )
            scaled_ref[out, tokens, :] = jnp.concatenate(scaled[1:], axis=1)
            gate_ref[out, tokens, :] = silu(z_ref[tokens, lanes].astype(F32)) * gain_ref[...]


def finish_side(
    half_ref, core_ref, near_ref, state_ref, scaled_0, base_0, gate_0, scaled_1, base_1, gate_1,
    *rest,
):
    out_ref = rest[-1]
    step = pl.program_id(0)
    half = half_ref[0]
    length = out_ref.shape[0]
    blocks = length // BLK
    levels = state_ref.shape[2] // BLK
    eye = jnp.where(iota2((BLK, BLK), 0) == iota2((BLK, BLK), 1), 1.0, 0.0).astype(BF)

    def part(scaled_ref, base_ref, gate_ref):
        for head in range(FINISH_HEADS):
            lanes = slice(head * BLK, (head + 1) * BLK)
            place = step * FINISH_HEADS + head
            near = near_ref[half * state_ref.shape[0] + place, :, :BLK]
            seen = dot(jnp.where(core_ref[0] == 1, near, eye), state_ref[place]).astype(BF)
            states = jnp.concatenate(
                [seen[:, level * BLK : (level + 1) * BLK] for level in range(levels)], axis=0
            )
            for block in range(blocks):
                tokens = slice(block * BLK, (block + 1) * BLK)
                opened = base_ref[place, tokens, :] + dot(scaled_ref[place, tokens, :], states)
                square = jnp.sum(opened * opened, axis=-1, keepdims=True) * (1.0 / BLK)
                normed = opened * lax.rsqrt(square + EPS)
                out_ref[tokens, lanes] = (normed * gate_ref[place, tokens, :]).astype(BF)

    @pl.when(half == 0)
    def _():
        part(scaled_0, base_0, gate_0)

    @pl.when(half == 1)
    def _():
        part(scaled_1, base_1, gate_1)


def merged(left, right_a, right_b):
    moved = dot(right_a.astype(BF), left.astype(BF))
    return jnp.concatenate([moved[:, :BLK], moved[:, BLK:] + right_b.astype(F32)], axis=1)


def fetch(pairs, sem):
    copies = [
        pltpu.make_async_copy(source, target, sem.at[i])
        for i, (source, target) in enumerate(pairs)
    ]
    for copy in copies:
        copy.start()
    for copy in copies:
        copy.wait()


def join_near(core_ref, pair_ref, far_ref, next_ref, own, far, sem):
    core = core_ref[0]
    half = pl.ds(core * own.shape[0], own.shape[0])
    fetch([(pair_ref.at[half], own), (far_ref.at[half], far)], sem)

    @pl.when(core == 1)
    def _():
        for head in range(own.shape[0]):
            next_ref[head] = merged(far[head], own[head, :, :BLK], own[head, :, BLK:]).astype(BF)

    @pl.when(core == 0)
    def _():
        for head in range(own.shape[0]):
            next_ref[head] = merged(own[head], far[head, :, :BLK], far[head, :, BLK:]).astype(BF)


def join_far(upper_ref, pair_ref, far_ref, *rest):
    next_ref, state_ref, onward_ref, own, far, sem = rest[-6:]
    reach_ref = rest[0] if len(rest) == 7 else None
    lanes = slice(2 * BLK - next_ref.shape[2], 2 * BLK)
    fetch([(pair_ref, own), (far_ref, far)], sem)

    @pl.when(upper_ref[0] == 1)
    def _():
        for head in range(own.shape[0]):
            seen = far[head] if reach_ref is None else dot(reach_ref[head], far[head]).astype(BF)
            onward_ref[head] = seen[:, :BLK]
            state_ref[head] = seen[:, BLK:]
            joined = merged(far[head], own[head, :, :BLK], own[head, :, BLK:]).astype(BF)
            next_ref[head] = joined[:, lanes]

    @pl.when(upper_ref[0] == 0)
    def _():
        row, col = iota2((BLK, BLK), 0), iota2((BLK, BLK), 1)
        for head in range(own.shape[0]):
            joined = merged(own[head], far[head, :, :BLK], far[head, :, BLK:]).astype(BF)
            next_ref[head] = joined[:, lanes]
            state_ref[head] = jnp.zeros((BLK, BLK), BF)
            if reach_ref is None:
                onward_ref[head] = jnp.where(row == col, 1.0, 0.0).astype(BF)
            else:
                onward_ref[head] = reach_ref[head]


def join_top(upper_ref, far_ref, reach_ref, *rest):
    state_refs, (out_ref, far, sem) = rest[:-3], rest[-3:]
    levels = len(state_refs)
    fetch([(far_ref, far)], sem)
    for level in range(levels):
        for head in range(far.shape[0]):
            out_ref[head, :, level * BLK : (level + 1) * BLK] = state_refs[level][head]

    @pl.when(upper_ref[0] == 1)
    def _():
        for head in range(far.shape[0]):
            out_ref[head, :, levels * BLK :] = dot(reach_ref[head], far[head]).astype(BF)

    @pl.when(upper_ref[0] == 0)
    def _():
        for head in range(far.shape[0]):
            out_ref[head, :, levels * BLK :] = jnp.zeros((BLK, BLK), BF)


def shape_of(shape, dtype):
    return jax.ShapeDtypeStruct(shape, dtype)


def in_vmem(*arrays):
    return [pltpu.with_memory_space_constraint(x, pltpu.VMEM) for x in arrays]


def in_hbm(*arrays):
    return [pltpu.with_memory_space_constraint(x, pltpu.HBM) for x in arrays]


def whole(shape):
    return pl.BlockSpec(shape, lambda i: (0,) * len(shape))


def by_head(count, shape, first=0, lane=0):
    tail = (0,) * (len(shape) - 1) + (lane,)
    return pl.BlockSpec((count,) + shape, lambda i: (i + first,) + tail)


def by_column(shape, first=0):
    lead = len(shape) - 1
    return pl.BlockSpec(shape, lambda i: (0,) * lead + (i + first,))


ANY = pl.BlockSpec(memory_space=pl.ANY)
SMEM = pl.BlockSpec(memory_space=pltpu.SMEM)
VMEM = pl.BlockSpec(memory_space=pltpu.VMEM)
COST = pl.CostEstimate(flops=10**10, bytes_accessed=2 * 10**7, transcendentals=10**7)
PARAMS = pltpu.CompilerParams(dimension_semantics=("arbitrary",), vmem_limit_bytes=22 << 20)

SMALL = pltpu.CompilerParams(vmem_limit_bytes=8 << 20)


def bit(position, level):
    return (position // 2**level % 2).astype(jnp.int32).reshape(1)


def keys_of(rows, g_pad, conv_weight, halo, k_in, v_in):
    heads, _, length = rows.shape
    blocks = length // BLK
    width = PAIR * BLK
    steps = heads // PAIR
    units = PAIR * blocks
    first = pl.BlockSpec((length, width), lambda i: (0, 0))
    following = pl.BlockSpec((length, width), lambda i: (0, jnp.minimum(i + 1, steps - 1)))
    keys, values = in_hbm(k_in, v_in)
    return pl.pallas_call(
        key_side,
        grid=(steps,),
        in_specs=[
            whole(rows.shape), whole(g_pad.shape), whole(conv_weight.shape), whole(halo.shape),
            first, first, following, following,
        ],
        out_specs=[VMEM] * 4,
        out_shape=[
            pltpu.VMEM((heads, BLK, length), BF), pltpu.VMEM((heads, length, 2 * BLK), BF),
            pltpu.VMEM((heads, BLK, 2 * BLK), BF),
            pltpu.VMEM((heads, blocks - 1, BLK, 2 * BLK), BF),
        ],
        scratch_shapes=[
            pltpu.VMEM((4 * PAIR, length + 8, BLK), F32),
            pltpu.VMEM((2, units, BLK, BLK), F32),
            pltpu.VMEM((2, units, BLK, 2 * BLK), BF),
            pltpu.VMEM((2, units, BLK, BLK), BF),
            pltpu.VMEM((6, BLK, BLK), BF),
        ],
        compiler_params=PARAMS,
        cost_estimate=COST,
        name="key_side",
    )(rows, g_pad, conv_weight, halo, keys, values, keys, values)


def queries_of(second, levels, core, rows, g_pad, weights, taps, halo, gain, q_in, z_in, *kept):
    heads, _, length = rows.shape
    steps = heads // QUERY_HEADS // 2
    first = steps if second else 0
    width = QUERY_HEADS * BLK
    return pl.pallas_call(
        functools.partial(query_side, first_step=first),
        grid=(steps,),
        in_specs=[
            SMEM, by_head(QUERY_HEADS, (2, length), first), whole(g_pad.shape),
            whole(weights.shape), by_column((3, 4, width), first), by_column((3, 4, width), first),
            whole(gain.shape), by_column((length, width), first), by_column((length, width), first),
        ]
        + [VMEM] * 4,
        out_specs=[VMEM] * 3,
        out_shape=[
            pltpu.VMEM((heads // 2, length, (levels - 1) * BLK), BF),
            pltpu.VMEM((heads // 2, length, BLK), F32),
            pltpu.VMEM((heads // 2, length, BLK), F32),
        ],
        scratch_shapes=[pltpu.VMEM((QUERY_HEADS, length + 8, BLK), F32)],
        compiler_params=PARAMS,
        cost_estimate=COST,
        name="query_side",
    )(core, rows, g_pad, weights, taps, halo, gain, *in_hbm(q_in, z_in), *in_vmem(*kept))


def finished(half, core, near, states, parts, previous):
    heads, length = near.shape[0], parts[0].shape[1]
    steps = heads // FINISH_HEADS // 2
    return pl.pallas_call(
        finish_side,
        grid_spec=pltpu.PrefetchScalarGridSpec(
            num_scalar_prefetch=1,
            grid=(steps,),
            in_specs=[SMEM] + [VMEM] * 8 + [ANY] * len(previous),
            out_specs=pl.BlockSpec(
                (length, FINISH_HEADS * BLK), lambda i, half: (0, half[0] * steps + i)
            ),
        ),
        out_shape=shape_of((length, heads * BLK), BF),
        input_output_aliases={10 + i: i for i in range(len(previous))},
        compiler_params=PARAMS,
        cost_estimate=COST,
        name="finish_side",
    )(half, core, *in_vmem(near, states, *parts), *previous)


def cut_edges(q_ref, k_ref, v_ref, out_ref, rows_ref, sem):
    length = q_ref.shape[0]
    last = pl.ds(length - 8, 8)
    fetch([(ref.at[last], rows_ref.at[i]) for i, ref in enumerate((q_ref, k_ref, v_ref))], sem)
    for i in range(3):
        out_ref[i] = rows_ref[i, 4:8, :]


def edges_of(*arrays):
    columns = arrays[0].shape[1]
    return pl.pallas_call(
        cut_edges,
        in_specs=[ANY] * 3,
        out_specs=VMEM,
        out_shape=pltpu.VMEM((3, 4, columns), BF),
        scratch_shapes=[pltpu.VMEM((3, 8, columns), BF), pltpu.SemaphoreType.DMA((3,))],
        compiler_params=SMALL,
        name="cut_edges",
    )(*in_hbm(*arrays))


def joined_near(core, pair, near):
    shape = (pair.shape[0] // 2,) + pair.shape[1:]
    return pl.pallas_call(
        join_near,
        in_specs=[SMEM, ANY, ANY],
        out_specs=VMEM,
        out_shape=shape_of(shape, BF),
        scratch_shapes=[
            pltpu.VMEM(shape, BF), pltpu.VMEM(shape, BF), pltpu.SemaphoreType.DMA((2,)),
        ],
        compiler_params=SMALL,
        name="join_near",
    )(core, pair, near)


def joined_far(upper, pair, far, reach, last):
    square = (pair.shape[0], BLK, BLK)
    given = () if reach is None else (reach,)
    return pl.pallas_call(
        join_far,
        in_specs=[SMEM, ANY, ANY] + [VMEM] * len(given),
        out_specs=[VMEM] * 3,
        out_shape=[shape_of(square if last else pair.shape, BF)] + [shape_of(square, BF)] * 2,
        scratch_shapes=[
            pltpu.VMEM(pair.shape, BF), pltpu.VMEM(pair.shape, BF), pltpu.SemaphoreType.DMA((2,)),
        ],
        compiler_params=SMALL,
        name="join_far",
    )(upper, pair, far, *given)


def joined_top(upper, far, reach, states):
    shape = (far.shape[0], BLK, (len(states) + 1) * BLK)
    return pl.pallas_call(
        join_top,
        in_specs=[SMEM, ANY] + [VMEM] * (1 + len(states)),
        out_specs=VMEM,
        out_shape=shape_of(shape, BF),
        scratch_shapes=[pltpu.VMEM(far.shape, BF), pltpu.SemaphoreType.DMA((1,))],
        compiler_params=SMALL,
        name="join_top",
    )(upper, far, reach, *states)


def per_device(q_in, k_in, v_in, z_in, log_gate, beta, level_weight, conv_weight, norm_gain):
    length, heads = log_gate.shape
    blocks = length // BLK
    ctx = lax.axis_size("ctx")
    levels = ctx.bit_length() - 1
    position = lax.axis_index("ctx")
    halo = lax.ppermute(edges_of(q_in, k_in, v_in), "ctx", [(i, i + 1) for i in range(ctx - 1)])

    g = jnp.cumsum(log_gate.reshape(blocks, BLK, heads), axis=1).reshape(length, heads) * LOG2_E
    g_pad = jnp.pad(g, ((0, 0), (0, BLK - heads)))
    rows = jnp.stack([g.T, beta.T], axis=1)
    weights = level_weight[:, :, : levels + 1].reshape(length, heads * (levels + 1))
    weights = jnp.pad(weights, ((0, 0), (0, -weights.shape[1] % BLK)))
    bits = [bit(position, level) for level in range(levels)] + [1 - bit(position, 0)]
    halo, rows, g_pad, weights, *bits = lax.optimization_barrier(
        (halo, rows, g_pad, weights, *bits)
    )
    core, beside = bits[0], bits[-1]

    kt, uw, pair, prior = keys_of(rows, g_pad, conv_weight, halo, k_in, v_in)
    near = lax.ppermute(pair, "ctx", [(i, i ^ 1) for i in range(ctx)])
    pair = joined_near(core, pair, near)

    gain = norm_gain.reshape(1, BLK)

    def queries(second, q_in):
        return queries_of(
            second, levels, core, rows, g_pad, weights, conv_weight, halo, gain, q_in, z_in,
            kt, uw, prior, near,
        )

    reach, states = None, []
    for level in range(1, levels - 1):
        far = lax.ppermute(pair, "ctx", [(i, i ^ 2**level) for i in range(ctx)])
        if level == 1:
            far, *parts = lax.optimization_barrier((far, *queries(False, q_in)))
        pair, state, reach = joined_far(bits[level], pair, far, reach, level == levels - 2)
        states.append(state)
    top = levels - 1
    pair, later_q = lax.optimization_barrier((pair, q_in))
    far = lax.ppermute(pair, "ctx", [(i, i ^ 2**top) for i in range(ctx)])
    far, *more = lax.optimization_barrier((far, *queries(True, later_q)))
    own = joined_top(bits[top], far, reach, states)
    other = lax.ppermute(own, "ctx", [(i, i ^ 1) for i in range(ctx)])
    parts = [*parts, *more]
    out = finished(core, core, near, own, parts, ())
    other, out = lax.optimization_barrier((other, out))
    return finished(beside, core, near, other, parts, (out,))


def solution(mesh):
    placed = (
        P(("batch", "ctx"), None),
        P(("batch", "ctx"), None),
        P(("batch", "ctx"), None),
        P(("batch", "ctx"), None),
        P(("batch", "ctx"), None),
        P(("batch", "ctx"), None),
        P(("batch", "ctx"), None, None),
        P(),
        P(),
    )
    return jax.shard_map(
        per_device, mesh=mesh, in_specs=placed, out_specs=P(("batch", "ctx"), None), check_vma=False
    )
```

```python
import functools

import jax
import jax.numpy as jnp
from jax import lax
from jax.experimental import pallas as pl
from jax.experimental.pallas import tpu as pltpu
from jax.sharding import PartitionSpec as P

BLK = 128
SUB = 16
PAIR = 4
QUERY_HEADS = 4
FINISH_HEADS = 4
EPS = 1e-06
LOG2_E = 1.4426950408889634
BF = jnp.bfloat16
F32 = jnp.float32


def dot(first, second):
    return lax.dot_general(
        first, second, (((1,), (0,)), ((), ())), preferred_element_type=F32
    )


def silu(value):
    return value * pl.reciprocal(1.0 + jnp.exp(-value), approx=False)


def fill_padded(pad_ref, slot, x_ref, halo, lanes):
    pad_ref[slot, 4:8, :] = halo.astype(F32)
    pad_ref[slot, 8:, :] = x_ref[:, lanes].astype(F32)


def conv_rows(pad_ref, slot, taps, start, count):
    total = taps[0:1] * pad_ref[slot, start + 5 : start + 5 + count, :]
    for tap in range(1, 4):
        total = total + taps[tap : tap + 1] * pad_ref[
            slot, start + 5 + tap : start + 5 + tap + count, :
        ]
    return silu(total)


def unit(rows):
    return rows * lax.rsqrt(jnp.sum(rows * rows, axis=-1, keepdims=True) + EPS)


def iota2(shape, dim):
    return lax.broadcasted_iota(jnp.int32, shape, dim)


def decay_matrix(g_col, g_row, beta_row):
    size = g_col.shape[0]
    causal = iota2((size, BLK), 1) <= iota2((size, BLK), 0)
    return jnp.exp2(jnp.where(causal, g_col - g_row, -1e30)) * beta_row


def make_masks(mask_ref):
    row, col = iota2((BLK, BLK), 0), iota2((BLK, BLK), 1)
    size, index = SUB, 0
    while size < BLK:
        same = row // size == col // size
        pair = row // (2 * size) == col // (2 * size)
        high_low = pair & (row // size % 2 == 1) & (col // size % 2 == 0)
        mask_ref[index] = jnp.where(same, 1.0, 0.0).astype(BF)
        mask_ref[index + 1] = jnp.where(high_low, 1.0, 0.0).astype(BF)
        size, index = size * 2, index + 2


def tiled(packed, times, mask):
    return jnp.concatenate([packed.astype(BF)] * times, axis=0) * mask


def picked(lower, size, offset):
    groups = BLK // size if offset is None else BLK // (2 * size)
    step = size if offset is None else 2 * size
    first = 0 if offset is None else offset
    lane = iota2((size, BLK), 1) // step
    out = lower[first : first + size]
    for group in range(1, groups):
        begin = first + group * step
        out = jnp.where(lane == group, lower[begin : begin + size], out)
    return out


def inverses(lowers, mask_ref, results):
    every = range(len(lowers))
    row, col = iota2((SUB, BLK), 0), iota2((SUB, BLK), 1) % SUB
    eye = jnp.where(row == col, 1.0, 0.0).astype(F32)
    strict = col < row
    same = mask_ref[0]
    times = BLK // SUB
    powers = [jnp.where(strict, -picked(lower, SUB, None), 0.0) for lower in lowers]
    results[:] = [eye + power for power in powers]
    powers = [dot(p.astype(BF), tiled(p, times, same)) for p in powers]
    yield
    reach = 2
    while reach < SUB // 2:
        both = [
            dot(
                jnp.concatenate([powers[i].astype(BF), results[i].astype(BF)], axis=0),
                tiled(powers[i], times, same),
            )
            for i in every
        ]
        yield
        powers = [x[:SUB] for x in both]
        results[:] = [results[i] + both[i][SUB:] for i in every]
        reach *= 2
    results[:] = [
        results[i] + dot(results[i].astype(BF), tiled(powers[i], times, same)) for i in every
    ]
    yield
    size, index = SUB, 0
    while size < BLK:
        times = BLK // size
        low = iota2((size, BLK), 1) // size % 2 == 0
        cross = [picked(lower, size, size).astype(BF) for lower in lowers]
        moved = [dot(cross[i], tiled(results[i], times, mask_ref[index])) for i in every]
        yield
        turned = [
            dot(results[i].astype(BF), tiled(moved[i], times, mask_ref[index + 1]))
            for i in every
        ]
        yield
        results[:] = [
            jnp.concatenate(
                [jnp.where(low, results[i], 0.0), jnp.where(low, -turned[i], results[i])], axis=0
            )
            for i in every
        ]
        size, index = size * 2, index + 2


def together(first, second):
    live = [first, second]
    while live:
        for stages in list(live):
            if next(stages, live) is live:
                live.remove(stages)


def key_side(
    rows_ref, g_ref, taps_ref, halo_ref, k_first, v_first, k_next, v_next,
    kt_ref, uw_ref, pair_ref, prior_ref, pad_ref, low_ref, right_ref, tail_ref, mask_ref,
):
    step = pl.program_id(0)
    length = k_first.shape[0]
    blocks = length // BLK
    last = kt_ref.shape[0] // PAIR - 1
    eye = jnp.where(iota2((BLK, BLK), 0) == iota2((BLK, BLK), 1), 1.0, 0.0).astype(F32)

    def front(pair, k_ref, v_ref, slot):
        turned_g = pltpu.roll(g_ref[...], BLK - PAIR * pair, 1)
        for place in range(PAIR):
            head = PAIR * pair + place
            lanes = slice(place * BLK, (place + 1) * BLK)
            columns = pl.ds(pl.multiple_of(head * BLK, BLK), BLK)
            pad = 2 * (PAIR * slot + place)
            fill_padded(pad_ref, pad, k_ref, halo_ref[1, :, columns], lanes)
            fill_padded(pad_ref, pad + 1, v_ref, halo_ref[2, :, columns], lanes)
            key_taps, value_taps = taps_ref[1, :, columns], taps_ref[2, :, columns]
            for block in range(blocks):
                i = place * blocks + block
                start = block * BLK
                tokens = slice(start, start + BLK)
                keys = unit(conv_rows(pad_ref, pad, key_taps, start, BLK)).astype(BF)
                values = conv_rows(pad_ref, pad + 1, value_taps, start, BLK)
                keys_f = keys.astype(F32)
                turned = keys_f.T
                turned_b = turned.astype(BF)
                kt_ref[head, :, tokens] = turned_b
                right_ref[slot, i, :, :BLK] = values.astype(BF)
                yield
                g_col = jnp.broadcast_to(turned_g[tokens, place : place + 1], (BLK, BLK))
                g_row = rows_ref[head, 0:1, tokens]
                beta_row = rows_ref[head, 1:2, tokens]
                g_last = g_row[:, BLK - 1 : BLK]
                low_ref[slot, i] = decay_matrix(g_col, g_row, beta_row) * dot(keys, turned_b)
                right_ref[slot, i, :, BLK:] = (jnp.exp2(g_col) * keys_f).astype(BF)
                tail_ref[slot, i] = (turned * (jnp.exp2(g_last - g_row) * beta_row)).astype(BF)
                yield

    def back(pair, slot):
        solved = []
        yield from inverses(
            [low_ref.at[slot, i] for i in range(PAIR * blocks)], mask_ref, solved
        )
        maps = []
        for i in range(PAIR * blocks):
            fresh = dot(solved[i].astype(BF), right_ref[slot, i]).astype(BF)
            tokens = slice(i % blocks * BLK, (i % blocks + 1) * BLK)
            uw_ref[PAIR * pair + i // blocks, tokens, :] = fresh
            maps.append(fresh)
        yield
        maps = [dot(tail_ref[slot, i], maps[i]) for i in range(PAIR * blocks)]
        yield
        states, falls = [], []
        for i in range(PAIR * blocks):
            end = (i % blocks + 1) * BLK
            falls.append(
                jnp.exp2(rows_ref[PAIR * pair + i // blocks, 0:1, end - 1 : end])
            )
        for place in range(PAIR):
            i = place * blocks
            states.append(
                jnp.concatenate([falls[i] * eye - maps[i][:, BLK:], maps[i][:, :BLK]], axis=1)
            )
        for block in range(1, blocks):
            for place in range(PAIR):
                i = place * blocks + block
                low = states[place].astype(BF)
                prior_ref[PAIR * pair + place, block - 1] = low
                state = falls[i] * states[place] - dot(maps[i][:, BLK:].astype(BF), low)
                states[place] = jnp.concatenate(
                    [state[:, :BLK], state[:, BLK:] + maps[i][:, :BLK]], axis=1
                )
            yield
        for place in range(PAIR):
            pair_ref[PAIR * pair + place] = states[place].astype(BF)

    @pl.when(step == 0)
    def _():
        make_masks(mask_ref)
        for _ in front(0, k_first, v_first, 0):
            pass

    for slot in range(2):

        @pl.when((step % 2 == slot) & (step < last))
        def _():
            together(back(step, slot), front(step + 1, k_next, v_next, 1 - slot))

    @pl.when(step == last)
    def _():
        for _ in back(last, last % 2):
            pass


def query_side(
    odd_ref, rows_ref, g_ref, weight_ref, taps_ref, halo_ref, gain_ref, q_ref, z_ref, kt_ref,
    uw_ref, prior_ref, near_ref, scaled_ref, base_ref, gate_ref, pad_ref, *, first_step,
):
    local_step = pl.program_id(0)
    step = local_step + first_step
    length = q_ref.shape[0]
    blocks = length // BLK
    levels = scaled_ref.shape[2] // BLK + 1
    per_head = levels + 1
    width = weight_ref.shape[1]
    odd = odd_ref[0].astype(F32)
    turned_g = pltpu.roll(g_ref[...], BLK - QUERY_HEADS * step, 1)
    turned_w = pltpu.roll(weight_ref[...], width - QUERY_HEADS * per_head * step, 1)
    for head in range(QUERY_HEADS):
        lanes = slice(head * BLK, (head + 1) * BLK)
        fill_padded(pad_ref, head, q_ref, halo_ref[0, :, lanes], lanes)
        where = QUERY_HEADS * step + head
        out = QUERY_HEADS * local_step + head
        near = near_ref[where, :, BLK:] * odd.astype(BF)
        first = head * per_head
        for block in range(blocks):
            start = block * BLK
            tokens = slice(start, start + BLK)
            queries = unit(conv_rows(pad_ref, head, taps_ref[0, :, lanes], start, BLK)).astype(BF)
            g_col = jnp.broadcast_to(turned_g[tokens, head : head + 1], (BLK, BLK))
            g_row = rows_ref[head, 0:1, tokens]
            beta_row = rows_ref[head, 1:2, tokens]
            mixing = (
                decay_matrix(g_col, g_row, beta_row) * dot(queries, kt_ref[where, :, tokens])
            ).astype(BF)
            inner = dot(mixing, uw_ref[where, tokens, :])
            through = jnp.exp2(g_col) * queries.astype(F32) - inner[:, BLK:]
            if block == 0:
                carried, local = through, inner[:, :BLK]
            else:
                passed = dot(through.astype(BF), prior_ref[where, block - 1])
                carried, local = passed[:, :BLK], inner[:, :BLK] + passed[:, BLK:]
            scaled = [
                (carried * turned_w[tokens, first + level : first + level + 1]).astype(BF)
                for level in range(1, per_head)
            ]
            base_ref[out, tokens, :] = turned_w[tokens, first : first + 1] * local + dot(
                scaled[0], near
            )
            scaled_ref[out, tokens, :] = jnp.concatenate(scaled[1:], axis=1)
            gate_ref[out, tokens, :] = silu(z_ref[tokens, lanes].astype(F32)) * gain_ref[...]


def finish_side(
    half_ref, core_ref, near_ref, state_ref, scaled_0, base_0, gate_0, scaled_1, base_1, gate_1,
    *rest,
):
    out_ref = rest[-1]
    step = pl.program_id(0)
    half = half_ref[0]
    length = out_ref.shape[0]
    blocks = length // BLK
    levels = state_ref.shape[2] // BLK
    eye = jnp.where(iota2((BLK, BLK), 0) == iota2((BLK, BLK), 1), 1.0, 0.0).astype(BF)

    def part(scaled_ref, base_ref, gate_ref):
        for head in range(FINISH_HEADS):
            lanes = slice(head * BLK, (head + 1) * BLK)
            place = step * FINISH_HEADS + head
            near = near_ref[half * state_ref.shape[0] + place, :, :BLK]
            seen = dot(jnp.where(core_ref[0] == 1, near, eye), state_ref[place]).astype(BF)
            states = jnp.concatenate(
                [seen[:, level * BLK : (level + 1) * BLK] for level in range(levels)], axis=0
            )
            for block in range(blocks):
                tokens = slice(block * BLK, (block + 1) * BLK)
                opened = base_ref[place, tokens, :] + dot(scaled_ref[place, tokens, :], states)
                square = jnp.sum(opened * opened, axis=-1, keepdims=True) * (1.0 / BLK)
                normed = opened * lax.rsqrt(square + EPS)
                out_ref[tokens, lanes] = (normed * gate_ref[place, tokens, :]).astype(BF)

    @pl.when(half == 0)
    def _():
        part(scaled_0, base_0, gate_0)

    @pl.when(half == 1)
    def _():
        part(scaled_1, base_1, gate_1)


def merged(left, right_a, right_b):
    moved = dot(right_a.astype(BF), left.astype(BF))
    return jnp.concatenate([moved[:, :BLK], moved[:, BLK:] + right_b.astype(F32)], axis=1)


def fetch(pairs, sem):
    copies = [
        pltpu.make_async_copy(source, target, sem.at[i])
        for i, (source, target) in enumerate(pairs)
    ]
    for copy in copies:
        copy.start()
    for copy in copies:
        copy.wait()


def join_near(core_ref, pair_ref, far_ref, next_ref, own, far, sem):
    core = core_ref[0]
    half = pl.ds(core * own.shape[0], own.shape[0])
    fetch([(pair_ref.at[half], own), (far_ref.at[half], far)], sem)

    @pl.when(core == 1)
    def _():
        for head in range(own.shape[0]):
            next_ref[head] = merged(far[head], own[head, :, :BLK], own[head, :, BLK:]).astype(BF)

    @pl.when(core == 0)
    def _():
        for head in range(own.shape[0]):
            next_ref[head] = merged(own[head], far[head, :, :BLK], far[head, :, BLK:]).astype(BF)


def join_far(upper_ref, pair_ref, far_ref, *rest):
    next_ref, state_ref, onward_ref, own, far, sem = rest[-6:]
    reach_ref = rest[0] if len(rest) == 7 else None
    lanes = slice(2 * BLK - next_ref.shape[2], 2 * BLK)
    fetch([(pair_ref, own), (far_ref, far)], sem)

    @pl.when(upper_ref[0] == 1)
    def _():
        for head in range(own.shape[0]):
            seen = far[head] if reach_ref is None else dot(reach_ref[head], far[head]).astype(BF)
            onward_ref[head] = seen[:, :BLK]
            state_ref[head] = seen[:, BLK:]
            joined = merged(far[head], own[head, :, :BLK], own[head, :, BLK:]).astype(BF)
            next_ref[head] = joined[:, lanes]

    @pl.when(upper_ref[0] == 0)
    def _():
        row, col = iota2((BLK, BLK), 0), iota2((BLK, BLK), 1)
        for head in range(own.shape[0]):
            joined = merged(own[head], far[head, :, :BLK], far[head, :, BLK:]).astype(BF)
            next_ref[head] = joined[:, lanes]
            state_ref[head] = jnp.zeros((BLK, BLK), BF)
            if reach_ref is None:
                onward_ref[head] = jnp.where(row == col, 1.0, 0.0).astype(BF)
            else:
                onward_ref[head] = reach_ref[head]


def join_top(upper_ref, far_ref, reach_ref, *rest):
    state_refs, (out_ref, far, sem) = rest[:-3], rest[-3:]
    levels = len(state_refs)
    fetch([(far_ref, far)], sem)
    for level in range(levels):
        for head in range(far.shape[0]):
            out_ref[head, :, level * BLK : (level + 1) * BLK] = state_refs[level][head]

    @pl.when(upper_ref[0] == 1)
    def _():
        for head in range(far.shape[0]):
            out_ref[head, :, levels * BLK :] = dot(reach_ref[head], far[head]).astype(BF)

    @pl.when(upper_ref[0] == 0)
    def _():
        for head in range(far.shape[0]):
            out_ref[head, :, levels * BLK :] = jnp.zeros((BLK, BLK), BF)


def shape_of(shape, dtype):
    return jax.ShapeDtypeStruct(shape, dtype)


def in_vmem(*arrays):
    return [pltpu.with_memory_space_constraint(x, pltpu.VMEM) for x in arrays]


def in_hbm(*arrays):
    return [pltpu.with_memory_space_constraint(x, pltpu.HBM) for x in arrays]


def whole(shape):
    return pl.BlockSpec(shape, lambda i: (0,) * len(shape))


def by_head(count, shape, first=0, lane=0):
    tail = (0,) * (len(shape) - 1) + (lane,)
    return pl.BlockSpec((count,) + shape, lambda i: (i + first,) + tail)


def by_column(shape, first=0):
    lead = len(shape) - 1
    return pl.BlockSpec(shape, lambda i: (0,) * lead + (i + first,))


ANY = pl.BlockSpec(memory_space=pl.ANY)
SMEM = pl.BlockSpec(memory_space=pltpu.SMEM)
VMEM = pl.BlockSpec(memory_space=pltpu.VMEM)
COST = pl.CostEstimate(flops=10**10, bytes_accessed=2 * 10**7, transcendentals=10**7)
PARAMS = pltpu.CompilerParams(dimension_semantics=("arbitrary",), vmem_limit_bytes=22 << 20)

SPREAD = pltpu.CompilerParams(
    dimension_semantics=("arbitrary",), vmem_limit_bytes=22 << 20,
)
SMALL = pltpu.CompilerParams(vmem_limit_bytes=8 << 20)


def bit(position, level):
    return (position // 2**level % 2).astype(jnp.int32).reshape(1)


def keys_of(rows, g_pad, conv_weight, halo, k_in, v_in):
    heads, _, length = rows.shape
    blocks = length // BLK
    width = PAIR * BLK
    steps = heads // PAIR
    units = PAIR * blocks
    first = pl.BlockSpec((length, width), lambda i: (0, 0))
    following = pl.BlockSpec((length, width), lambda i: (0, jnp.minimum(i + 1, steps - 1)))
    keys, values = in_hbm(k_in, v_in)
    return pl.pallas_call(
        key_side,
        grid=(steps,),
        in_specs=[
            whole(rows.shape), whole(g_pad.shape), whole(conv_weight.shape), whole(halo.shape),
            first, first, following, following,
        ],
        out_specs=[VMEM] * 4,
        out_shape=[
            pltpu.VMEM((heads, BLK, length), BF), pltpu.VMEM((heads, length, 2 * BLK), BF),
            pltpu.VMEM((heads, BLK, 2 * BLK), BF),
            pltpu.VMEM((heads, blocks - 1, BLK, 2 * BLK), BF),
        ],
        scratch_shapes=[
            pltpu.VMEM((4 * PAIR, length + 8, BLK), F32),
            pltpu.VMEM((2, units, BLK, BLK), F32),
            pltpu.VMEM((2, units, BLK, 2 * BLK), BF),
            pltpu.VMEM((2, units, BLK, BLK), BF),
            pltpu.VMEM((6, BLK, BLK), BF),
        ],
        compiler_params=PARAMS,
        cost_estimate=COST,
        name="key_side",
    )(rows, g_pad, conv_weight, halo, keys, values, keys, values)


def queries_of(second, levels, core, rows, g_pad, weights, taps, halo, gain, q_in, z_in, *kept):
    heads, _, length = rows.shape
    steps = heads // QUERY_HEADS // 2
    first = steps if second else 0
    width = QUERY_HEADS * BLK
    return pl.pallas_call(
        functools.partial(query_side, first_step=first),
        grid=(steps,),
        in_specs=[
            SMEM, by_head(QUERY_HEADS, (2, length), first), whole(g_pad.shape),
            whole(weights.shape), by_column((3, 4, width), first), by_column((3, 4, width), first),
            whole(gain.shape), by_column((length, width), first), by_column((length, width), first),
        ]
        + [VMEM] * 4,
        out_specs=[VMEM] * 3,
        out_shape=[
            pltpu.VMEM((heads // 2, length, (levels - 1) * BLK), BF),
            pltpu.VMEM((heads // 2, length, BLK), F32),
            pltpu.VMEM((heads // 2, length, BLK), F32),
        ],
        scratch_shapes=[pltpu.VMEM((QUERY_HEADS, length + 8, BLK), F32)],
        compiler_params=SPREAD,
        cost_estimate=COST,
        name="query_side",
    )(core, rows, g_pad, weights, taps, halo, gain, *in_hbm(q_in, z_in), *in_vmem(*kept))


def finished(half, core, near, states, parts, previous):
    heads, length = near.shape[0], parts[0].shape[1]
    steps = heads // FINISH_HEADS // 2
    return pl.pallas_call(
        finish_side,
        grid_spec=pltpu.PrefetchScalarGridSpec(
            num_scalar_prefetch=1,
            grid=(steps,),
            in_specs=[SMEM] + [VMEM] * 8 + [ANY] * len(previous),
            out_specs=pl.BlockSpec(
                (length, FINISH_HEADS * BLK), lambda i, half: (0, half[0] * steps + i)
            ),
        ),
        out_shape=shape_of((length, heads * BLK), BF),
        input_output_aliases={10 + i: i for i in range(len(previous))},
        compiler_params=PARAMS,
        cost_estimate=COST,
        name="finish_side",
    )(half, core, *in_vmem(near, states, *parts), *previous)


def cut_edges(q_ref, k_ref, v_ref, out_ref, rows_ref, sem):
    length = q_ref.shape[0]
    last = pl.ds(length - 8, 8)
    fetch([(ref.at[last], rows_ref.at[i]) for i, ref in enumerate((q_ref, k_ref, v_ref))], sem)
    for i in range(3):
        out_ref[i] = rows_ref[i, 4:8, :]


def edges_of(*arrays):
    columns = arrays[0].shape[1]
    return pl.pallas_call(
        cut_edges,
        in_specs=[ANY] * 3,
        out_specs=VMEM,
        out_shape=pltpu.VMEM((3, 4, columns), BF),
        scratch_shapes=[pltpu.VMEM((3, 8, columns), BF), pltpu.SemaphoreType.DMA((3,))],
        compiler_params=SMALL,
        name="cut_edges",
    )(*in_hbm(*arrays))


def joined_near(core, pair, near):
    shape = (pair.shape[0] // 2,) + pair.shape[1:]
    return pl.pallas_call(
        join_near,
        in_specs=[SMEM, ANY, ANY],
        out_specs=VMEM,
        out_shape=shape_of(shape, BF),
        scratch_shapes=[
            pltpu.VMEM(shape, BF), pltpu.VMEM(shape, BF), pltpu.SemaphoreType.DMA((2,)),
        ],
        compiler_params=SMALL,
        name="join_near",
    )(core, pair, near)


def joined_far(upper, pair, far, reach, last):
    square = (pair.shape[0], BLK, BLK)
    given = () if reach is None else (reach,)
    return pl.pallas_call(
        join_far,
        in_specs=[SMEM, ANY, ANY] + [VMEM] * len(given),
        out_specs=[VMEM] * 3,
        out_shape=[shape_of(square if last else pair.shape, BF)] + [shape_of(square, BF)] * 2,
        scratch_shapes=[
            pltpu.VMEM(pair.shape, BF), pltpu.VMEM(pair.shape, BF), pltpu.SemaphoreType.DMA((2,)),
        ],
        compiler_params=SMALL,
        name="join_far",
    )(upper, pair, far, *given)


def joined_top(upper, far, reach, states):
    shape = (far.shape[0], BLK, (len(states) + 1) * BLK)
    return pl.pallas_call(
        join_top,
        in_specs=[SMEM, ANY] + [VMEM] * (1 + len(states)),
        out_specs=VMEM,
        out_shape=shape_of(shape, BF),
        scratch_shapes=[pltpu.VMEM(far.shape, BF), pltpu.SemaphoreType.DMA((1,))],
        compiler_params=SMALL,
        name="join_top",
    )(upper, far, reach, *states)


def per_device(q_in, k_in, v_in, z_in, log_gate, beta, level_weight, conv_weight, norm_gain):
    length, heads = log_gate.shape
    blocks = length // BLK
    ctx = lax.axis_size("ctx")
    levels = ctx.bit_length() - 1
    position = lax.axis_index("ctx")
    halo = lax.ppermute(edges_of(q_in, k_in, v_in), "ctx", [(i, i + 1) for i in range(ctx - 1)])

    g = jnp.cumsum(log_gate.reshape(blocks, BLK, heads), axis=1).reshape(length, heads) * LOG2_E
    g_pad = jnp.pad(g, ((0, 0), (0, BLK - heads)))
    rows = jnp.stack([g.T, beta.T], axis=1)
    weights = level_weight[:, :, : levels + 1].reshape(length, heads * (levels + 1))
    weights = jnp.pad(weights, ((0, 0), (0, -weights.shape[1] % BLK)))
    bits = [bit(position, level) for level in range(levels)] + [1 - bit(position, 0)]
    halo, rows, g_pad, weights, *bits = lax.optimization_barrier(
        (halo, rows, g_pad, weights, *bits)
    )
    core, beside = bits[0], bits[-1]

    kt, uw, pair, prior = keys_of(rows, g_pad, conv_weight, halo, k_in, v_in)
    near = lax.ppermute(pair, "ctx", [(i, i ^ 1) for i in range(ctx)])
    pair = joined_near(core, pair, near)

    gain = norm_gain.reshape(1, BLK)

    def queries(second, q_in):
        return queries_of(
            second, levels, core, rows, g_pad, weights, conv_weight, halo, gain, q_in, z_in,
            kt, uw, prior, near,
        )

    reach, states = None, []
    for level in range(1, levels - 1):
        far = lax.ppermute(pair, "ctx", [(i, i ^ 2**level) for i in range(ctx)])
        if level == 1:
            far, *parts = lax.optimization_barrier((far, *queries(False, q_in)))
        pair, state, reach = joined_far(bits[level], pair, far, reach, level == levels - 2)
        states.append(state)
    top = levels - 1
    pair, later_q = lax.optimization_barrier((pair, q_in))
    far = lax.ppermute(pair, "ctx", [(i, i ^ 2**top) for i in range(ctx)])
    far, *more = lax.optimization_barrier((far, *queries(True, later_q)))
    own = joined_top(bits[top], far, reach, states)
    other = lax.ppermute(own, "ctx", [(i, i ^ 1) for i in range(ctx)])
    parts = [*parts, *more]
    out = finished(core, core, near, own, parts, ())
    other, out = lax.optimization_barrier((other, out))
    return finished(beside, core, near, other, parts, (out,))


def solution(mesh):
    placed = (
        P(("batch", "ctx"), None),
        P(("batch", "ctx"), None),
        P(("batch", "ctx"), None),
        P(("batch", "ctx"), None),
        P(("batch", "ctx"), None),
        P(("batch", "ctx"), None),
        P(("batch", "ctx"), None, None),
        P(),
        P(),
    )
    return jax.shard_map(
        per_device, mesh=mesh, in_specs=placed, out_specs=P(("batch", "ctx"), None), check_vma=False
    )
```
